32 devices in a mesh: dp: 8 (over z, x), ctx: 4 (over y, core).
Axes of the slice: x: 2, y: 2, z: 4, core: 2. Of those that a mesh axis runs over, the one named last changes fastest.
Arguments:
- layer_input: bfloat16 [16, 1024, 2048], P('dp', 'ctx'), may hold values from -6 to 6
- lengths: int32 [16], P('dp'), may hold values from 256 to 1024, as said below
- attn_gain: float32 [2048], replicated, may hold values from 0.5 to 1.5
- w_query: bfloat16 [2048, 1280], P('dp', 'ctx'), may hold values from -0.125 to 0.125
- w_key: bfloat16 [2048, 320], P('dp', 'ctx'), may hold values from -0.125 to 0.125
- w_value: bfloat16 [2048, 320], P('dp', 'ctx'), may hold values from -0.125 to 0.125
- query_gain: float32 [64], replicated, may hold values from 0.1 to 1.9
- key_gain: float32 [64], replicated, may hold values from 0.1 to 1.9
- w_out: bfloat16 [2048, 1280], P('dp', 'ctx'), may hold values from -3 to 3
- ffn_gain: float32 [2048], replicated, may hold values from 0.5 to 1.5
- w_gate: bfloat16 [2048, 5120], P('dp', 'ctx'), may hold values from -0.125 to 0.125
- w_up: bfloat16 [2048, 5120], P('dp', 'ctx'), may hold values from -0.125 to 0.125
- w_down: bfloat16 [2048, 5120], P('dp', 'ctx'), may hold values from -0.078125 to 0.078125
- cotangent: bfloat16 [16, 1024, 2048], P('dp', 'ctx'), may hold values from -6 to 6
Outputs:
- layer_output: bfloat16 [16, 1024, 2048], P('dp', 'ctx')
- input_grad: bfloat16 [16, 1024, 2048], P('dp', 'ctx')
- attn_gain_grad: float32 [2048], replicated
- w_query_grad: float32 [2048, 1280], P('dp', 'ctx')
- w_key_grad: float32 [2048, 320], P('dp', 'ctx')
- w_value_grad: float32 [2048, 320], P('dp', 'ctx')
- query_gain_grad: float32 [64], replicated
- key_gain_grad: float32 [64], replicated
- w_out_grad: float32 [2048, 1280], P('dp', 'ctx')
- ffn_gain_grad: float32 [2048], replicated
- w_gate_grad: float32 [2048, 5120], P('dp', 'ctx')
- w_up_grad: float32 [2048, 5120], P('dp', 'ctx')
- w_down_grad: float32 [2048, 5120], P('dp', 'ctx')
The draws below stay inside these ranges and needn't reach their ends.
Inputs may be any that keep to these rules, and one draw needn't show every extreme that they name: `lengths`: some row has all 1024 slots valid.
All inputs are finite; a program needn't handle non-finite values.
Results may differ from the reference program's by a relative error of at most 0.02.
Values may be sent and summed in bfloat16 or wider, within the bound.
A program may use at most 384 MiB of HBM per device.

```python
import math
from functools import partial
import jax
import jax.numpy as jnp
from jax import lax

D = 2048
HQ = 20
KVH = 5
HD = 64
FF = 5120
SLOTS = 1024
QW = 1280
KVW = 320
ROWS = 16


def draw_lengths(key, part):
    first_key, second_key = jax.random.split(key)
    drawn = jax.random.randint(first_key, (ROWS,), SLOTS // 4, SLOTS + 1)
    chosen = jax.random.randint(second_key, (), 0, ROWS)
    return jnp.where(jnp.arange(ROWS) == chosen, SLOTS, drawn).astype(jnp.int32)


def strengthened(array, rng, source, target, shards_of, factor):
    owner, partner = [(jnp.arange(array.shape[axis_at]) // (array.shape[axis_at] // shards_of)).reshape([-1 if axis == axis_at else 1 for axis in range(array.ndim)]) for axis_at in (source, target)]
    chosen = jax.random.permutation(rng, shards_of)[partner]
    strong = (owner == chosen) | (owner == (partner + shards_of // 2) % shards_of)
    return jnp.where(strong, factor * array, array)


def shard_levels(rng, shape, cuts, smallest, top_value):
    loudness, own = 1.0, jax.random.fold_in(rng, 6)
    for axis_at, parts in cuts:
        draws = jnp.exp(jax.random.uniform(jax.random.fold_in(own, axis_at), (parts,), jnp.float32, smallest / len(cuts), top_value / len(cuts)))
        loudness = loudness * jnp.repeat(draws, shape[axis_at] // parts).reshape([-1 if axis == axis_at else 1 for axis in range(len(shape))])
    return loudness


def bell_draw(key, extent, spread, bound, cuts=(), held_as=jnp.bfloat16):
    values = jax.random.normal(key, extent, jnp.float32) * spread
    if len(cuts) > 0:
        values = shard_levels(key, extent, cuts, -0.22, 0.18) * values
    return jnp.clip(values, min=-bound, max=bound).astype(held_as)


def bell_draw_with(rng, dims, spread, reach, pieces, heavy, held_as=jnp.bfloat16):
    result = spread * jax.random.normal(rng, dims, jnp.float32)
    if pieces:
        result = result * shard_levels(rng, dims, pieces, -0.22, 0.18)
    return jnp.clip(strengthened(result, jax.random.fold_in(rng, 3), *heavy), -reach, reach).astype(held_as)


def setup_inputs(seed: int = 0) -> dict:
    arg_keys = jax.random.split(jax.random.key(seed), 15)
    return {
        "layer_input": bell_draw(arg_keys[0], (ROWS, SLOTS, D), 1.0, 6.0, ((0, 8), (1, 4))),
        "lengths": draw_lengths(jax.random.fold_in(arg_keys[14], 71), 0),
        "attn_gain": jnp.clip(1.0 + 0.1 * jax.random.normal(arg_keys[2], (D,), jnp.float32), 0.5, 1.5),
        "w_query": bell_draw(arg_keys[3], (D, QW), D ** -0.5, 0.125, ((0, 8), (1, 4))),
        "w_key": bell_draw(arg_keys[4], (D, KVW), D ** -0.5, 0.125, ((0, 8), (1, 4))),
        "w_value": bell_draw(arg_keys[5], (D, KVW), D ** -0.5, 0.125, ((0, 8), (1, 4))),
        "query_gain": jnp.clip(1.0 + 0.18 * jax.random.normal(arg_keys[6], (HD,), jnp.float32), 0.1, 1.9),
        "key_gain": jnp.clip(1.0 + 0.18 * jax.random.normal(arg_keys[7], (HD,), jnp.float32), 0.1, 1.9),
        "w_out": bell_draw(arg_keys[8], (D, QW), (max(1, QW // 320)) ** -0.5, 3.0, ((0, 8), (1, 4))),
        "ffn_gain": jnp.clip(1.0 + 0.1 * jax.random.normal(arg_keys[9], (D,), jnp.float32), 0.5, 1.5),
        "w_gate": bell_draw(arg_keys[10], (D, FF), D ** -0.5, 0.125, ((0, 8), (1, 4))),
        "w_up": bell_draw(arg_keys[11], (D, FF), D ** -0.5, 0.125, ((0, 8), (1, 4))),
        "w_down": bell_draw(arg_keys[12], (D, FF), FF ** -0.5, 0.078125, ((0, 8), (1, 4))),
        "cotangent": bell_draw_with(arg_keys[13], (ROWS, SLOTS, D), 1.0, 6.0, ((0, 8), (1, 4)), (0, 2, 8, 2.0)),
    }


EPSILON = 1e-06
ROPE_BASE = 10000.0
HIGHEST = lax.Precision.HIGHEST

@jax.custom_vjp
def low(v):
    return lax.optimization_barrier(v.astype(jnp.bfloat16)).astype(jnp.float32)

@jax.custom_vjp
def low_back(v):
    return v

def low_keep(v):
    return (low(v), None)

def low_pass(kept, grad):
    return (grad,)

def back_keep(v):
    return (v, None)

def back_low(kept, grad):
    return (low(grad),)
low.defvjp(low_keep, low_pass)
low_back.defvjp(back_keep, back_low)

def rms_scale(values, gain_vec):
    return values * lax.rsqrt(lax.optimization_barrier(jnp.mean(values * values, -1, keepdims=True)) + EPSILON) * gain_vec

def rope_tables(positions, head_size):
    steps_half = jnp.arange(head_size // 2, dtype=jnp.float32)
    inverse = jnp.exp(steps_half * (-2.0 * math.log(ROPE_BASE) / head_size))
    angles = positions.astype(jnp.float32)[:, None] * inverse[None, :]
    cosine_table = jnp.concatenate([jnp.cos(angles), jnp.cos(angles)], -1)[:, None, :]
    sine_table = jnp.concatenate([jnp.sin(angles), jnp.sin(angles)], -1)[:, None, :]
    return (cosine_table, sine_table)

def rotate(values, cosine_table, sine_table):
    half_size = values.shape[-1] // 2
    turned = jnp.concatenate([-values[..., half_size:], values[..., :half_size]], -1)
    return values * cosine_table + turned * sine_table

def attend(queries, key_rows, values, row_length):
    grouped = queries.reshape(SLOTS, KVH, HQ // KVH, HD)
    scores = low_back(jnp.einsum('skgh,tkh->kgst', grouped, key_rows, precision=HIGHEST) * (1.0 / math.sqrt(HD)))
    slots = jnp.arange(SLOTS)
    allowed = (slots[None, :] <= slots[:, None]) & (slots[None, :] < row_length)
    scores = jnp.where(allowed, scores, -1e+30)
    largest = lax.optimization_barrier(jnp.max(scores, -1, keepdims=True))
    log_total = largest + jnp.log(lax.optimization_barrier(jnp.sum(jnp.exp(scores - largest), -1, keepdims=True)))
    weights = low(jnp.exp(scores - log_total))
    mixed_heads = jnp.einsum('kgst,tkh->skgh', weights, values, precision=HIGHEST)
    return mixed_heads.reshape(SLOTS, HQ * HD)

def layer_row(row_length, row_input, attn_gain, w_query, w_key, w_value, query_gain, key_gain, w_out, ffn_gain, w_gate, w_up, w_down):
    slots = jnp.arange(SLOTS)
    valid_mask = (slots < row_length).astype(jnp.float32)[:, None]
    cosine_table, sine_table = rope_tables(slots, HD)
    normed = low(rms_scale(row_input, attn_gain))
    query_lin = low_back(jnp.dot(normed, w_query, precision=HIGHEST))
    key_lin = low_back(jnp.dot(normed, w_key, precision=HIGHEST))
    value_lin = low_back(jnp.dot(normed, w_value, precision=HIGHEST))
    queries = low(rotate(rms_scale(query_lin.reshape(SLOTS, HQ, HD), query_gain), cosine_table, sine_table))
    key_rows = low(rotate(rms_scale(key_lin.reshape(SLOTS, KVH, HD), key_gain), cosine_table, sine_table))
    values = low(value_lin).reshape(SLOTS, KVH, HD)
    mixed_heads = low_back(low(jax.checkpoint(attend)(queries, key_rows, values, row_length)))
    attended = low_back(jnp.einsum('sc,dc->sd', mixed_heads, w_out, precision=HIGHEST))
    middle = row_input + attended
    normed_two = low(rms_scale(middle, ffn_gain))
    gate_lin = low_back(jnp.dot(normed_two, w_gate, precision=HIGHEST))
    upward = low_back(jnp.dot(normed_two, w_up, precision=HIGHEST))
    hidden = low(jax.nn.silu(gate_lin) * upward)
    branch = low_back(jnp.einsum('sf,df->sd', hidden, w_down, precision=HIGHEST))
    return valid_mask * (middle + branch)

def reference(layer_input, lengths, attn_gain, w_query, w_key, w_value, query_gain, key_gain, w_out, ffn_gain, w_gate, w_up, w_down, cotangent):
    params = tuple((weight_arg.astype(jnp.float32) for weight_arg in (attn_gain, w_query, w_key, w_value, query_gain, key_gain, w_out, ffn_gain, w_gate, w_up, w_down)))

    def one_row(totals, row_data):
        row_input, row_length, row_cot = row_data
        outputs, pullback = jax.vjp(partial(layer_row, row_length), row_input.astype(jnp.float32), *params)
        gradients = pullback(row_cot.astype(jnp.float32))
        totals = tuple((running + update for running, update in zip(totals, gradients[1:])))
        return (totals, (outputs.astype(jnp.bfloat16), gradients[0].astype(jnp.bfloat16)))
    starting = tuple((jnp.zeros_like(weight_arg) for weight_arg in params))
    totals, (outputs, input_grads) = lax.scan(one_row, starting, (layer_input, lengths, cotangent))
    return (outputs, input_grads, totals[0], totals[1], totals[2], totals[3], totals[4], totals[5], totals[6], totals[7], totals[8], totals[9], totals[10])
```

```python
import math

import jax
import jax.numpy as jnp
import numpy as np
from jax import lax
from jax.experimental import pallas as pl
from jax.experimental.pallas import tpu as pltpu
from jax.sharding import PartitionSpec as P

HQ = 20
KVH = 5
HD = 64
GROUP = HQ // KVH
QW = HQ * HD
KVW = KVH * HD
GW = GROUP * HD
LANES = 2 * HD
NEG = -1e30
EPSILON = 1e-06
ROPE_BASE = 10000.0
F32 = jnp.float32
BF16 = jnp.bfloat16
VMEM_LIMIT = 60 << 20


def nn(a, b):
    return lax.dot_general(a, b, (((1,), (0,)), ((), ())), preferred_element_type=F32)


def nt(a, b):
    return lax.dot_general(a, b, (((1,), (1,)), ((), ())), preferred_element_type=F32)


def tn(a, b):
    return lax.dot_general(a, b, (((0,), (0,)), ((), ())), preferred_element_type=F32)


def params(limit=VMEM_LIMIT):
    return pltpu.CompilerParams(vmem_limit_bytes=limit)


class Ring:
    def __init__(self, axis, size, direct, late):
        self.axis, self.size, self.direct, self.late = axis, size, direct, late
        combos = [0]
        for bit in direct:
            combos = combos + [c | bit for c in combos]
        self.combos = combos
        masks = list(combos)
        for bit in late:
            masks = masks + [m | bit for m in masks]
        self.masks = masks

    def swap(self, value, mask):
        return lax.ppermute(value, self.axis, [(i, i ^ mask) for i in range(self.size)])

    def gather(self, own):
        held = [own] + [self.swap(own, mask) for mask in self.combos[1:]]
        first = list(held)
        for bit in self.late:
            held = held + [self.swap(piece, bit) for piece in held]
        return held, first

    def scatter_late(self, blocks):
        for bit in reversed(self.late):
            half = len(blocks) // 2
            got = [self.swap(b.astype(BF16), bit) for b in blocks[half:]]
            blocks = [b + g.astype(F32) for b, g in zip(blocks[:half], got)]
        return blocks

    def scatter_direct(self, blocks):
        got = [self.swap(b.astype(BF16), m) for b, m in zip(blocks[1:], self.combos[1:])]
        total = blocks[0]
        for g in got:
            total = total + g.astype(F32)
        return total

    def scatter(self, blocks):
        return self.scatter_direct(self.scatter_late(blocks))


def split_bits(devices, axis_size):
    return [1 << i for i in range(axis_size.bit_length() - 1)]


def rings(mesh):
    grid = mesh.devices
    dp, ctx = mesh.shape["dp"], mesh.shape["ctx"]

    def place(d):
        return tuple(d.coords)

    far, near = [], []
    for bit in split_bits(grid, dp):
        a, b = place(grid[0, 0]), place(grid[bit, 0])
        (far if a[2] != b[2] else near).append(bit)
    outer, core = [], []
    for bit in split_bits(grid, ctx):
        a, b = place(grid[0, 0]), place(grid[0, bit])
        (core if a == b else outer).append(bit)
    return Ring("dp", dp, far, near), Ring("ctx", ctx, outer, core)


def permute_columns(value, index):
    rows, width = value.shape
    count = index.shape[0]
    block = width // count

    def body(index_ref, in_ref, out_ref):
        out_ref[...] = in_ref[...]

    return pl.pallas_call(
        body,
        out_shape=jax.ShapeDtypeStruct(value.shape, value.dtype),
        grid_spec=pltpu.PrefetchScalarGridSpec(
            num_scalar_prefetch=1,
            grid=(count,),
            in_specs=[pl.BlockSpec((rows, block), lambda i, ix: (0, ix[i]))],
            out_specs=pl.BlockSpec((rows, block), lambda i, ix: (0, i)),
        ),
        compiler_params=params(),
        name="permute_columns",
    )(index, value)


def head_stats(x, low):
    square = x * x
    first = jnp.sum(jnp.where(low, square, 0.0), -1, keepdims=True)
    second = jnp.sum(jnp.where(low, 0.0, square), -1, keepdims=True)
    return lax.rsqrt(jnp.where(low, first, second) * (1.0 / HD) + EPSILON)


def head_mean(x, low):
    first = jnp.sum(jnp.where(low, x, 0.0), -1, keepdims=True)
    second = jnp.sum(jnp.where(low, 0.0, x), -1, keepdims=True)
    return jnp.where(low, first, second) * (1.0 / HD)


def lane_masks(rows):
    lane = lax.broadcasted_iota(jnp.int32, (rows, LANES), 1)
    return lane < HD, lax.rem(lane, HD) < HD // 2


def qk_forward(lin, qgain, kgain, cosine, sine, rows, slots):
    total = QW + 2 * KVW

    def body(lin_ref, qgain_ref, kgain_ref, cos_ref, sin_ref, q_ref, kv_ref):
        low, front = lane_masks(slots)
        cos, sin = cos_ref[...], sin_ref[...]

        def turn(x, gain):
            n = x * head_stats(x, low) * gain
            turned = jnp.where(
                front, -pltpu.roll(n, LANES - HD // 2, 1), pltpu.roll(n, HD // 2, 1)
            )
            return n * cos + turned * sin

        for c in range(QW // LANES):
            x = lin_ref[:, c * LANES : (c + 1) * LANES]
            y = turn(x, qgain_ref[...]) * (1.0 / math.sqrt(HD))
            q_ref[:, c * LANES : (c + 1) * LANES] = y.astype(BF16)
        for g in range(KVH):
            x = lin_ref[:, QW + g * LANES : QW + (g + 1) * LANES]
            y = jnp.where(low, turn(x, kgain_ref[...]), x)
            kv_ref[:, g * LANES : (g + 1) * LANES] = y.astype(BF16)

    n = rows * slots
    whole = lambda r: (0, 0)
    return pl.pallas_call(
        body,
        out_shape=(
            jax.ShapeDtypeStruct((n, QW), BF16),
            jax.ShapeDtypeStruct((n, 2 * KVW), BF16),
        ),
        grid=(rows,),
        in_specs=[
            pl.BlockSpec((slots, total), lambda r: (r, 0)),
            pl.BlockSpec((1, LANES), whole),
            pl.BlockSpec((1, LANES), whole),
            pl.BlockSpec((slots, LANES), whole),
            pl.BlockSpec((slots, LANES), whole),
        ],
        out_specs=(
            pl.BlockSpec((slots, QW), lambda r: (r, 0)),
            pl.BlockSpec((slots, 2 * KVW), lambda r: (r, 0)),
        ),
        compiler_params=params(),
        name="qk_forward",
    )(lin, qgain, kgain, cosine, sine)


def qk_backward(dq, dkv, lin, qgain, kgain, cosine, sine, rows, slots):
    total = QW + 2 * KVW

    def body(
        dq_ref, dkv_ref, lin_ref, qgain_ref, kgain_ref, cos_ref, sin_ref, out_ref, gq_ref, gk_ref
    ):
        low, front = lane_masks(slots)
        cos, sin = cos_ref[...], sin_ref[...]

        @pl.when(pl.program_id(0) == 0)
        def _():
            gq_ref[...] = jnp.zeros_like(gq_ref)
            gk_ref[...] = jnp.zeros_like(gk_ref)

        def back(e, x, gain):
            t = e * sin
            e = e * cos + jnp.where(
                front, pltpu.roll(t, LANES - HD // 2, 1), -pltpu.roll(t, HD // 2, 1)
            )
            inv = head_stats(x, low)
            unit = x * inv
            part = e * unit
            u = e * gain
            return inv * (u - unit * head_mean(u * unit, low)), part

        gq = jnp.zeros((1, LANES), F32)
        for c in range(QW // LANES):
            at = slice(c * LANES, (c + 1) * LANES)
            y, part = back(dq_ref[:, at], lin_ref[:, at], qgain_ref[...])
            out_ref[:, at] = y.astype(BF16)
            gq = gq + jnp.sum(part, 0, keepdims=True)
        gk = jnp.zeros((1, LANES), F32)
        for g in range(KVH):
            at = slice(QW + g * LANES, QW + (g + 1) * LANES)
            e = dkv_ref[:, g * LANES : (g + 1) * LANES]
            y, part = back(e, lin_ref[:, at], kgain_ref[...])
            out_ref[:, at] = jnp.where(low, y, e).astype(BF16)
            gk = gk + jnp.sum(jnp.where(low, part, 0.0), 0, keepdims=True)
        gq_ref[...] += gq
        gk_ref[...] += gk

    n = rows * slots
    whole = lambda r: (0, 0)
    return pl.pallas_call(
        body,
        out_shape=(
            jax.ShapeDtypeStruct((n, total), BF16),
            jax.ShapeDtypeStruct((1, LANES), F32),
            jax.ShapeDtypeStruct((1, LANES), F32),
        ),
        grid=(rows,),
        in_specs=[
            pl.BlockSpec((slots, QW), lambda r: (r, 0)),
            pl.BlockSpec((slots, 2 * KVW), lambda r: (r, 0)),
            pl.BlockSpec((slots, total), lambda r: (r, 0)),
            pl.BlockSpec((1, LANES), whole),
            pl.BlockSpec((1, LANES), whole),
            pl.BlockSpec((slots, LANES), whole),
            pl.BlockSpec((slots, LANES), whole),
        ],
        out_specs=(
            pl.BlockSpec((slots, total), lambda r: (r, 0)),
            pl.BlockSpec((1, LANES), whole),
            pl.BlockSpec((1, LANES), whole),
        ),
        compiler_params=params(),
        name="qk_backward",
    )(dq, dkv, lin, qgain, kgain, cosine, sine)


def fill_bias(bias_ref, info_ref, row, masks, slots):
    place, length = info_ref[0], info_ref[1 + row]
    query = place * slots + lax.broadcasted_iota(jnp.int32, (slots, slots), 1)
    for i, mask in enumerate(masks):
        key = (place ^ mask) * slots + lax.broadcasted_iota(jnp.int32, (slots, slots), 0)
        allowed = (key <= query) & (key < length)
        bias_ref[i * slots : (i + 1) * slots, :] = jnp.where(allowed, 0.0, NEG)


def attend(info, q, kv_pieces, masks, rows, slots):
    count = len(masks)
    keys = count * slots

    def body(info_ref, q_ref, *refs):
        kv_refs, (o_ref, lse_ref, bias_ref) = refs[:count], refs[count:]
        row = pl.program_id(0)
        live = info_ref[0] * slots < info_ref[1 + row]

        @pl.when(live & (pl.program_id(1) == 0))
        def _():
            fill_bias(bias_ref, info_ref, row, masks, slots)

        @pl.when(jnp.logical_not(live))
        def _():
            o_ref[...] = jnp.zeros_like(o_ref)
            lse_ref[...] = jnp.zeros_like(lse_ref)

        @pl.when(live)
        def _():
            kv = jnp.concatenate([r[...] for r in kv_refs], 0)
            k, v = kv[:, :HD], kv[:, HD:]
            for h in range(GROUP):
                qh = q_ref[:, h * HD : (h + 1) * HD]
                s = nt(k, qh) + bias_ref[...]
                m = jnp.max(s, 0, keepdims=True)
                e = jnp.exp(s - m)
                l = jnp.sum(e, 0, keepdims=True)
                p = (e * (1.0 / l)).astype(BF16)
                o = tn(v, p)
                o_ref[:, h * HD : (h + 1) * HD] = o.T.astype(BF16)
                lse_ref[0, 0, h : h + 1, :] = m + jnp.log(l)

    n = rows * slots
    return pl.pallas_call(
        body,
        out_shape=(
            jax.ShapeDtypeStruct((n, QW), BF16),
            jax.ShapeDtypeStruct((rows, KVH, GROUP, slots), F32),
        ),
        grid_spec=pltpu.PrefetchScalarGridSpec(
            num_scalar_prefetch=1,
            grid=(rows, KVH),
            in_specs=[pl.BlockSpec((slots, GW), lambda r, g, s: (r, g))]
            + [pl.BlockSpec((slots, LANES), lambda r, g, s: (r, g))] * count,
            out_specs=(
                pl.BlockSpec((slots, GW), lambda r, g, s: (r, g)),
                pl.BlockSpec((1, 1, GROUP, slots), lambda r, g, s: (r, g, 0, 0)),
            ),
            scratch_shapes=[pltpu.VMEM((keys, slots), F32)],
        ),
        compiler_params=params(),
        cost_estimate=pl.CostEstimate(
            flops=16 * n * keys * QW, bytes_accessed=8 * n * QW, transcendentals=n * keys * HQ
        ),
        name="attend",
    )(info, q, *kv_pieces)


def attend_back(info, q, kv_pieces, do, lse, masks, rows, slots):
    count = len(masks)
    keys = count * slots

    def body(info_ref, q_ref, do_ref, lse_ref, *refs):
        kv_refs, dq_ref = refs[:count], refs[count]
        dkv_refs, bias_ref = refs[count + 1 : -1], refs[-1]
        row = pl.program_id(0)
        live = info_ref[0] * slots < info_ref[1 + row]

        @pl.when(live & (pl.program_id(1) == 0))
        def _():
            fill_bias(bias_ref, info_ref, row, masks, slots)

        @pl.when(jnp.logical_not(live))
        def _():
            dq_ref[...] = jnp.zeros_like(dq_ref)
            for r in dkv_refs:
                r[...] = jnp.zeros_like(r)

        @pl.when(live)
        def _():
            kv = jnp.concatenate([r[...] for r in kv_refs], 0)
            k, v = kv[:, :HD], kv[:, HD:]
            dk = jnp.zeros((keys, HD), F32)
            dv = jnp.zeros((keys, HD), F32)
            for h in range(GROUP):
                at = slice(h * HD, (h + 1) * HD)
                qh, doh = q_ref[:, at], do_ref[:, at]
                p = jnp.exp(nt(k, qh) + bias_ref[...] - lse_ref[0, 0, h : h + 1, :])
                dp = nt(v, doh)
                delta = jnp.sum(p * dp, 0, keepdims=True)
                ds = (p * (dp - delta)).astype(BF16)
                dv = dv + nn(p.astype(BF16), doh)
                dk = dk + nn(ds, qh)
                dq_ref[:, at] = tn(k, ds).T * (1.0 / math.sqrt(HD))
            both = jnp.concatenate([dk, dv], 1).astype(BF16)
            for i, r in enumerate(dkv_refs):
                r[...] = both[i * slots : (i + 1) * slots, :]

    n = rows * slots
    kv_spec = pl.BlockSpec((slots, LANES), lambda r, g, s: (r, g))
    q_spec = pl.BlockSpec((slots, GW), lambda r, g, s: (r, g))
    return pl.pallas_call(
        body,
        out_shape=(
            jax.ShapeDtypeStruct((n, QW), F32),
            *([jax.ShapeDtypeStruct((n, 2 * KVW), BF16)] * count),
        ),
        grid_spec=pltpu.PrefetchScalarGridSpec(
            num_scalar_prefetch=1,
            grid=(rows, KVH),
            in_specs=[
                q_spec,
                q_spec,
                pl.BlockSpec((1, 1, GROUP, slots), lambda r, g, s: (r, g, 0, 0)),
            ]
            + [kv_spec] * count,
            out_specs=(q_spec, *([kv_spec] * count)),
            scratch_shapes=[pltpu.VMEM((keys, slots), F32)],
        ),
        compiler_params=params(),
        cost_estimate=pl.CostEstimate(
            flops=40 * n * keys * QW, bytes_accessed=16 * n * QW, transcendentals=n * keys * HQ
        ),
        name="attend_back",
    )(info, q, do, lse, *kv_pieces)


def feed_forward(w_pieces, n2, bg, sums, acts, total, offset, last):
    parts, (tokens, depth), units = len(n2), n2[0].shape, w_pieces[0].shape[1]
    count, block = len(w_pieces), depth // len(w_pieces)
    tile = min(256, tokens)
    per = tokens // tile
    steps = parts * per
    shift = offset // tile
    tu = 256 if units % 256 == 0 else units
    td = 256
    sum_type = BF16 if last else F32
    has_sums, has_acts = sums is not None, acts is not None

    def body(*refs):
        w_refs, refs = refs[:count], refs[count:]
        n2_refs, refs = refs[:parts], refs[parts:]
        bg_refs, refs = refs[:parts], refs[parts:]
        sum_refs = ()
        if has_sums:
            sum_refs, refs = refs[:2], refs[2:]
        if has_acts:
            refs = refs[3:]
        branch_ref, grad_ref, h_ref, gg_ref, ug_ref = refs[:5]
        wg, wu, wd, sem = refs[5:]
        step = pl.program_id(0)

        @pl.when(step == 0)
        def _():
            copies = []
            for i, w in enumerate(w_refs):
                for j, dst in enumerate((wg, wu, wd)):
                    copies.append(
                        pltpu.make_async_copy(
                            w.at[j * block : (j + 1) * block, :],
                            dst.at[i * block : (i + 1) * block, :],
                            sem.at[3 * i + j],
                        )
                    )
            for c in copies:
                c.start()
            for c in copies:
                c.wait()

        x, b = n2_refs[0][...], bg_refs[0][...]
        for p in range(1, parts):
            here = step >= p * per
            x = jnp.where(here, n2_refs[p][...], x)
            b = jnp.where(here, bg_refs[p][...], b)
        for j in range(units // tu):
            at = slice(j * tu, (j + 1) * tu)
            gate, up = nn(x, wg[:, at]), nn(x, wu[:, at])
            dh = nn(b, wd[:, at])
            sig = 1.0 / (1.0 + jnp.exp(-gate))
            act = gate * sig
            h_ref[:, at] = (act * up).astype(BF16)
            gg_ref[:, at] = (dh * up * sig * (1.0 + gate * (1.0 - sig))).astype(BF16)
            ug_ref[:, at] = (dh * act).astype(BF16)
        h, gg, ug = h_ref[...], gg_ref[...], ug_ref[...]
        for j in range(depth // td):
            at = slice(j * td, (j + 1) * td)
            branch = nt(h, wd[at, :])
            grad = nt(gg, wg[at, :]) + nt(ug, wu[at, :])
            if has_sums:
                branch = branch + sum_refs[0][:, at]
                grad = grad + sum_refs[1][:, at]
            branch_ref[:, at] = branch.astype(sum_type)
            grad_ref[:, at] = grad.astype(sum_type)

    def token_map(p):
        return lambda i: (jnp.clip(i - p * per, 0, per - 1), 0)

    tok = [pl.BlockSpec((tile, depth), token_map(p)) for p in range(parts)]
    any_spec = pl.BlockSpec(memory_space=pl.ANY)
    sum_spec = pl.BlockSpec((tile, depth), lambda i: (i, 0))
    act_spec = pl.BlockSpec((tile, units), lambda i: (i + shift, 0))
    operands = [*w_pieces, *n2, *bg]
    in_specs = [any_spec] * count + tok + tok
    aliases = {}
    if has_sums:
        operands += sums
        in_specs += [sum_spec] * 2
    if has_acts:
        for j in range(3):
            aliases[len(operands) + j] = 2 + j
        operands += acts
        in_specs += [any_spec] * 3
    n = parts * tokens
    flops = 12 * n * depth * units
    out = pl.pallas_call(
        body,
        out_shape=(
            *([jax.ShapeDtypeStruct((n, depth), sum_type)] * 2),
            *([jax.ShapeDtypeStruct((total, units), BF16)] * 3),
        ),
        grid=(steps,),
        in_specs=in_specs,
        out_specs=(sum_spec, sum_spec, act_spec, act_spec, act_spec),
        scratch_shapes=[pltpu.VMEM((depth, units), BF16)] * 3
        + [pltpu.SemaphoreType.DMA((3 * count,))],
        input_output_aliases=aliases,
        compiler_params=params(),
        cost_estimate=pl.CostEstimate(
            flops=flops, bytes_accessed=16 * n * depth, transcendentals=n * units
        ),
        name="feed_forward",
    )(*operands)
    return list(out[:2]), list(out[2:])


def rope_tables(positions):
    steps_half = jnp.arange(HD // 2, dtype=F32)
    inverse = jnp.exp(steps_half * (-2.0 * math.log(ROPE_BASE) / HD))
    angles = positions.astype(F32)[:, None] * inverse[None, :]
    return jnp.tile(jnp.cos(angles), (1, 4)), jnp.tile(jnp.sin(angles), (1, 4))


def norm_rows(values, gain_vec):
    scale_inv = lax.rsqrt(jnp.mean(values * values, -1, keepdims=True) + EPSILON)
    unit_rows = values * scale_inv
    return unit_rows * gain_vec, unit_rows, scale_inv


def norm_back(grad_unit, unit_rows, scale_inv):
    return scale_inv * (grad_unit - unit_rows * jnp.mean(grad_unit * unit_rows, -1, keepdims=True))


def after(value, *others):
    return lax.optimization_barrier((value, *others))[0]


def make_layer(dp_ring, ctx_ring):
    nd, nc = dp_ring.size, ctx_ring.size
    dp_masks, ctx_masks = dp_ring.masks, ctx_ring.masks

    def column_blocks(stack):
        place = lax.axis_index("ctx")
        by_mask = jnp.stack([stack[ctx_masks.index(m)] for m in range(nc)], 0)
        ordered = jnp.take(by_mask, place ^ jnp.arange(nc), axis=0)
        return jnp.transpose(ordered, (1, 0, 2)).reshape(ordered.shape[1], -1)

    def relative_columns(value):
        place = lax.axis_index("ctx")
        width = value.shape[1] // nc
        return [
            lax.dynamic_slice_in_dim(value, (place ^ m) * width, width, 1) for m in ctx_masks
        ]

    def interleave(k, v):
        rows = k.shape[0]
        both = jnp.stack([k.reshape(rows, KVH, HD), v.reshape(rows, KVH, HD)], 2)
        return both.reshape(rows, 2 * KVW)

    def per_device(
        layer_input,
        lengths,
        attn_gain,
        w_query,
        w_key,
        w_value,
        query_gain,
        key_gain,
        w_out,
        ffn_gain,
        w_gate,
        w_up,
        w_down,
        cotangent,
    ):
        rows, slots, depth = layer_input.shape
        n = rows * slots
        block = depth // nd
        qc, kc, units = w_query.shape[1], w_key.shape[1], w_gate.shape[1]
        group, place = lax.axis_index("dp"), lax.axis_index("ctx")
        to_relative = group ^ jnp.array(dp_masks, jnp.int32)
        where_mask = np.argsort(np.array(dp_masks))
        to_absolute = jnp.array(where_mask, jnp.int32)[group ^ jnp.arange(nd)]
        positions = place * slots + jnp.arange(slots, dtype=jnp.int32)
        cosine, sine = rope_tables(positions)
        info = jnp.concatenate([place[None].astype(jnp.int32), lengths])
        valid = (positions[None, :] < lengths[:, None]).astype(F32).reshape(n, 1)
        qgain2 = jnp.tile(query_gain, 2)[None, :]
        kgain2 = jnp.tile(key_gain, 2)[None, :]

        qkv_held, first = dp_ring.gather(jnp.concatenate([w_query, w_key, w_value], 1))
        out_held, first_out = dp_ring.gather(after(w_out, *first[1:]))
        sizes = [768, 512] if units == 1280 else [units]
        chunks, start, behind = [], 0, first_out
        for size in sizes:
            at = slice(start, start + size)
            local = jnp.concatenate([w_gate[:, at], w_up[:, at], w_down[:, at]], 0)
            held, behind = dp_ring.gather(after(local, *behind[1:]))
            chunks.append(held)
            start += size

        x_bf = permute_columns(layer_input.reshape(n, depth), to_relative)
        bg = permute_columns(
            (cotangent.reshape(n, depth).astype(F32) * valid).astype(BF16), to_relative
        )
        gain_one = jnp.take(attn_gain.reshape(nd, block), to_relative, axis=0).reshape(depth)
        gain_two = jnp.take(ffn_gain.reshape(nd, block), to_relative, axis=0).reshape(depth)
        bg_all, _ = ctx_ring.gather(bg)

        x = x_bf.astype(F32)
        normed_one, unit_one, inv_one = norm_rows(x, gain_one)
        normed_bf = normed_one.astype(BF16)

        qkv_cols, _ = ctx_ring.gather(jnp.concatenate(qkv_held, 0))
        mat_q = column_blocks([c[:, :qc] for c in qkv_cols])
        mat_k = column_blocks([c[:, qc : qc + kc] for c in qkv_cols])
        mat_v = column_blocks([c[:, qc + kc :] for c in qkv_cols])
        mat_qkv = jnp.concatenate([mat_q, interleave(mat_k, mat_v)], 1)
        out_cols, _ = ctx_ring.gather(jnp.concatenate(out_held, 0))
        mat_out = column_blocks(out_cols)

        lin = nn(normed_bf, mat_qkv)
        q, kv = qk_forward(lin, qgain2, kgain2, cosine, sine, rows, slots)
        kv_all, _ = ctx_ring.gather(kv)
        mixed, lse = attend(info, q, kv_all, ctx_masks, rows, slots)
        middle = x + nt(mixed, mat_out)
        normed_two, unit_two, inv_two = norm_rows(middle, gain_two)
        n2_all, _ = ctx_ring.gather(normed_two.astype(BF16))

        half = nc // 2
        near = [i for i in range(nc) if not ctx_masks[i] & (nc >> 1)]
        far = [i for i in range(nc) if ctx_masks[i] & (nc >> 1)]
        pick = lambda pieces, which: [pieces[i] for i in which]
        sums = {"near": None, "far": None}
        acts_of = []
        for c, held in enumerate(chunks):
            last = c == len(chunks) - 1
            order = ("near", "far") if c == 0 else ("far", "near")
            acts = None
            for side in order:
                which, offset = (near, 0) if side == "near" else (far, half * n)
                sums[side], acts = feed_forward(
                    held,
                    pick(n2_all, which),
                    pick(bg_all, which),
                    sums[side],
                    acts,
                    nc * n,
                    offset,
                    last,
                )
            acts_of.append(acts)

        def pieces_of(k):
            out = [None] * nc
            for side, which in (("near", near), ("far", far)):
                for slot, i in enumerate(which):
                    out[i] = sums[side][k][slot * n : (slot + 1) * n].astype(F32)
            return out

        n2_cat = jnp.concatenate(pick(n2_all, near + far), 0)
        bg_cat = jnp.concatenate(pick(bg_all, near + far), 0)

        def scatter_rows(left, right):
            width = depth // (1 << len(dp_ring.late))
            parts = [
                tn(left[:, i * width : (i + 1) * width], right)
                for i in range(1 << len(dp_ring.late))
            ]
            parts = dp_ring.scatter_late(parts)[0]
            return dp_ring.scatter_direct(
                [parts[i * block : (i + 1) * block] for i in range(len(dp_ring.combos))]
            )

        gate_parts, up_parts, down_parts = [], [], []
        for h, gg, ug in acts_of:
            gate_parts.append(scatter_rows(n2_cat, gg))
            up_parts.append(scatter_rows(n2_cat, ug))
            down_parts.append(scatter_rows(bg_cat, h))

        grad_two = ctx_ring.scatter(pieces_of(1))
        branch = ctx_ring.scatter(pieces_of(0))
        out_rows = permute_columns((valid * (middle + branch)).astype(BF16), to_absolute)
        ffn_gain_part = jnp.sum(grad_two * unit_two, 0)
        middle_grad = bg.astype(F32) + norm_back(grad_two * gain_two, unit_two, inv_two)
        attn_grad = middle_grad.astype(BF16)
        mixed_grad = nn(attn_grad, mat_out).astype(BF16)

        dq, *dkv = attend_back(info, q, kv_all, mixed_grad, lse, ctx_masks, rows, slots)
        dkv_own = ctx_ring.scatter([d.astype(F32) for d in dkv])
        dlin, gq, gk = qk_backward(dq, dkv_own, lin, qgain2, kgain2, cosine, sine, rows, slots)
        normed_grad = nt(dlin, mat_qkv)
        attn_gain_part = jnp.sum(normed_grad * unit_one, 0)
        input_grad = (middle_grad + norm_back(normed_grad * gain_one, unit_one, inv_one)).astype(
            BF16
        )
        input_grad = permute_columns(input_grad, to_absolute)

        def scatter_both(blocks):
            own = ctx_ring.scatter(blocks)
            width = depth // (1 << len(dp_ring.late))
            parts = [own[i * width : (i + 1) * width] for i in range(1 << len(dp_ring.late))]
            parts = dp_ring.scatter_late(parts)[0]
            return dp_ring.scatter_direct(
                [parts[i * block : (i + 1) * block] for i in range(len(dp_ring.combos))]
            )

        w_out_grad = scatter_both([tn(attn_grad, m) for m in relative_columns(mixed)])
        dkv_heads = dlin[:, QW:].reshape(n, KVH, 2, HD)
        dk, dv = dkv_heads[:, :, 0].reshape(n, KVW), dkv_heads[:, :, 1].reshape(n, KVW)
        cuts = zip(
            relative_columns(dlin[:, :QW]), relative_columns(dk), relative_columns(dv)
        )
        w_qkv_grad = scatter_both(
            [tn(normed_bf, jnp.concatenate(cut, 1)) for cut in cuts]
        )

        def absolute(part):
            return jnp.take(part.reshape(nd, block), to_absolute, axis=0).reshape(depth)

        gains = jnp.concatenate(
            [absolute(attn_gain_part), absolute(ffn_gain_part), gq[0], gk[0]]
        )
        gains = lax.psum(gains, ("dp", "ctx"))
        gq = gains[2 * depth : 2 * depth + LANES]
        gk = gains[2 * depth + LANES :]
        return (
            out_rows.reshape(rows, slots, depth),
            input_grad.reshape(rows, slots, depth),
            gains[:depth],
            w_qkv_grad[:, :qc],
            w_qkv_grad[:, qc : qc + kc],
            w_qkv_grad[:, qc + kc :],
            gq[:HD] + gq[HD:],
            gk[:HD] + gk[HD:],
            w_out_grad,
            gains[depth : 2 * depth],
            jnp.concatenate(gate_parts, 1),
            jnp.concatenate(up_parts, 1),
            jnp.concatenate(down_parts, 1),
        )

    return per_device


def solution(mesh):
    wide = P("dp", "ctx")
    rows = P("dp", "ctx", None)
    in_specs = (
        rows, P("dp"), P(), wide, wide, wide, P(), P(), wide, P(), wide, wide, wide, rows,
    )
    out_specs = (
        rows, rows, P(), wide, wide, wide, P(), P(), wide, P(), wide, wide, wide,
    )
    return jax.shard_map(
        make_layer(*rings(mesh)),
        mesh=mesh,
        in_specs=in_specs,
        out_specs=out_specs,
        check_vma=False,
    )
```

```python
import math

import jax
import jax.numpy as jnp
import numpy as np
from jax import lax
from jax.experimental import pallas as pl
from jax.experimental.pallas import tpu as pltpu
from jax.sharding import Mesh, PartitionSpec as P

HQ = 20
KVH = 5
HD = 64
GROUP = HQ // KVH
QW = HQ * HD
KVW = KVH * HD
GW = GROUP * HD
LANES = 2 * HD
NEG = -1e30
EPSILON = 1e-06
ROPE_BASE = 10000.0
F32 = jnp.float32
BF16 = jnp.bfloat16
VMEM_LIMIT = 60 << 20


def nn(a, b):
    return lax.dot_general(a, b, (((1,), (0,)), ((), ())), preferred_element_type=F32)


def nt(a, b):
    return lax.dot_general(a, b, (((1,), (1,)), ((), ())), preferred_element_type=F32)


def tn(a, b):
    return lax.dot_general(a, b, (((0,), (0,)), ((), ())), preferred_element_type=F32)


def cost(**_):
    return pl.CostEstimate(flops=1, bytes_accessed=1, transcendentals=0)


def params(limit=VMEM_LIMIT):
    return pltpu.CompilerParams(vmem_limit_bytes=limit)


def after(value, *others):
    return lax.optimization_barrier((value, *others))[0] if others else value


def swap(value, axis, size, mask):
    return lax.ppermute(value, axis, [(i, i ^ mask) for i in range(size)])


class Place:
    def __init__(self, mesh):
        grid = mesh.devices
        self.nd, self.nc = mesh.shape["dp"], mesh.shape["ctx"]
        first = tuple(grid[0, 0].coords)
        bits = [1 << i for i in range(self.nd.bit_length() - 1)]
        far = [b for b in bits if tuple(grid[b, 0].coords)[2] != first[2]]
        self.nf = 1 << len(far)
        self.nn = self.nd // self.nf
        self.far_low = 1 in far
        bits = [1 << i for i in range(self.nc.bit_length() - 1)]
        self.core = [b for b in bits if tuple(grid[0, b].coords) == first]
        self.outer = [b for b in bits if b not in self.core]
        shape = (self.nn, self.nf) if self.far_low else (self.nf, self.nn)
        self.dp = ("near", "far") if self.far_low else ("far", "near")
        self.mesh = Mesh(grid.reshape(*shape, self.nc), (*self.dp, "ctx"))
        combos = [0]
        for bit in self.outer:
            combos = combos + [c | bit for c in combos]
        self.combos = combos
        masks = list(combos)
        for bit in self.core:
            masks = [m for pair in masks for m in (pair, pair | bit)]
        self.masks = masks

    def block(self, far, near):
        return near * self.nf + far if self.far_low else far * self.nn + near

    def cross(self, own, *first):
        held = {m: swap(own, "ctx", self.nc, m) if m else own for m in self.combos}
        for bit in self.core:
            held[bit] = swap(after(own, *first), "ctx", self.nc, bit)
        return held

    def gather(self, held, *hold):
        if not isinstance(held, dict):
            held = self.cross(held)
        held = dict(held)
        for bit in self.core:
            for m in self.combos[1:]:
                held[m | bit] = swap(after(held[m], *hold), "ctx", self.nc, bit)
        return [held[m] for m in self.masks]

    def arrived(self, held):
        return [v for m, v in held.items() if m]

    def exchange(self, blocks):
        return [blocks[0]] + [
            swap(b, "ctx", self.nc, m) for b, m in zip(blocks[1:], self.masks[1:])
        ]

    def scatter_core(self, blocks, kind=BF16):
        came = []
        for bit in self.core:
            kept = {}
            for m in blocks:
                if not m & bit:
                    got = swap(blocks[m | bit].astype(BF16), "ctx", self.nc, bit)
                    came.append(got)
                    kept[m] = combine([blocks[m], got], BF16 if m else kind)[0]
            blocks = kept
        return blocks, came

    def total(self, value):
        for axis, size in (("ctx", self.nc), ("near", self.nn), ("far", self.nf)):
            value = sum([swap(value, axis, size, m) for m in range(1, size)], value)
        return value

    def send_outer(self, blocks):
        return [swap(b, "ctx", self.nc, m) for m, b in blocks.items() if m]


def combine(parts, kind, pieces=1):
    shape = parts[0].shape
    tile = 256 if pieces == 1 and shape[0] % 256 == 0 else shape[0]
    block = (tile, *shape[1:])
    out = (shape[0] // pieces, *shape[1:])
    step = tile // pieces

    def body(*refs):
        part_refs, out_refs = refs[: len(parts)], refs[len(parts) :]
        for i, o in enumerate(out_refs):
            at = slice(i * step, (i + 1) * step)
            value = part_refs[0][at].astype(F32)
            for r in part_refs[1:]:
                value = value + r[at].astype(F32)
            o[...] = value.astype(kind)

    index = lambda i: (i,) + (0,) * (len(shape) - 1)
    return pl.pallas_call(
        body,
        out_shape=[jax.ShapeDtypeStruct(out, kind)] * pieces,
        grid=(shape[0] // tile,),
        in_specs=[pl.BlockSpec(block, index)] * len(parts),
        out_specs=[pl.BlockSpec((step, *shape[1:]), index)] * pieces,
        compiler_params=params(),
        cost_estimate=cost(),
        name="combine",
    )(*parts)


def finish_rows(middles, parts, valid):
    rows, (slots, depth) = len(middles), middles[0].shape

    def body(valid_ref, *refs):
        mid_refs, part_refs, out_ref = refs[:rows], refs[rows:-1], refs[-1]
        step = pl.program_id(0)
        y = mid_refs[0][...]
        for r in range(1, rows):
            y = jnp.where(step >= r, mid_refs[r][...], y)
        for p in part_refs:
            y = y + p[...].astype(F32)
        out_ref[...] = (y * valid_ref[...]).astype(BF16)

    whole = lambda i: (0, 0)
    by_row = lambda i: (i, 0)
    return pl.pallas_call(
        body,
        out_shape=jax.ShapeDtypeStruct((rows * slots, depth), BF16),
        grid=(rows,),
        in_specs=[pl.BlockSpec((slots, 1), by_row)]
        + [pl.BlockSpec((slots, depth), whole)] * rows
        + [pl.BlockSpec((slots, depth), by_row)] * len(parts),
        out_specs=pl.BlockSpec((slots, depth), by_row),
        compiler_params=params(),
        cost_estimate=cost(),
        name="finish_rows",
    )(valid, *middles, *parts)


def finish_grads(own, start, width, previous):
    many, units, block = own.shape

    def body(own_ref, *refs):
        for k in range(many):
            refs[-many + k][...] = own_ref[k].astype(F32).T

    extra = [] if previous is None else list(previous)
    return pl.pallas_call(
        body,
        out_shape=[jax.ShapeDtypeStruct((block, width), F32)] * many,
        grid=(1,),
        in_specs=[pl.BlockSpec((many, units, block), lambda i: (0, 0, 0))]
        + [pl.BlockSpec(memory_space=pl.ANY)] * len(extra),
        out_specs=[pl.BlockSpec((block, units), lambda i: (0, start // units))] * many,
        input_output_aliases={1 + k: k for k in range(len(extra))},
        compiler_params=params(),
        cost_estimate=cost(),
        name="finish_grads",
    )(own, *extra)


def head_stats(x, low):
    return lax.rsqrt(head_mean(x * x, low) + EPSILON)


def head_mean(x, low):
    first = jnp.sum(jnp.where(low, x, 0.0), -1, keepdims=True)
    second = jnp.sum(jnp.where(low, 0.0, x), -1, keepdims=True)
    return jnp.where(low, first, second) * (1.0 / HD)


def lane_masks(rows):
    lane = lax.broadcasted_iota(jnp.int32, (rows, LANES), 1)
    return lane < HD, lax.rem(lane, HD) < HD // 2


def spans(start, stop, width):
    out = []
    while start < stop:
        j = start // width
        end = min(stop, (j + 1) * width)
        out.append((j, start - j * width, end - j * width))
        start = end
    return out


def joined(parts):
    return parts[0] if len(parts) == 1 else jnp.concatenate(parts, 1)


def slot_copies(info_ref, place, w_refs, slots_ref, sem):
    copies = []
    for k, m in enumerate(place.masks):
        block = w_refs[k].shape[2]
        for i in range(place.nd):
            copies.append(
                pltpu.make_async_copy(
                    w_refs[k].at[i],
                    slots_ref.at[info_ref[0] ^ m, :, i * block : (i + 1) * block],
                    sem.at[len(copies)],
                )
            )
    return copies


def load_slots(*args):
    copies = slot_copies(*args)
    for c in copies:
        c.start()
    for c in copies:
        c.wait()


def project(info, place, x, gain, w_cols, qc, kc, qgain, kgain, cosine, sine, rows, slots):
    nc, depth, wc = place.nc, x.shape[1], w_cols[0].shape[-2]
    n = rows * slots

    def body(info_ref, x_ref, gain_ref, qgain_ref, kgain_ref, cos_ref, sin_ref, *refs):
        w_refs, (normed_ref, lin_ref, q_ref, kv_ref, w_ref, sem) = refs[:nc], refs[nc:]

        @pl.when(pl.program_id(0) == 0)
        def _():
            load_slots(info_ref, place, w_refs, w_ref, sem)

        xf = x_ref[...].astype(F32)
        inv = lax.rsqrt(jnp.mean(xf * xf, -1, keepdims=True) + EPSILON)
        normed_ref[...] = (xf * inv * gain_ref[...]).astype(BF16)
        for j in range(nc):
            lin_ref[j] = nt(normed_ref[...], w_ref[j])
        low, front = lane_masks(slots)
        cos, sin = cos_ref[...], sin_ref[...]

        def columns(base, width, start, stop):
            return [lin_ref[j, :, base + a : base + b] for j, a, b in spans(start, stop, width)]

        def turn(v, gain):
            v = v * head_stats(v, low) * gain
            turned = jnp.where(
                front, -pltpu.roll(v, LANES - HD // 2, 1), pltpu.roll(v, HD // 2, 1)
            )
            return v * cos + turned * sin

        for c in range(QW // LANES):
            at = slice(c * LANES, (c + 1) * LANES)
            y = turn(joined(columns(0, qc, at.start, at.stop)), qgain_ref[...])
            q_ref[:, at] = (y * (1.0 / math.sqrt(HD))).astype(BF16)
        for g in range(KVH):
            v = joined(
                columns(qc, kc, g * HD, (g + 1) * HD) + columns(qc + kc, kc, g * HD, (g + 1) * HD)
            )
            y = jnp.where(low, turn(v, kgain_ref[...]), v)
            kv_ref[:, g * LANES : (g + 1) * LANES] = y.astype(BF16)

    whole = lambda r, s: (0, 0)
    by_row = lambda r, s: (r, 0)
    return pl.pallas_call(
        body,
        out_shape=(
            jax.ShapeDtypeStruct((n, depth), BF16),
            jax.ShapeDtypeStruct((nc, n, wc), F32),
            jax.ShapeDtypeStruct((n, QW), BF16),
            jax.ShapeDtypeStruct((n, 2 * KVW), BF16),
        ),
        grid_spec=pltpu.PrefetchScalarGridSpec(
            num_scalar_prefetch=1,
            grid=(rows,),
            in_specs=[
                pl.BlockSpec((slots, depth), by_row),
                pl.BlockSpec((1, depth), whole),
                pl.BlockSpec((1, LANES), whole),
                pl.BlockSpec((1, LANES), whole),
                pl.BlockSpec((slots, LANES), whole),
                pl.BlockSpec((slots, LANES), whole),
            ]
            + [pl.BlockSpec(memory_space=pl.ANY)] * nc,
            out_specs=(
                pl.BlockSpec((slots, depth), by_row),
                pl.BlockSpec((nc, slots, wc), lambda r, s: (0, r, 0)),
                pl.BlockSpec((slots, QW), by_row),
                pl.BlockSpec((slots, 2 * KVW), by_row),
            ),
            scratch_shapes=[
                pltpu.VMEM((nc, wc, depth), BF16),
                pltpu.SemaphoreType.DMA((nc * place.nd,)),
            ],
        ),
        compiler_params=params(),
        cost_estimate=cost(
            flops=2 * n * depth * nc * wc, bytes_accessed=2 * nc * depth * wc, transcendentals=n
        ),
        name="project",
    )(info, x, gain, qgain, kgain, cosine, sine, *w_cols)


def project_back(
    info, place, dq, dkv_parts, lin, x, middle_grad, gain, w_cols, qc, kc, qgain, kgain, cosine, sine, row, slots
):
    nc, depth, wc = place.nc, x.shape[1], w_cols[0].shape[-2]

    def body(
        info_ref, dq_ref, lin_ref, x_ref, mid_ref, gain_ref, qgain_ref, kgain_ref, cos_ref, sin_ref, *refs
    ):
        dkv_refs, refs = refs[: len(dkv_parts)], refs[len(dkv_parts) :]
        w_refs, refs = refs[:nc], refs[nc:]
        out_ref, ga_ref, gq_ref, gk_ref = refs[:4]
        dlin_refs, (w_ref, dqs, dks, dvs, dlin_ref, sem) = refs[4 : 4 + nc], refs[4 + nc :]
        copies = slot_copies(info_ref, place, w_refs, w_ref, sem)
        for c in copies:
            c.start()
        low, front = lane_masks(slots)
        cos, sin = cos_ref[...], sin_ref[...]

        def columns(base, width, start, stop):
            return [lin_ref[j, :, base + a : base + b] for j, a, b in spans(start, stop, width)]

        def back(e, v, gain):
            t = e * sin
            e = e * cos + jnp.where(
                front, pltpu.roll(t, LANES - HD // 2, 1), -pltpu.roll(t, HD // 2, 1)
            )
            inv = head_stats(v, low)
            unit = v * inv
            part = e * unit
            u = e * gain
            return inv * (u - unit * head_mean(u * unit, low)), part

        gq = jnp.zeros((1, LANES), F32)
        for c in range(QW // LANES):
            at = slice(c * LANES, (c + 1) * LANES)
            v = joined(columns(0, qc, at.start, at.stop))
            y, part = back(dq_ref[:, at], v, qgain_ref[...])
            dqs[:, at] = y
            gq = gq + jnp.sum(part, 0, keepdims=True)
        gk = jnp.zeros((1, LANES), F32)
        for g in range(KVH):
            e = dkv_refs[0][:, g * LANES : (g + 1) * LANES].astype(F32)
            for ref in dkv_refs[1:]:
                e = e + ref[:, g * LANES : (g + 1) * LANES].astype(F32)
            v = joined(
                columns(qc, kc, g * HD, (g + 1) * HD) + columns(qc + kc, kc, g * HD, (g + 1) * HD)
            )
            y, part = back(e, v, kgain_ref[...])
            dks[:, g * HD : (g + 1) * HD] = y[:, :HD]
            dvs[:, g * HD : (g + 1) * HD] = e[:, HD:]
            gk = gk + jnp.sum(jnp.where(low, part, 0.0), 0, keepdims=True)
        gq_ref[...] = gq
        gk_ref[...] = gk
        for c in copies:
            c.wait()
        grad = None
        for j in range(nc):
            dlin = jnp.concatenate(
                [
                    dqs[:, j * qc : (j + 1) * qc],
                    dks[:, j * kc : (j + 1) * kc],
                    dvs[:, j * kc : (j + 1) * kc],
                ],
                1,
            )
            dlin_ref[j] = dlin.T.astype(BF16)
            part = nn(dlin.astype(BF16), w_ref[j])
            grad = part if grad is None else grad + part
        for k, m in enumerate(place.masks):
            dlin_refs[k][...] = dlin_ref[info_ref[0] ^ m]
        xf = x_ref[...].astype(F32)
        inv = lax.rsqrt(jnp.mean(xf * xf, -1, keepdims=True) + EPSILON)
        unit = xf * inv
        ga_ref[...] = jnp.sum(grad * unit, 0, keepdims=True)
        u = grad * gain_ref[...]
        back_x = inv * (u - unit * jnp.mean(u * unit, -1, keepdims=True))
        out_ref[...] = (mid_ref[...] + back_x).astype(BF16)

    whole = lambda i, s: (0, 0)
    by_row = lambda i, s: (row, 0)
    return pl.pallas_call(
        body,
        out_shape=(
            jax.ShapeDtypeStruct((slots, depth), BF16),
            jax.ShapeDtypeStruct((1, depth), F32),
            jax.ShapeDtypeStruct((1, LANES), F32),
            jax.ShapeDtypeStruct((1, LANES), F32),
            *([jax.ShapeDtypeStruct((wc, slots), BF16)] * nc),
        ),
        grid_spec=pltpu.PrefetchScalarGridSpec(
            num_scalar_prefetch=1,
            grid=(1,),
            in_specs=[
                pl.BlockSpec((slots, QW), whole),
                pl.BlockSpec((nc, slots, wc), lambda i, s: (0, row, 0)),
                pl.BlockSpec((slots, depth), by_row),
                pl.BlockSpec((slots, depth), by_row),
                pl.BlockSpec((1, depth), whole),
                pl.BlockSpec((1, LANES), whole),
                pl.BlockSpec((1, LANES), whole),
                pl.BlockSpec((slots, LANES), whole),
                pl.BlockSpec((slots, LANES), whole),
            ]
            + [pl.BlockSpec((slots, 2 * KVW), whole)] * len(dkv_parts)
            + [pl.BlockSpec(memory_space=pl.ANY)] * nc,
            out_specs=(
                pl.BlockSpec((slots, depth), whole),
                pl.BlockSpec((1, depth), whole),
                pl.BlockSpec((1, LANES), whole),
                pl.BlockSpec((1, LANES), whole),
                *([pl.BlockSpec((wc, slots), whole)] * nc),
            ),
            scratch_shapes=[
                pltpu.VMEM((nc, wc, depth), BF16),
                pltpu.VMEM((slots, QW), F32),
                pltpu.VMEM((slots, KVW), F32),
                pltpu.VMEM((slots, KVW), F32),
                pltpu.VMEM((nc, wc, slots), BF16),
                pltpu.SemaphoreType.DMA((nc * place.nd,)),
            ],
        ),
        compiler_params=params(),
        cost_estimate=cost(
            flops=2 * slots * depth * nc * wc,
            bytes_accessed=2 * nc * depth * wc,
            transcendentals=slots,
        ),
        name="project_back",
    )(info, dq, lin, x, middle_grad, gain, qgain, kgain, cosine, sine, *dkv_parts, *w_cols)


def fill_bias(bias_ref, info_ref, row, masks, slots):
    place, length = info_ref[0], info_ref[1 + row]
    query = place * slots + lax.broadcasted_iota(jnp.int32, (slots, slots), 1)
    for i, mask in enumerate(masks):
        key = (place ^ mask) * slots + lax.broadcasted_iota(jnp.int32, (slots, slots), 0)
        allowed = (key <= query) & (key < length)
        bias_ref[i * slots : (i + 1) * slots, :] = jnp.where(allowed, 0.0, NEG)


def attend(info, q, kv_pieces, masks, row, slots):
    count = len(masks)
    keys = count * slots

    def body(info_ref, q_ref, *refs):
        kv_refs, (o_ref, ot_ref, lse_ref, bias_ref) = refs[:count], refs[count:]
        live = info_ref[0] * slots < info_ref[1 + row]

        @pl.when(live & (pl.program_id(0) == 0))
        def _():
            fill_bias(bias_ref, info_ref, row, masks, slots)

        @pl.when(jnp.logical_not(live))
        def _():
            o_ref[...] = jnp.zeros_like(o_ref)
            ot_ref[...] = jnp.zeros_like(ot_ref)
            lse_ref[...] = jnp.zeros_like(lse_ref)

        @pl.when(live)
        def _():
            kv = jnp.concatenate([r[...] for r in kv_refs], 0)
            k, v = kv[:, :HD], kv[:, HD:]
            for h in range(GROUP):
                qh = q_ref[:, h * HD : (h + 1) * HD]
                s = nt(k, qh) + bias_ref[...]
                m = jnp.max(s, 0, keepdims=True)
                e = jnp.exp(s - m)
                l = jnp.sum(e, 0, keepdims=True)
                p = (e * (1.0 / l)).astype(BF16)
                o = tn(v, p)
                o_ref[:, h * HD : (h + 1) * HD] = o.T.astype(BF16)
                ot_ref[h * HD : (h + 1) * HD, :] = o.astype(BF16)
                lse_ref[0, h : h + 1, :] = m + jnp.log(l)

    n = slots
    return pl.pallas_call(
        body,
        out_shape=(
            jax.ShapeDtypeStruct((n, QW), BF16),
            jax.ShapeDtypeStruct((QW, n), BF16),
            jax.ShapeDtypeStruct((KVH, GROUP, slots), F32),
        ),
        grid_spec=pltpu.PrefetchScalarGridSpec(
            num_scalar_prefetch=1,
            grid=(KVH,),
            in_specs=[pl.BlockSpec((slots, GW), lambda g, s: (row, g))]
            + [pl.BlockSpec((slots, LANES), lambda g, s: (row, g))] * count,
            out_specs=(
                pl.BlockSpec((slots, GW), lambda g, s: (0, g)),
                pl.BlockSpec((GW, slots), lambda g, s: (g, 0)),
                pl.BlockSpec((1, GROUP, slots), lambda g, s: (g, 0, 0)),
            ),
            scratch_shapes=[pltpu.VMEM((keys, slots), F32)],
        ),
        compiler_params=params(),
        cost_estimate=cost(
            flops=16 * n * keys * QW, bytes_accessed=8 * n * QW, transcendentals=n * keys * HQ
        ),
        name="attend",
    )(info, q, *kv_pieces)


def attend_back(info, q, kv_pieces, do, lse, masks, row, slots):
    count = len(masks)
    keys = count * slots

    def body(info_ref, q_ref, do_ref, lse_ref, *refs):
        kv_refs, dq_ref = refs[:count], refs[count]
        dkv_refs, bias_ref = refs[count + 1 : -1], refs[-1]
        live = info_ref[0] * slots < info_ref[1 + row]

        @pl.when(live & (pl.program_id(0) == 0))
        def _():
            fill_bias(bias_ref, info_ref, row, masks, slots)

        @pl.when(jnp.logical_not(live))
        def _():
            dq_ref[...] = jnp.zeros_like(dq_ref)
            for r in dkv_refs:
                r[...] = jnp.zeros_like(r)

        @pl.when(live)
        def _():
            kv = jnp.concatenate([r[...] for r in kv_refs], 0)
            k, v = kv[:, :HD], kv[:, HD:]
            dk = jnp.zeros((keys, HD), F32)
            dv = jnp.zeros((keys, HD), F32)
            for h in range(GROUP):
                at = slice(h * HD, (h + 1) * HD)
                qh, doh = q_ref[:, at], do_ref[:, at]
                p = jnp.exp(nt(k, qh) + bias_ref[...] - lse_ref[0, h : h + 1, :])
                dp = nt(v, doh)
                delta = jnp.sum(p * dp, 0, keepdims=True)
                ds = (p * (dp - delta)).astype(BF16)
                dv = dv + nn(p.astype(BF16), doh)
                dk = dk + nn(ds, qh)
                dq_ref[:, at] = tn(k, ds).T * (1.0 / math.sqrt(HD))
            both = jnp.concatenate([dk, dv], 1).astype(BF16)
            for i, r in enumerate(dkv_refs):
                r[...] = both[i * slots : (i + 1) * slots, :]

    n = slots
    kv_spec = pl.BlockSpec((slots, LANES), lambda g, s: (row, g))
    q_spec = pl.BlockSpec((slots, GW), lambda g, s: (row, g))
    out_kv = pl.BlockSpec((slots, LANES), lambda g, s: (0, g))
    out_q = pl.BlockSpec((slots, GW), lambda g, s: (0, g))
    return pl.pallas_call(
        body,
        out_shape=(
            jax.ShapeDtypeStruct((n, QW), F32),
            *([jax.ShapeDtypeStruct((n, 2 * KVW), BF16)] * count),
        ),
        grid_spec=pltpu.PrefetchScalarGridSpec(
            num_scalar_prefetch=1,
            grid=(KVH,),
            in_specs=[
                q_spec,
                q_spec,
                pl.BlockSpec((1, GROUP, slots), lambda g, s: (g, 0, 0)),
            ]
            + [kv_spec] * count,
            out_specs=(out_q, *([out_kv] * count)),
            scratch_shapes=[pltpu.VMEM((keys, slots), F32)],
        ),
        compiler_params=params(),
        cost_estimate=cost(
            flops=40 * n * keys * QW, bytes_accessed=16 * n * QW, transcendentals=n * keys * HQ
        ),
        name="attend_back",
    )(info, q, do, lse, *kv_pieces)


def out_project(info, place, mixed, x, gain, w_cols, row):
    nc, depth, oc = place.nc, x.shape[1], w_cols[0].shape[-2]
    slots = mixed.shape[0]
    td = 256

    def body(info_ref, mixed_ref, x_ref, gain_ref, *refs):
        w_refs, (mid_ref, n2_ref, w_ref, sem) = refs[:nc], refs[nc:]
        load_slots(info_ref, place, w_refs, w_ref, sem)
        parts = [mixed_ref[:, j * oc : (j + 1) * oc] for j in range(nc)]
        square = jnp.zeros((slots, 1), F32)
        for d in range(depth // td):
            at = slice(d * td, (d + 1) * td)
            y = x_ref[:, at].astype(F32)
            for j in range(nc):
                y = y + nn(parts[j], w_ref[j, :, at])
            mid_ref[:, at] = y
            square = square + jnp.sum(y * y, -1, keepdims=True)
        inv = lax.rsqrt(square * (1.0 / depth) + EPSILON)
        n2_ref[...] = (mid_ref[...] * inv * gain_ref[...]).astype(BF16)

    whole = lambda i, s: (0, 0)
    return pl.pallas_call(
        body,
        out_shape=(
            jax.ShapeDtypeStruct((slots, depth), F32),
            jax.ShapeDtypeStruct((slots, depth), BF16),
        ),
        grid_spec=pltpu.PrefetchScalarGridSpec(
            num_scalar_prefetch=1,
            grid=(1,),
            in_specs=[
                pl.BlockSpec((slots, nc * oc), whole),
                pl.BlockSpec((slots, depth), lambda i, s: (row, 0)),
                pl.BlockSpec((1, depth), whole),
            ]
            + [pl.BlockSpec(memory_space=pl.ANY)] * nc,
            out_specs=(pl.BlockSpec((slots, depth), whole), pl.BlockSpec((slots, depth), whole)),
            scratch_shapes=[
                pltpu.VMEM((nc, oc, depth), BF16),
                pltpu.SemaphoreType.DMA((nc * place.nd,)),
            ],
        ),
        compiler_params=params(),
        cost_estimate=cost(
            flops=2 * slots * depth * nc * oc, bytes_accessed=4 * nc * depth * oc, transcendentals=0
        ),
        name="out_project",
    )(info, mixed, x, gain, *w_cols)


def middle_back(info, place, parts, middles, bg, gain, w_cols, rows, slots):
    nc, depth, oc, count = place.nc, bg.shape[1], w_cols[0].shape[-2], len(parts)
    n = rows * slots

    def body(info_ref, *refs):
        part_refs, refs = refs[:count], refs[count:]
        mid_refs, refs = refs[:rows], refs[rows:]
        bg_ref, gain_ref, refs = refs[0], refs[1], refs[2:]
        w_refs, (mg_ref, ag_ref, xg_ref, gf_ref, w_ref, sem) = refs[:nc], refs[nc:]
        step = pl.program_id(0)

        @pl.when(step == 0)
        def _():
            load_slots(info_ref, place, w_refs, w_ref, sem)
            gf_ref[...] = jnp.zeros_like(gf_ref)

        grad = part_refs[0][...].astype(F32)
        for p in part_refs[1:]:
            grad = grad + p[...].astype(F32)
        mid = mid_refs[0][...]
        for r in range(1, rows):
            mid = jnp.where(step >= r, mid_refs[r][...], mid)
        inv = lax.rsqrt(jnp.mean(mid * mid, -1, keepdims=True) + EPSILON)
        unit = mid * inv
        gf_ref[...] += jnp.sum(grad * unit, 0, keepdims=True)
        u = grad * gain_ref[...]
        y = bg_ref[...].astype(F32) + inv * (u - unit * jnp.mean(u * unit, -1, keepdims=True))
        mg_ref[...] = y
        ag_ref[...] = y.astype(BF16)
        xg_ref[...] = jnp.concatenate(
            [nt(ag_ref[...], w_ref[j]) for j in range(nc)], 1
        ).astype(BF16)

    whole = lambda i, s: (0, 0)
    by_row = lambda i, s: (i, 0)
    token = pl.BlockSpec((slots, depth), by_row)
    return pl.pallas_call(
        body,
        out_shape=(
            jax.ShapeDtypeStruct((n, depth), F32),
            jax.ShapeDtypeStruct((n, depth), BF16),
            jax.ShapeDtypeStruct((n, nc * oc), BF16),
            jax.ShapeDtypeStruct((1, depth), F32),
        ),
        grid_spec=pltpu.PrefetchScalarGridSpec(
            num_scalar_prefetch=1,
            grid=(rows,),
            in_specs=[token] * count
            + [pl.BlockSpec((slots, depth), whole)] * rows
            + [token, pl.BlockSpec((1, depth), whole)]
            + [pl.BlockSpec(memory_space=pl.ANY)] * nc,
            out_specs=(
                token,
                token,
                pl.BlockSpec((slots, nc * oc), by_row),
                pl.BlockSpec((1, depth), whole),
            ),
            scratch_shapes=[
                pltpu.VMEM((nc, oc, depth), BF16),
                pltpu.SemaphoreType.DMA((nc * place.nd,)),
            ],
        ),
        compiler_params=params(),
        cost_estimate=cost(
            flops=2 * n * depth * nc * oc, bytes_accessed=20 * n * depth, transcendentals=0
        ),
        name="middle_back",
    )(info, *parts, *middles, bg, gain, *w_cols)


def feed_forward(info, place, weights, n2, bg, sums, acts, total, first, last):
    owners, (tokens, depth), units = len(n2), bg[0].shape, weights.shape[1]
    cuts = len(n2[0])
    part = tokens // cuts
    block = depth // place.nd
    tu = 256 if units % 256 == 0 else units
    td = 256
    sum_type = BF16 if last else F32
    has_sums, has_acts = sums is not None, acts is not None

    def body(info_ref, w_ref, *refs):
        n2_refs, refs = refs[: owners * cuts], refs[owners * cuts :]
        bg_refs, refs = refs[:owners], refs[owners:]
        sum_refs = ()
        if has_sums:
            sum_refs, refs = refs[: 2 * owners], refs[2 * owners :]
        if has_acts:
            refs = refs[3:]
        out_refs, refs = refs[: 2 * owners], refs[2 * owners :]
        ht_ref, ggt_ref, ugt_ref, wg, wu, wd, acts_buf, tok_buf, out_buf = refs[:9]
        w_sem, tok_sem, out_sem = refs[9:12]
        in_buf, in_sem = refs[12:] if has_sums else (None, None)
        step = pl.program_id(0)
        slot = lax.rem(step, 2)

        def token_copies(p, to):
            found = [
                pltpu.make_async_copy(
                    n2_refs[p * cuts + i],
                    tok_buf.at[to, 0, i * part : (i + 1) * part, :],
                    tok_sem.at[to, i],
                )
                for i in range(cuts)
            ]
            return found + [
                pltpu.make_async_copy(bg_refs[p], tok_buf.at[to, 1], tok_sem.at[to, cuts])
            ]

        def sum_copies(p):
            return [
                pltpu.make_async_copy(sum_refs[2 * p + k], in_buf.at[k], in_sem.at[k])
                for k in range(2)
            ]

        def out_copies(p):
            return [
                pltpu.make_async_copy(out_buf.at[k], out_refs[2 * p + k], out_sem.at[k])
                for k in range(2)
            ]

        @pl.when(step == 0)
        def _():
            for c in token_copies(0, 0):
                c.start()
            copies = []
            for i in range(place.nd):
                for j, dst in enumerate((wg, wu, wd)):
                    start = (3 * i + j) * block
                    copies.append(
                        pltpu.make_async_copy(
                            w_ref.at[start : start + block, :],
                            dst.at[i * block : (i + 1) * block, :],
                            w_sem.at[len(copies)],
                        )
                    )
            for c in copies:
                c.start()
            for c in copies:
                c.wait()

        for p in range(owners):

            @pl.when(step == p)
            def _():
                if p + 1 < owners:
                    for c in token_copies(p + 1, (p + 1) % 2):
                        c.start()
                if has_sums:
                    for c in sum_copies(p):
                        c.start()

        for c in token_copies(0, slot):
            c.wait()
        x, b = tok_buf[slot, 0], tok_buf[slot, 1]
        for j in range(units // tu):
            at = slice(j * tu, (j + 1) * tu)
            gate, up = nn(x, wg[:, at]), nn(x, wu[:, at])
            dh = nn(b, wd[:, at])
            sig = 1.0 / (1.0 + jnp.exp(-gate))
            act = gate * sig
            h = act * up
            gg = dh * up * sig * (1.0 + gate * (1.0 - sig))
            ug = dh * act
            for k, (value, ref) in enumerate(((h, ht_ref), (gg, ggt_ref), (ug, ugt_ref))):
                acts_buf[k, :, at] = value.astype(BF16)
                ref[at, :] = value.T.astype(BF16)

        @pl.when(step > 0)
        def _():
            for c in out_copies(0):
                c.wait()

        if has_sums:
            for c in sum_copies(0):
                c.wait()
        h, gg, ug = acts_buf[0], acts_buf[1], acts_buf[2]
        for j in range(depth // td):
            at = slice(j * td, (j + 1) * td)
            values = [nt(h, wd[at, :]), nt(gg, wg[at, :]) + nt(ug, wu[at, :])]
            for k in range(2):
                value = values[k]
                if has_sums:
                    value = value + in_buf[k, :, at]
                out_buf[k, :, at] = value.astype(sum_type)
        for p in range(owners):

            @pl.when(step == p)
            def _():
                for c in out_copies(p):
                    c.start()

        @pl.when(step == owners - 1)
        def _():
            for c in out_copies(0):
                c.wait()

    any_spec = pl.BlockSpec(memory_space=pl.ANY)
    act_spec = pl.BlockSpec((units, tokens), lambda i, s: (0, i + first))
    operands = [weights, *[v for group in n2 for v in group], *bg]
    aliases = {}
    if has_sums:
        operands += [v for pair in sums for v in pair]
    if has_acts:
        for j in range(3):
            aliases[1 + len(operands) + j] = 2 * owners + j
        operands += acts
    n = owners * tokens
    scratch = [pltpu.VMEM((depth, units), BF16)] * 3 + [
        pltpu.VMEM((3, tokens, units), BF16),
        pltpu.VMEM((2, 2, tokens, depth), BF16),
        pltpu.VMEM((2, tokens, depth), sum_type),
        pltpu.SemaphoreType.DMA((3 * place.nd,)),
        pltpu.SemaphoreType.DMA((2, cuts + 1)),
        pltpu.SemaphoreType.DMA((2,)),
    ]
    if has_sums:
        scratch += [pltpu.VMEM((2, tokens, depth), F32), pltpu.SemaphoreType.DMA((2,))]
    out = pl.pallas_call(
        body,
        out_shape=(
            *([jax.ShapeDtypeStruct((tokens, depth), sum_type)] * (2 * owners)),
            *([jax.ShapeDtypeStruct((units, total), BF16)] * 3),
        ),
        grid_spec=pltpu.PrefetchScalarGridSpec(
            num_scalar_prefetch=1,
            grid=(owners,),
            in_specs=[any_spec] * len(operands),
            out_specs=(*([any_spec] * (2 * owners)), act_spec, act_spec, act_spec),
            scratch_shapes=scratch,
        ),
        input_output_aliases=aliases,
        compiler_params=params(),
        cost_estimate=cost(
            flops=12 * n * depth * units, bytes_accessed=16 * n * depth, transcendentals=n * units
        ),
        name="feed_forward",
    )(info, *operands)
    return [list(out[2 * o : 2 * o + 2]) for o in range(owners)], list(out[2 * owners :])


def weight_grads(order, block, sets, width, added=None, apart=False):
    lefts = [v for left, _ in sets for v in left]
    rights = [v for _, right in sets for group in right for v in group]
    many, blocks = sum(len(right) for _, right in sets), order.shape[0]

    def body(order_ref, *refs):
        left_refs, refs = refs[: len(lefts)], refs[len(lefts) :]
        right_refs, refs = refs[: len(rights)], refs[len(rights) :]
        extra_ref, out_refs = (None, refs) if added is None else (refs[0], refs[1:])
        i = k = at = 0
        for left, right in sets:
            tall = joined_rows([r[...] for r in left_refs[i : i + len(left)]])
            i += len(left)
            wides = []
            for group in right:
                wides.append(joined([r[...] for r in right_refs[at : at + len(group)]]))
                at += len(group)
            values = nn(joined_rows(wides), tall)
            for m in range(len(right)):
                value = values[m * width : (m + 1) * width]
                if added is not None:
                    value = value + extra_ref[0, k].astype(F32)
                if apart:
                    for f in range(blocks):

                        @pl.when(pl.program_id(0) == f)
                        def _():
                            out_refs[f][k] = value.astype(BF16)
                else:
                    out_refs[0][0, k] = value.astype(BF16)
                k += 1

    part = pl.BlockSpec((1, many, width, block), lambda i, ix: (i, 0, 0, 0))
    extra = [] if added is None else [added]
    if apart:
        shapes = [jax.ShapeDtypeStruct((many, width, block), BF16)] * blocks
        specs = [pl.BlockSpec((many, width, block), lambda i, ix: (0, 0, 0))] * blocks
    else:
        shapes = jax.ShapeDtypeStruct((blocks, many, width, block), BF16)
        specs = part
    return pl.pallas_call(
        body,
        out_shape=shapes,
        grid_spec=pltpu.PrefetchScalarGridSpec(
            num_scalar_prefetch=1,
            grid=(blocks,),
            in_specs=[pl.BlockSpec((v.shape[0], block), lambda i, ix: (0, ix[i])) for v in lefts]
            + [pl.BlockSpec((width, v.shape[1]), lambda i, ix: (0, 0)) for v in rights]
            + [part] * len(extra),
            out_specs=specs,
        ),
        compiler_params=params(),
        cost_estimate=cost(),
        name="weight_grads",
    )(order, *lefts, *rights, *extra)


def out_weight_grads(order, place, block, left, rights):
    nc, blocks = place.nc, order.shape[0] - 1
    width = rights[0].shape[0]
    part = width // nc

    def body(order_ref, left_ref, *refs):
        right_refs, refs = refs[: len(rights)], refs[len(rights) :]
        out_refs, value_ref = refs[:nc], refs[nc]
        value_ref[...] = nn(joined([r[...] for r in right_refs]), left_ref[...])
        for k, m in enumerate(place.masks):
            start = pl.multiple_of((order_ref[blocks] ^ m) * part, part & -part)
            out_refs[k][0] = value_ref[pl.ds(start, part), :].astype(BF16)

    return pl.pallas_call(
        body,
        out_shape=[jax.ShapeDtypeStruct((blocks, part, block), BF16)] * nc,
        grid_spec=pltpu.PrefetchScalarGridSpec(
            num_scalar_prefetch=1,
            grid=(blocks,),
            in_specs=[pl.BlockSpec((left.shape[0], block), lambda i, ix: (0, ix[i]))]
            + [pl.BlockSpec(v.shape, lambda i, ix: (0, 0)) for v in rights],
            out_specs=[pl.BlockSpec((1, part, block), lambda i, ix: (i, 0, 0))] * nc,
            scratch_shapes=[pltpu.VMEM((width, block), F32)],
        ),
        compiler_params=params(),
        cost_estimate=cost(),
        name="out_weight_grads",
    )(order, left, *rights)


def joined_rows(parts):
    return parts[0] if len(parts) == 1 else jnp.concatenate(parts, 0)


def rope_tables(positions):
    steps_half = jnp.arange(HD // 2, dtype=F32)
    inverse = jnp.exp(steps_half * (-2.0 * math.log(ROPE_BASE) / HD))
    angles = positions.astype(F32)[:, None] * inverse[None, :]
    return jnp.tile(jnp.cos(angles), (1, 4)), jnp.tile(jnp.sin(angles), (1, 4))


def make_layer(place):
    nd, nc, nf, nn_, masks = place.nd, place.nc, place.nf, place.nn, place.masks
    half = nc // 2

    def per_device(
        layer_input,
        lengths,
        attn_gain,
        w_query,
        w_key,
        w_value,
        query_gain,
        key_gain,
        w_out,
        ffn_gain,
        w_gate,
        w_up,
        w_down,
        cotangent,
    ):
        rows, slots, depth = layer_input.shape
        n = rows * slots
        block = depth // nd
        qc, kc, oc, units = w_query.shape[1], w_key.shape[1], w_out.shape[1], w_gate.shape[1]
        per = rows if slots % LANES == 0 else 1
        far, near = lax.axis_index("far"), lax.axis_index("near")
        spot = lax.axis_index("ctx")
        fars = jnp.arange(nf, dtype=jnp.int32)
        to_near = [place.block(fars, near ^ i) for i in range(nn_)]
        to_near_far = [place.block(far ^ fars, near ^ i) for i in range(nn_)]
        everywhere = jnp.arange(nd, dtype=jnp.int32)
        every = jnp.concatenate([*to_near, spot[None].astype(jnp.int32)], 0)
        positions = spot * slots + jnp.arange(slots, dtype=jnp.int32)
        cosine, sine = rope_tables(positions)
        info = jnp.concatenate([spot[None].astype(jnp.int32), lengths])
        valid = (positions[None, :] < lengths[:, None]).astype(F32).reshape(n, 1)
        qgain2 = jnp.tile(query_gain, 2)[None, :]
        kgain2 = jnp.tile(key_gain, 2)[None, :]
        gain_one, gain_two = attn_gain[None, :], ffn_gain[None, :]
        x = layer_input.reshape(n, depth)

        def gather_dp(value, tiled):
            return lax.all_gather(value, place.dp, axis=0, tiled=tiled)

        bg = (cotangent.reshape(n, depth).astype(F32) * valid).astype(BF16)
        qkv_dp = gather_dp(jnp.concatenate([w_query.T, w_key.T, w_value.T], 0), False)
        qkv_cross = place.cross(
            qkv_dp, bg, info, valid, cosine, sine, qgain2, kgain2, *to_near, every
        )
        qkv_cols = place.gather(qkv_cross)
        out_dp = gather_dp(after(w_out.T, qkv_dp), False)
        out_cross = place.cross(after(out_dp, *place.arrived(qkv_cross)))
        sizes = [512, 512, 256] if units == 1280 else [units]
        starts = [sum(sizes[:c]) for c in range(len(sizes))]
        chunks = []
        for start, size in zip(starts, sizes):
            at = slice(start, start + size)
            local = jnp.concatenate([w_gate[:, at], w_up[:, at], w_down[:, at]], 0)
            chunks.append(gather_dp(after(local, qkv_dp), True))

        normed, lin, q, kv = project(
            info, place, x, gain_one, qkv_cols, qc, kc, qgain2, kgain2, cosine, sine, rows, slots
        )
        out_cols = place.gather(out_cross, q)
        kv_cross = place.cross(kv)
        kv_all = place.gather(kv_cross)
        bg_cross = place.cross(after(bg, *place.arrived(kv_cross)))
        bg_all = place.gather(bg_cross)
        mixed_t, lse, middles, n2_cross = [], [], [], []
        before, due = place.arrived(out_cross), []
        for r in range(rows):
            m, mt, l = attend(info, after(q, *before), kv_all, masks, r, slots)
            if r == rows - 1:
                due = due + place.arrived(bg_cross)
            mid, n2 = out_project(info, place, after(m, *due), x, gain_two, out_cols, r)
            mixed_t.append(mt)
            lse.append(l)
            middles.append(mid)
            before, due = [mid], []
            if per == rows:
                n2_cross.append(place.cross(n2))
                due = place.arrived(n2_cross[-1])
            else:
                n2_cross.append(n2)
        if per != rows:
            n2_cross = [place.cross(jnp.concatenate(n2_cross, 0))]

        sides = {"near": slice(0, half), "far": slice(half, nc)}
        sums = {"near": None, "far": None}
        ffn_grads, last_out = [], []
        n2_near = [[c[m] for c in n2_cross] for m in masks[:half] if m in n2_cross[0]]
        n2_all = None

        def whole(sets, size):
            part = weight_grads(after(everywhere, *last_out), block, sets, size)
            own = lax.psum_scatter(
                part.reshape(nd * 3 * size, block), place.dp, scatter_dimension=0, tiled=True
            )
            ffn_grads.append(own.reshape(3, size, block))
            return part

        def send(sets, size):
            got = None
            for i in range(1, nn_):
                mine = weight_grads(after(to_near[i], *last_out), block, sets, size)
                part = swap(mine, "near", nn_, i)
                got = part if got is None else got + part
            return mine, (sets, size, got)

        def keep(entry):
            sets, size, got = entry
            part = weight_grads(after(to_near[0], *last_out), block, sets, size, got)
            own = lax.psum_scatter(
                part.reshape(nf * 3 * size, block), "far", scatter_dimension=0, tiled=True
            )
            ffn_grads.append(own.reshape(3, size, block))
            return part

        def scatter_core_of(k, *hold):
            pieces = [after(s[k], *hold) for s in (*sums["near"], *sums["far"])]
            return place.scatter_core(dict(zip(masks, pieces)))

        waiting = []
        for c, weights in enumerate(chunks):
            acts = None
            for side in ("far", "near") if c == len(chunks) - 1 and c else ("near", "far"):
                at = sides[side]
                if n2_all is None and len(n2_near) < half:
                    n2_all = [place.gather(v) for v in n2_cross]
                    n2_all = [[v[i] for v in n2_all] for i in range(nc)]
                sums[side], acts = feed_forward(
                    after(info, *last_out), place, weights, (n2_all or n2_near)[at], bg_all[at],
                    sums[side], acts, nc * n, at.start, c == len(chunks) - 1,
                )
                last_out = [acts[0]]
                if n2_all is None:
                    n2_all = [place.gather(v, acts[0]) for v in n2_cross]
                    n2_all = [[v[i] for v in n2_all] for i in range(nc)]
            h, gg, ug = [[a] for a in acts]
            n2_flat = [v for group in n2_all for v in group]
            sets = [(n2_flat, [gg, ug]), (bg_all, [h])]
            if c == 0:
                normed_cross = place.cross(after(normed, acts[0]))
            if c == 1:
                last_out = last_out + place.arrived(normed_cross)
            if c == len(chunks) - 1:
                grads, _ = scatter_core_of(1)
                grad_parts = [grads[0]] + place.send_outer(grads)
                last_out = last_out + [grads[m] for m in place.combos[1:]]
            if c == 0 or nn_ == 1:
                last_out = [whole(sets, sizes[c])]
            else:
                mine, entry = send(sets, sizes[c])
                waiting.append(entry)
                last_out = [mine]
        normed_got = place.gather(normed_cross, *last_out)

        branches, _ = scatter_core_of(0, *last_out)
        branch_far = [branches[m] for m in place.combos[1:]]
        last_out = last_out + branch_far
        middle_grad, attn_grad, mixed_grad, gf = middle_back(
            after(info, *last_out), place, grad_parts, middles, bg, gain_two, out_cols, rows, slots
        )
        branch_got = place.send_outer({m: after(b, middle_grad) for m, b in branches.items()})
        w_out_all = out_weight_grads(after(every, mixed_grad), place, block, attn_grad, mixed_t)
        w_out_core, _ = place.scatter_core(dict(zip(masks, w_out_all)))
        dqs, cores = [], []
        last_out = [mixed_grad, w_out_all[0]]
        for r in range(rows):
            dq, *dkv = attend_back(
                after(info, *last_out), q, kv_all, mixed_grad, lse[r], masks, r, slots
            )
            dqs.append(dq)
            last_out = [dq]
            if waiting:
                last_out = [keep(waiting.pop(0))]
            if r == 0:
                last_out = last_out + [w_out_core[m] for m in place.combos[1:]]
                w_out_got = place.send_outer({m: after(b, dq) for m, b in w_out_core.items()})
                last_out = last_out + ffn_grads[:1]
            cores.append(place.scatter_core(dict(zip(masks, dkv)), F32))
        dkvs = [[core[0], *place.send_outer(core)] for core, _ in cores]

        out_rows = finish_rows(
            middles, [branches[0], *branch_got], valid
        )
        last_out = last_out + [core[m] for core, _ in cores for m in place.combos[1:]]
        last_out = last_out + ffn_grads[1:2] + branch_got

        input_grads, dlin_got, ga, gq, gk = [], [], [], [], []
        for r in range(rows):
            ig, ga_r, gq_r, gk_r, *dlin = project_back(
                after(info, *last_out), place, dqs[r], dkvs[r], lin, x, middle_grad, gain_one, qkv_cols,
                qc, kc, qgain2, kgain2, cosine, sine, r, slots,
            )
            last_out = [ig, out_rows, *w_out_got]
            input_grads.append(ig)
            dlin_got.append(place.exchange(dlin))
            ga.append(ga_r[0])
            gq.append(gq_r[0])
            gk.append(gk_r[0])
        halves = combine(
            [w_out_core[0], *[after(g, input_grads[0]) for g in w_out_got]], BF16, nn_
        )
        halves = [halves[0]] + [
            swap(h, "near", nn_, i) for i, h in enumerate(halves[1:], 1)
        ]
        w_out_half = combine([halves[0], *[after(h, input_grads[-1]) for h in halves[1:]]], BF16)[0]
        w_out_grad = lax.psum_scatter(
            w_out_half.reshape(nf * oc, block), "far", scatter_dimension=0, tiled=True
        )

        def summed(parts):
            total = parts[0].astype(F32)
            for p in parts[1:]:
                total = total + p.astype(F32)
            return total[0]

        right = [dlin_got[r][i] for i in range(nc) for r in range(rows)]
        if per != rows:
            right = [jnp.concatenate(right, 1)]
        got = None
        for i in reversed(range(nn_)):
            part = weight_grads(
                to_near_far[i], block, [(normed_got, [right])], qc + 2 * kc,
                got if i == 0 else None, i == 0,
            )
            if i:
                part = swap(part, "near", nn_, i)
                got = part if got is None else got + part
        w_qkv_grad = summed([part[0]] + [swap(part[m], "far", nf, m) for m in range(1, nf)])
        gains = place.total(after(jnp.concatenate([sum(ga), gf[0], sum(gq), sum(gk)]), part[0]))
        gq = gains[2 * depth : 2 * depth + LANES]
        gk = gains[2 * depth + LANES :]

        grads = None
        for own, start in zip(ffn_grads, starts):
            grads = finish_grads(own, start, units, grads)
        return (
            out_rows.reshape(rows, slots, depth),
            jnp.stack(input_grads, 0),
            gains[:depth],
            w_qkv_grad[:qc].T,
            w_qkv_grad[qc : qc + kc].T,
            w_qkv_grad[qc + kc :].T,
            gq[:HD] + gq[HD:],
            gk[:HD] + gk[HD:],
            w_out_grad.astype(F32).T,
            gains[depth : 2 * depth],
            grads[0],
            grads[1],
            grads[2],
        )

    return per_device


def solution(mesh):
    place = Place(mesh)
    wide = P(place.dp, "ctx")
    rows = P(place.dp, "ctx", None)
    in_specs = (
        rows, P(place.dp), P(), wide, wide, wide, P(), P(), wide, P(), wide, wide, wide, rows,
    )
    out_specs = (
        rows, rows, P(), wide, wide, wide, P(), P(), wide, P(), wide, wide, wide,
    )
    return jax.shard_map(
        make_layer(place),
        mesh=place.mesh,
        in_specs=in_specs,
        out_specs=out_specs,
        check_vma=False,
    )
```

```python
import math

import jax
import jax.numpy as jnp
import numpy as np
from jax import lax
from jax.experimental import pallas as pl
from jax.experimental.pallas import tpu as pltpu
from jax.sharding import Mesh, PartitionSpec as P

HQ = 20
KVH = 5
HD = 64
GROUP = HQ // KVH
QW = HQ * HD
KVW = KVH * HD
GW = GROUP * HD
LANES = 2 * HD
NEG = -1e30
EPSILON = 1e-06
ROPE_BASE = 10000.0
F32 = jnp.float32
BF16 = jnp.bfloat16
VMEM_LIMIT = 60 << 20


def nn(a, b):
    return lax.dot_general(a, b, (((1,), (0,)), ((), ())), preferred_element_type=F32)


def nt(a, b):
    return lax.dot_general(a, b, (((1,), (1,)), ((), ())), preferred_element_type=F32)


def tn(a, b):
    return lax.dot_general(a, b, (((0,), (0,)), ((), ())), preferred_element_type=F32)


def cost(**_):
    return pl.CostEstimate(flops=1, bytes_accessed=1, transcendentals=0)


def params(limit=VMEM_LIMIT):
    return pltpu.CompilerParams(vmem_limit_bytes=limit)


def after(value, *others):
    return lax.optimization_barrier((value, *others))[0] if others else value


def swap(value, axis, size, mask):
    return lax.ppermute(value, axis, [(i, i ^ mask) for i in range(size)])


class Place:
    def __init__(self, mesh):
        grid = mesh.devices
        self.nd, self.nc = mesh.shape["dp"], mesh.shape["ctx"]
        first = tuple(grid[0, 0].coords)
        bits = [1 << i for i in range(self.nd.bit_length() - 1)]
        far = [b for b in bits if tuple(grid[b, 0].coords)[2] != first[2]]
        self.nf = 1 << len(far)
        self.nn = self.nd // self.nf
        self.far_low = 1 in far
        bits = [1 << i for i in range(self.nc.bit_length() - 1)]
        self.core = [b for b in bits if tuple(grid[0, b].coords) == first]
        self.outer = [b for b in bits if b not in self.core]
        shape = (self.nn, self.nf) if self.far_low else (self.nf, self.nn)
        self.dp = ("near", "far") if self.far_low else ("far", "near")
        self.mesh = Mesh(grid.reshape(*shape, self.nc), (*self.dp, "ctx"))
        combos = [0]
        for bit in self.outer:
            combos = combos + [c | bit for c in combos]
        self.combos = combos
        masks = list(combos)
        for bit in self.core:
            masks = [m for pair in masks for m in (pair, pair | bit)]
        self.masks = masks

    def block(self, far, near):
        return near * self.nf + far if self.far_low else far * self.nn + near

    def cross(self, own, *first):
        held = {m: swap(own, "ctx", self.nc, m) if m else own for m in self.combos}
        for bit in self.core:
            held[bit] = swap(after(own, *first), "ctx", self.nc, bit)
        return held

    def gather(self, held, *hold):
        if not isinstance(held, dict):
            held = self.cross(held)
        held = dict(held)
        for bit in self.core:
            for m in self.combos[1:]:
                held[m | bit] = swap(after(held[m], *hold), "ctx", self.nc, bit)
        return [held[m] for m in self.masks]

    def arrived(self, held):
        return [v for m, v in held.items() if m]

    def exchange(self, blocks):
        return [blocks[0]] + [
            swap(b, "ctx", self.nc, m) for b, m in zip(blocks[1:], self.masks[1:])
        ]

    def scatter_core(self, blocks, kind=BF16):
        came = []
        for bit in self.core:
            kept = {}
            for m in blocks:
                if not m & bit:
                    got = swap(blocks[m | bit].astype(BF16), "ctx", self.nc, bit)
                    came.append(got)
                    kept[m] = combine([blocks[m], got], BF16 if m else kind)[0]
            blocks = kept
        return blocks, came

    def total(self, value):
        got = [swap(value, "ctx", self.nc, m) for m in range(1, self.nc)]
        return sum(got, value), got

    def total_dp(self, value, *hold):
        value = sum([swap(value, "far", self.nf, m) for m in range(1, self.nf)], value)
        value = after(value, *hold)
        return sum([swap(value, "near", self.nn, m) for m in range(1, self.nn)], value)

    def send_outer(self, blocks):
        return [swap(b, "ctx", self.nc, m) for m, b in blocks.items() if m]


def combine(parts, kind, pieces=1):
    shape = parts[0].shape
    tile = 256 if pieces == 1 and shape[0] % 256 == 0 else shape[0]
    block = (tile, *shape[1:])
    out = (shape[0] // pieces, *shape[1:])
    step = tile // pieces

    def body(*refs):
        part_refs, out_refs = refs[: len(parts)], refs[len(parts) :]
        for i, o in enumerate(out_refs):
            at = slice(i * step, (i + 1) * step)
            value = part_refs[0][at].astype(F32)
            for r in part_refs[1:]:
                value = value + r[at].astype(F32)
            o[...] = value.astype(kind)

    index = lambda i: (i,) + (0,) * (len(shape) - 1)
    return pl.pallas_call(
        body,
        out_shape=[jax.ShapeDtypeStruct(out, kind)] * pieces,
        grid=(shape[0] // tile,),
        in_specs=[pl.BlockSpec(block, index)] * len(parts),
        out_specs=[pl.BlockSpec((step, *shape[1:]), index)] * pieces,
        compiler_params=params(),
        cost_estimate=cost(),
        name="combine",
    )(*parts)


def finish_rows(middles, parts, valid):
    rows, (slots, depth) = len(middles), middles[0].shape

    def body(valid_ref, *refs):
        mid_refs, part_refs, out_ref = refs[:rows], refs[rows:-1], refs[-1]
        step = pl.program_id(0)
        y = mid_refs[0][...]
        for r in range(1, rows):
            y = jnp.where(step >= r, mid_refs[r][...], y)
        for p in part_refs:
            y = y + p[...].astype(F32)
        out_ref[...] = (y * valid_ref[...]).astype(BF16)

    whole = lambda i: (0, 0)
    by_row = lambda i: (i, 0)
    return pl.pallas_call(
        body,
        out_shape=jax.ShapeDtypeStruct((rows * slots, depth), BF16),
        grid=(rows,),
        in_specs=[pl.BlockSpec((slots, 1), by_row)]
        + [pl.BlockSpec((slots, depth), whole)] * rows
        + [pl.BlockSpec((slots, depth), by_row)] * len(parts),
        out_specs=pl.BlockSpec((slots, depth), by_row),
        compiler_params=params(),
        cost_estimate=cost(),
        name="finish_rows",
    )(valid, *middles, *parts)


def finish_grads(own, start, width, previous):
    many, units, block = own.shape
    tile = 256 if units % 256 == 0 else units

    def body(own_ref, *refs):
        for k in range(many):
            refs[-many + k][...] = own_ref[k].astype(F32).T

    extra = [] if previous is None else list(previous)
    return pl.pallas_call(
        body,
        out_shape=[jax.ShapeDtypeStruct((block, width), F32)] * many,
        grid=(units // tile,),
        in_specs=[pl.BlockSpec((many, tile, block), lambda i: (0, i, 0))]
        + [pl.BlockSpec(memory_space=pl.ANY)] * len(extra),
        out_specs=[pl.BlockSpec((block, tile), lambda i: (0, start // tile + i))] * many,
        input_output_aliases={1 + k: k for k in range(len(extra))},
        compiler_params=params(),
        cost_estimate=cost(),
        name="finish_grads",
    )(own, *extra)


def head_stats(x, low):
    return lax.rsqrt(head_mean(x * x, low) + EPSILON)


def head_mean(x, low):
    first = jnp.sum(jnp.where(low, x, 0.0), -1, keepdims=True)
    second = jnp.sum(jnp.where(low, 0.0, x), -1, keepdims=True)
    return jnp.where(low, first, second) * (1.0 / HD)


def lane_masks(rows):
    lane = lax.broadcasted_iota(jnp.int32, (rows, LANES), 1)
    return lane < HD, lax.rem(lane, HD) < HD // 2


def spans(start, stop, width):
    out = []
    while start < stop:
        j = start // width
        end = min(stop, (j + 1) * width)
        out.append((j, start - j * width, end - j * width))
        start = end
    return out


def joined(parts):
    return parts[0] if len(parts) == 1 else jnp.concatenate(parts, 1)


def slot_copies(info_ref, place, w_refs, slots_ref, sem):
    copies = []
    for k, m in enumerate(place.masks):
        block = w_refs[k].shape[2]
        for i in range(place.nd):
            copies.append(
                pltpu.make_async_copy(
                    w_refs[k].at[i],
                    slots_ref.at[info_ref[0] ^ m, :, i * block : (i + 1) * block],
                    sem.at[len(copies)],
                )
            )
    return copies


def load_slots(*args):
    copies = slot_copies(*args)
    for c in copies:
        c.start()
    for c in copies:
        c.wait()


def project(info, place, x, gain, w_cols, qc, kc, qgain, kgain, cosine, sine, rows, slots):
    nc, depth, wc = place.nc, x.shape[1], w_cols[0].shape[-2]
    n = rows * slots

    def body(info_ref, x_ref, gain_ref, qgain_ref, kgain_ref, cos_ref, sin_ref, *refs):
        w_refs, (normed_ref, lin_ref, q_ref, kv_ref, w_ref, sem) = refs[:nc], refs[nc:]

        @pl.when(pl.program_id(0) == 0)
        def _():
            load_slots(info_ref, place, w_refs, w_ref, sem)

        xf = x_ref[...].astype(F32)
        inv = lax.rsqrt(jnp.mean(xf * xf, -1, keepdims=True) + EPSILON)
        normed_ref[...] = (xf * inv * gain_ref[...]).astype(BF16)
        for j in range(nc):
            lin_ref[j] = nt(normed_ref[...], w_ref[j])
        low, front = lane_masks(slots)
        cos, sin = cos_ref[...], sin_ref[...]

        def columns(base, width, start, stop):
            return [lin_ref[j, :, base + a : base + b] for j, a, b in spans(start, stop, width)]

        def turn(v, gain):
            v = v * head_stats(v, low) * gain
            turned = jnp.where(
                front, -pltpu.roll(v, LANES - HD // 2, 1), pltpu.roll(v, HD // 2, 1)
            )
            return v * cos + turned * sin

        for c in range(QW // LANES):
            at = slice(c * LANES, (c + 1) * LANES)
            y = turn(joined(columns(0, qc, at.start, at.stop)), qgain_ref[...])
            q_ref[:, at] = (y * (1.0 / math.sqrt(HD))).astype(BF16)
        for g in range(KVH):
            v = joined(
                columns(qc, kc, g * HD, (g + 1) * HD) + columns(qc + kc, kc, g * HD, (g + 1) * HD)
            )
            y = jnp.where(low, turn(v, kgain_ref[...]), v)
            kv_ref[:, g * LANES : (g + 1) * LANES] = y.astype(BF16)

    whole = lambda r, s: (0, 0)
    by_row = lambda r, s: (r, 0)
    return pl.pallas_call(
        body,
        out_shape=(
            jax.ShapeDtypeStruct((n, depth), BF16),
            jax.ShapeDtypeStruct((nc, n, wc), F32),
            jax.ShapeDtypeStruct((n, QW), BF16),
            jax.ShapeDtypeStruct((n, 2 * KVW), BF16),
        ),
        grid_spec=pltpu.PrefetchScalarGridSpec(
            num_scalar_prefetch=1,
            grid=(rows,),
            in_specs=[
                pl.BlockSpec((slots, depth), by_row),
                pl.BlockSpec((1, depth), whole),
                pl.BlockSpec((1, LANES), whole),
                pl.BlockSpec((1, LANES), whole),
                pl.BlockSpec((slots, LANES), whole),
                pl.BlockSpec((slots, LANES), whole),
            ]
            + [pl.BlockSpec(memory_space=pl.ANY)] * nc,
            out_specs=(
                pl.BlockSpec((slots, depth), by_row),
                pl.BlockSpec((nc, slots, wc), lambda r, s: (0, r, 0)),
                pl.BlockSpec((slots, QW), by_row),
                pl.BlockSpec((slots, 2 * KVW), by_row),
            ),
            scratch_shapes=[
                pltpu.VMEM((nc, wc, depth), BF16),
                pltpu.SemaphoreType.DMA((nc * place.nd,)),
            ],
        ),
        compiler_params=params(),
        cost_estimate=cost(
            flops=2 * n * depth * nc * wc, bytes_accessed=2 * nc * depth * wc, transcendentals=n
        ),
        name="project",
    )(info, x, gain, qgain, kgain, cosine, sine, *w_cols)


def heads_back(info, place, dq, dkv_parts, lin, qc, kc, qgain, kgain, cosine, sine, row, slots):
    nc, wc = place.nc, lin.shape[2]

    def body(info_ref, dq_ref, lin_ref, qgain_ref, kgain_ref, cos_ref, sin_ref, *refs):
        dkv_refs, refs = refs[: len(dkv_parts)], refs[len(dkv_parts) :]
        out_ref, gq_ref, gk_ref = refs[:3]
        dlin_refs, (dqs, dks, dvs, dlin_ref) = refs[3 : 3 + nc], refs[3 + nc :]
        low, front = lane_masks(slots)
        cos, sin = cos_ref[...], sin_ref[...]

        def columns(base, width, start, stop):
            return [lin_ref[j, :, base + a : base + b] for j, a, b in spans(start, stop, width)]

        def back(e, v, gain):
            t = e * sin
            e = e * cos + jnp.where(
                front, pltpu.roll(t, LANES - HD // 2, 1), -pltpu.roll(t, HD // 2, 1)
            )
            inv = head_stats(v, low)
            unit = v * inv
            part = e * unit
            u = e * gain
            return inv * (u - unit * head_mean(u * unit, low)), part

        gq = jnp.zeros((1, LANES), F32)
        for c in range(QW // LANES):
            at = slice(c * LANES, (c + 1) * LANES)
            v = joined(columns(0, qc, at.start, at.stop))
            y, part = back(dq_ref[:, at], v, qgain_ref[...])
            dqs[:, at] = y
            gq = gq + jnp.sum(part, 0, keepdims=True)
        gk = jnp.zeros((1, LANES), F32)
        for g in range(KVH):
            e = dkv_refs[0][:, g * LANES : (g + 1) * LANES].astype(F32)
            for ref in dkv_refs[1:]:
                e = e + ref[:, g * LANES : (g + 1) * LANES].astype(F32)
            v = joined(
                columns(qc, kc, g * HD, (g + 1) * HD) + columns(qc + kc, kc, g * HD, (g + 1) * HD)
            )
            y, part = back(e, v, kgain_ref[...])
            dks[:, g * HD : (g + 1) * HD] = y[:, :HD]
            dvs[:, g * HD : (g + 1) * HD] = e[:, HD:]
            gk = gk + jnp.sum(jnp.where(low, part, 0.0), 0, keepdims=True)
        gq_ref[...] = gq
        gk_ref[...] = gk
        for j in range(nc):
            dlin = jnp.concatenate(
                [
                    dqs[:, j * qc : (j + 1) * qc],
                    dks[:, j * kc : (j + 1) * kc],
                    dvs[:, j * kc : (j + 1) * kc],
                ],
                1,
            )
            out_ref[j] = dlin.astype(BF16)
            dlin_ref[j] = dlin.T.astype(BF16)
        for k, m in enumerate(place.masks):
            dlin_refs[k][...] = dlin_ref[info_ref[0] ^ m]

    whole = lambda i, s: (0, 0)
    cube = lambda i, s: (0, 0, 0)
    lane = pl.BlockSpec((1, LANES), whole)
    table = pl.BlockSpec((slots, LANES), whole)
    return pl.pallas_call(
        body,
        out_shape=(
            jax.ShapeDtypeStruct((nc, slots, wc), BF16),
            jax.ShapeDtypeStruct((1, LANES), F32),
            jax.ShapeDtypeStruct((1, LANES), F32),
            *([jax.ShapeDtypeStruct((wc, slots), BF16)] * nc),
        ),
        grid_spec=pltpu.PrefetchScalarGridSpec(
            num_scalar_prefetch=1,
            grid=(1,),
            in_specs=[
                pl.BlockSpec((slots, QW), whole),
                pl.BlockSpec((nc, slots, wc), lambda i, s: (0, row, 0)),
                lane,
                lane,
                table,
                table,
            ]
            + [pl.BlockSpec((slots, 2 * KVW), whole)] * len(dkv_parts),
            out_specs=(
                pl.BlockSpec((nc, slots, wc), cube),
                lane,
                lane,
                *([pl.BlockSpec((wc, slots), whole)] * nc),
            ),
            scratch_shapes=[
                pltpu.VMEM((slots, QW), F32),
                pltpu.VMEM((slots, KVW), F32),
                pltpu.VMEM((slots, KVW), F32),
                pltpu.VMEM((nc, wc, slots), BF16),
            ],
        ),
        compiler_params=params(),
        cost_estimate=cost(),
        name="heads_back",
    )(info, dq, lin, qgain, kgain, cosine, sine, *dkv_parts)


def project_back(info, place, dlins, x, middle_grad, gain, w_cols, rows, slots):
    nc, depth, wc = place.nc, x.shape[1], w_cols[0].shape[-2]

    def body(info_ref, x_ref, mid_ref, gain_ref, *refs):
        dlin_refs, refs = refs[:rows], refs[rows:]
        w_refs, (out_ref, ga_ref, w_ref, sem) = refs[:nc], refs[nc:]
        step = pl.program_id(0)

        @pl.when(step == 0)
        def _():
            load_slots(info_ref, place, w_refs, w_ref, sem)
            ga_ref[...] = jnp.zeros_like(ga_ref)

        grad = None
        for j in range(nc):
            dlin = dlin_refs[0][j]
            for r in range(1, rows):
                dlin = jnp.where(step >= r, dlin_refs[r][j], dlin)
            part = nn(dlin, w_ref[j])
            grad = part if grad is None else grad + part
        xf = x_ref[...].astype(F32)
        inv = lax.rsqrt(jnp.mean(xf * xf, -1, keepdims=True) + EPSILON)
        unit = xf * inv
        ga_ref[...] += jnp.sum(grad * unit, 0, keepdims=True)
        u = grad * gain_ref[...]
        back_x = inv * (u - unit * jnp.mean(u * unit, -1, keepdims=True))
        out_ref[...] = (mid_ref[...] + back_x).astype(BF16)

    whole = lambda i, s: (0, 0)
    by_row = lambda i, s: (i, 0)
    return pl.pallas_call(
        body,
        out_shape=(
            jax.ShapeDtypeStruct((rows * slots, depth), BF16),
            jax.ShapeDtypeStruct((1, depth), F32),
        ),
        grid_spec=pltpu.PrefetchScalarGridSpec(
            num_scalar_prefetch=1,
            grid=(rows,),
            in_specs=[
                pl.BlockSpec((slots, depth), by_row),
                pl.BlockSpec((slots, depth), by_row),
                pl.BlockSpec((1, depth), whole),
            ]
            + [pl.BlockSpec((nc, slots, wc), lambda i, s: (0, 0, 0))] * rows
            + [pl.BlockSpec(memory_space=pl.ANY)] * nc,
            out_specs=(pl.BlockSpec((slots, depth), by_row), pl.BlockSpec((1, depth), whole)),
            scratch_shapes=[
                pltpu.VMEM((nc, wc, depth), BF16),
                pltpu.SemaphoreType.DMA((nc * place.nd,)),
            ],
        ),
        compiler_params=params(),
        cost_estimate=cost(),
        name="project_back",
    )(info, x, middle_grad, gain, *dlins, *w_cols)


def fill_bias(bias_ref, info_ref, row, masks, slots):
    place, length = info_ref[0], info_ref[1 + row]
    query = place * slots + lax.broadcasted_iota(jnp.int32, (slots, slots), 1)
    for i, mask in enumerate(masks):
        key = (place ^ mask) * slots + lax.broadcasted_iota(jnp.int32, (slots, slots), 0)
        allowed = (key <= query) & (key < length)
        bias_ref[i * slots : (i + 1) * slots, :] = jnp.where(allowed, 0.0, NEG)


def attend(info, q, kv_pieces, masks, row, slots):
    count = len(masks)
    keys = count * slots

    def body(info_ref, q_ref, *refs):
        kv_refs, (o_ref, ot_ref, lse_ref, bias_ref) = refs[:count], refs[count:]
        live = info_ref[0] * slots < info_ref[1 + row]

        @pl.when(live & (pl.program_id(0) == 0))
        def _():
            fill_bias(bias_ref, info_ref, row, masks, slots)

        @pl.when(jnp.logical_not(live))
        def _():
            o_ref[...] = jnp.zeros_like(o_ref)
            ot_ref[...] = jnp.zeros_like(ot_ref)
            lse_ref[...] = jnp.zeros_like(lse_ref)

        @pl.when(live)
        def _():
            kv = jnp.concatenate([r[...] for r in kv_refs], 0)
            k, v = kv[:, :HD], kv[:, HD:]
            for h in range(GROUP):
                qh = q_ref[:, h * HD : (h + 1) * HD]
                e = jnp.exp(nt(k, qh) + bias_ref[...])
                l = jnp.sum(e, 0, keepdims=True)
                o = tn(v, (e * (1.0 / l)).astype(BF16))
                o_ref[:, h * HD : (h + 1) * HD] = o.T.astype(BF16)
                ot_ref[h * HD : (h + 1) * HD, :] = o.astype(BF16)
                lse_ref[0, h : h + 1, :] = jnp.log(l)

    n = slots
    return pl.pallas_call(
        body,
        out_shape=(
            jax.ShapeDtypeStruct((n, QW), BF16),
            jax.ShapeDtypeStruct((QW, n), BF16),
            jax.ShapeDtypeStruct((KVH, GROUP, slots), F32),
        ),
        grid_spec=pltpu.PrefetchScalarGridSpec(
            num_scalar_prefetch=1,
            grid=(KVH,),
            in_specs=[pl.BlockSpec((slots, GW), lambda g, s: (row, g))]
            + [pl.BlockSpec((slots, LANES), lambda g, s: (row, g))] * count,
            out_specs=(
                pl.BlockSpec((slots, GW), lambda g, s: (0, g)),
                pl.BlockSpec((GW, slots), lambda g, s: (g, 0)),
                pl.BlockSpec((1, GROUP, slots), lambda g, s: (g, 0, 0)),
            ),
            scratch_shapes=[pltpu.VMEM((keys, slots), F32)],
        ),
        compiler_params=params(),
        cost_estimate=cost(
            flops=16 * n * keys * QW, bytes_accessed=8 * n * QW, transcendentals=n * keys * HQ
        ),
        name="attend",
    )(info, q, *kv_pieces)


def attend_back(info, q, kv_pieces, do, lse, masks, row, slots):
    count = len(masks)
    keys = count * slots

    def body(info_ref, q_ref, do_ref, lse_ref, *refs):
        kv_refs, dq_ref = refs[:count], refs[count]
        dkv_refs, bias_ref = refs[count + 1 : -1], refs[-1]
        live = info_ref[0] * slots < info_ref[1 + row]

        @pl.when(live & (pl.program_id(0) == 0))
        def _():
            fill_bias(bias_ref, info_ref, row, masks, slots)

        @pl.when(jnp.logical_not(live))
        def _():
            dq_ref[...] = jnp.zeros_like(dq_ref)
            for r in dkv_refs:
                r[...] = jnp.zeros_like(r)

        @pl.when(live)
        def _():
            kv = jnp.concatenate([r[...] for r in kv_refs], 0)
            k, v = kv[:, :HD], kv[:, HD:]
            dk = jnp.zeros((keys, HD), F32)
            dv = jnp.zeros((keys, HD), F32)
            for h in range(GROUP):
                at = slice(h * HD, (h + 1) * HD)
                qh, doh = q_ref[:, at], do_ref[:, at]
                p = jnp.exp(nt(k, qh) + bias_ref[...] - lse_ref[0, h : h + 1, :])
                dp = nt(v, doh)
                delta = jnp.sum(p * dp, 0, keepdims=True)
                ds = (p * (dp - delta)).astype(BF16)
                dv = dv + nn(p.astype(BF16), doh)
                dk = dk + nn(ds, qh)
                dq_ref[:, at] = tn(k, ds).T * (1.0 / math.sqrt(HD))
            both = jnp.concatenate([dk, dv], 1).astype(BF16)
            for i, r in enumerate(dkv_refs):
                r[...] = both[i * slots : (i + 1) * slots, :]

    n = slots
    kv_spec = pl.BlockSpec((slots, LANES), lambda g, s: (row, g))
    q_spec = pl.BlockSpec((slots, GW), lambda g, s: (row, g))
    out_kv = pl.BlockSpec((slots, LANES), lambda g, s: (0, g))
    out_q = pl.BlockSpec((slots, GW), lambda g, s: (0, g))
    return pl.pallas_call(
        body,
        out_shape=(
            jax.ShapeDtypeStruct((n, QW), F32),
            *([jax.ShapeDtypeStruct((n, 2 * KVW), BF16)] * count),
        ),
        grid_spec=pltpu.PrefetchScalarGridSpec(
            num_scalar_prefetch=1,
            grid=(KVH,),
            in_specs=[
                q_spec,
                q_spec,
                pl.BlockSpec((1, GROUP, slots), lambda g, s: (g, 0, 0)),
            ]
            + [kv_spec] * count,
            out_specs=(out_q, *([out_kv] * count)),
            scratch_shapes=[pltpu.VMEM((keys, slots), F32)],
        ),
        compiler_params=params(),
        cost_estimate=cost(
            flops=40 * n * keys * QW, bytes_accessed=16 * n * QW, transcendentals=n * keys * HQ
        ),
        name="attend_back",
    )(info, q, do, lse, *kv_pieces)


def out_project(info, place, mixed, x, gain, w_cols, row):
    nc, depth, oc = place.nc, x.shape[1], w_cols[0].shape[-2]
    slots = mixed.shape[0]
    td = 256

    def body(info_ref, mixed_ref, x_ref, gain_ref, *refs):
        w_refs, (mid_ref, n2_ref, w_ref, sem) = refs[:nc], refs[nc:]
        load_slots(info_ref, place, w_refs, w_ref, sem)
        parts = [mixed_ref[:, j * oc : (j + 1) * oc] for j in range(nc)]
        square = jnp.zeros((slots, 1), F32)
        for d in range(depth // td):
            at = slice(d * td, (d + 1) * td)
            y = x_ref[:, at].astype(F32)
            for j in range(nc):
                y = y + nn(parts[j], w_ref[j, :, at])
            mid_ref[:, at] = y
            square = square + jnp.sum(y * y, -1, keepdims=True)
        inv = lax.rsqrt(square * (1.0 / depth) + EPSILON)
        n2_ref[...] = (mid_ref[...] * inv * gain_ref[...]).astype(BF16)

    whole = lambda i, s: (0, 0)
    return pl.pallas_call(
        body,
        out_shape=(
            jax.ShapeDtypeStruct((slots, depth), F32),
            jax.ShapeDtypeStruct((slots, depth), BF16),
        ),
        grid_spec=pltpu.PrefetchScalarGridSpec(
            num_scalar_prefetch=1,
            grid=(1,),
            in_specs=[
                pl.BlockSpec((slots, nc * oc), whole),
                pl.BlockSpec((slots, depth), lambda i, s: (row, 0)),
                pl.BlockSpec((1, depth), whole),
            ]
            + [pl.BlockSpec(memory_space=pl.ANY)] * nc,
            out_specs=(pl.BlockSpec((slots, depth), whole), pl.BlockSpec((slots, depth), whole)),
            scratch_shapes=[
                pltpu.VMEM((nc, oc, depth), BF16),
                pltpu.SemaphoreType.DMA((nc * place.nd,)),
            ],
        ),
        compiler_params=params(),
        cost_estimate=cost(
            flops=2 * slots * depth * nc * oc, bytes_accessed=4 * nc * depth * oc, transcendentals=0
        ),
        name="out_project",
    )(info, mixed, x, gain, *w_cols)


def middle_back(info, place, parts, middles, bg, gain, w_cols, rows, slots):
    nc, depth, oc, count = place.nc, bg.shape[1], w_cols[0].shape[-2], len(parts)
    n = rows * slots

    def body(info_ref, *refs):
        part_refs, refs = refs[:count], refs[count:]
        mid_refs, refs = refs[:rows], refs[rows:]
        bg_ref, gain_ref, refs = refs[0], refs[1], refs[2:]
        w_refs, (mg_ref, ag_ref, xg_ref, gf_ref, w_ref, sem) = refs[:nc], refs[nc:]
        step = pl.program_id(0)

        @pl.when(step == 0)
        def _():
            load_slots(info_ref, place, w_refs, w_ref, sem)
            gf_ref[...] = jnp.zeros_like(gf_ref)

        grad = part_refs[0][...].astype(F32)
        for p in part_refs[1:]:
            grad = grad + p[...].astype(F32)
        mid = mid_refs[0][...]
        for r in range(1, rows):
            mid = jnp.where(step >= r, mid_refs[r][...], mid)
        inv = lax.rsqrt(jnp.mean(mid * mid, -1, keepdims=True) + EPSILON)
        unit = mid * inv
        gf_ref[...] += jnp.sum(grad * unit, 0, keepdims=True)
        u = grad * gain_ref[...]
        y = bg_ref[...].astype(F32) + inv * (u - unit * jnp.mean(u * unit, -1, keepdims=True))
        mg_ref[...] = y
        ag_ref[...] = y.astype(BF16)
        xg_ref[...] = jnp.concatenate(
            [nt(ag_ref[...], w_ref[j]) for j in range(nc)], 1
        ).astype(BF16)

    whole = lambda i, s: (0, 0)
    by_row = lambda i, s: (i, 0)
    token = pl.BlockSpec((slots, depth), by_row)
    return pl.pallas_call(
        body,
        out_shape=(
            jax.ShapeDtypeStruct((n, depth), F32),
            jax.ShapeDtypeStruct((n, depth), BF16),
            jax.ShapeDtypeStruct((n, nc * oc), BF16),
            jax.ShapeDtypeStruct((1, depth), F32),
        ),
        grid_spec=pltpu.PrefetchScalarGridSpec(
            num_scalar_prefetch=1,
            grid=(rows,),
            in_specs=[token] * count
            + [pl.BlockSpec((slots, depth), whole)] * rows
            + [token, pl.BlockSpec((1, depth), whole)]
            + [pl.BlockSpec(memory_space=pl.ANY)] * nc,
            out_specs=(
                token,
                token,
                pl.BlockSpec((slots, nc * oc), by_row),
                pl.BlockSpec((1, depth), whole),
            ),
            scratch_shapes=[
                pltpu.VMEM((nc, oc, depth), BF16),
                pltpu.SemaphoreType.DMA((nc * place.nd,)),
            ],
        ),
        compiler_params=params(),
        cost_estimate=cost(
            flops=2 * n * depth * nc * oc, bytes_accessed=20 * n * depth, transcendentals=0
        ),
        name="middle_back",
    )(info, *parts, *middles, bg, gain, *w_cols)


def feed_forward(info, place, weights, n2, bg, sums, acts, total, first, last):
    owners, (tokens, depth), units = len(n2), bg[0].shape, weights.shape[1]
    cuts = len(n2[0])
    part = tokens // cuts
    block = depth // place.nd
    tu = 256 if units % 256 == 0 else units
    td = 256
    sum_type = BF16 if last else F32
    has_sums, has_acts = sums is not None, acts is not None

    def body(info_ref, w_ref, *refs):
        n2_refs, refs = refs[: owners * cuts], refs[owners * cuts :]
        bg_refs, refs = refs[:owners], refs[owners:]
        sum_refs = ()
        if has_sums:
            sum_refs, refs = refs[: 2 * owners], refs[2 * owners :]
        if has_acts:
            refs = refs[3:]
        out_refs, refs = refs[: 2 * owners], refs[2 * owners :]
        ht_ref, ggt_ref, ugt_ref, wg, wu, wd, acts_buf, tok_buf, out_buf = refs[:9]
        w_sem, tok_sem, out_sem = refs[9:12]
        in_buf, in_sem = refs[12:] if has_sums else (None, None)
        step = pl.program_id(0)
        slot = lax.rem(step, 2)

        def token_copies(p, to):
            found = [
                pltpu.make_async_copy(
                    n2_refs[p * cuts + i],
                    tok_buf.at[to, 0, i * part : (i + 1) * part, :],
                    tok_sem.at[to, i],
                )
                for i in range(cuts)
            ]
            return found + [
                pltpu.make_async_copy(bg_refs[p], tok_buf.at[to, 1], tok_sem.at[to, cuts])
            ]

        def sum_copies(p):
            return [
                pltpu.make_async_copy(sum_refs[2 * p + k], in_buf.at[k], in_sem.at[k])
                for k in range(2)
            ]

        def out_copies(p):
            return [
                pltpu.make_async_copy(out_buf.at[k], out_refs[2 * p + k], out_sem.at[k])
                for k in range(2)
            ]

        @pl.when(step == 0)
        def _():
            for c in token_copies(0, 0):
                c.start()
            copies = []
            for i in range(place.nd):
                for j, dst in enumerate((wg, wu, wd)):
                    start = (3 * i + j) * block
                    copies.append(
                        pltpu.make_async_copy(
                            w_ref.at[start : start + block, :],
                            dst.at[i * block : (i + 1) * block, :],
                            w_sem.at[len(copies)],
                        )
                    )
            for c in copies:
                c.start()
            for c in copies:
                c.wait()

        for p in range(owners):

            @pl.when(step == p)
            def _():
                if p + 1 < owners:
                    for c in token_copies(p + 1, (p + 1) % 2):
                        c.start()
                if has_sums:
                    for c in sum_copies(p):
                        c.start()

        for c in token_copies(0, slot):
            c.wait()
        x, b = tok_buf[slot, 0], tok_buf[slot, 1]
        for j in range(units // tu):
            at = slice(j * tu, (j + 1) * tu)
            gate, up = nn(x, wg[:, at]), nn(x, wu[:, at])
            dh = nn(b, wd[:, at])
            sig = 1.0 / (1.0 + jnp.exp(-gate))
            act = gate * sig
            h = act * up
            gg = dh * up * sig * (1.0 + gate * (1.0 - sig))
            ug = dh * act
            for k, (value, ref) in enumerate(((h, ht_ref), (gg, ggt_ref), (ug, ugt_ref))):
                acts_buf[k, :, at] = value.astype(BF16)
                ref[at, :] = value.T.astype(BF16)

        @pl.when(step > 0)
        def _():
            for c in out_copies(0):
                c.wait()

        if has_sums:
            for c in sum_copies(0):
                c.wait()
        h, gg, ug = acts_buf[0], acts_buf[1], acts_buf[2]
        for j in range(depth // td):
            at = slice(j * td, (j + 1) * td)
            values = [nt(h, wd[at, :]), nt(gg, wg[at, :]) + nt(ug, wu[at, :])]
            for k in range(2):
                value = values[k]
                if has_sums:
                    value = value + in_buf[k, :, at]
                out_buf[k, :, at] = value.astype(sum_type)
        for p in range(owners):

            @pl.when(step == p)
            def _():
                for c in out_copies(p):
                    c.start()

        @pl.when(step == owners - 1)
        def _():
            for c in out_copies(0):
                c.wait()

    any_spec = pl.BlockSpec(memory_space=pl.ANY)
    act_spec = pl.BlockSpec((units, tokens), lambda i, s: (0, i + first))
    operands = [weights, *[v for group in n2 for v in group], *bg]
    aliases = {}
    if has_sums:
        operands += [v for pair in sums for v in pair]
    if has_acts:
        for j in range(3):
            aliases[1 + len(operands) + j] = 2 * owners + j
        operands += acts
    n = owners * tokens
    scratch = [pltpu.VMEM((depth, units), BF16)] * 3 + [
        pltpu.VMEM((3, tokens, units), BF16),
        pltpu.VMEM((2, 2, tokens, depth), BF16),
        pltpu.VMEM((2, tokens, depth), sum_type),
        pltpu.SemaphoreType.DMA((3 * place.nd,)),
        pltpu.SemaphoreType.DMA((2, cuts + 1)),
        pltpu.SemaphoreType.DMA((2,)),
    ]
    if has_sums:
        scratch += [pltpu.VMEM((2, tokens, depth), F32), pltpu.SemaphoreType.DMA((2,))]
    out = pl.pallas_call(
        body,
        out_shape=(
            *([jax.ShapeDtypeStruct((tokens, depth), sum_type)] * (2 * owners)),
            *([jax.ShapeDtypeStruct((units, total), BF16)] * 3),
        ),
        grid_spec=pltpu.PrefetchScalarGridSpec(
            num_scalar_prefetch=1,
            grid=(owners,),
            in_specs=[any_spec] * len(operands),
            out_specs=(*([any_spec] * (2 * owners)), act_spec, act_spec, act_spec),
            scratch_shapes=scratch,
        ),
        input_output_aliases=aliases,
        compiler_params=params(),
        cost_estimate=cost(
            flops=12 * n * depth * units, bytes_accessed=16 * n * depth, transcendentals=n * units
        ),
        name="feed_forward",
    )(info, *operands)
    return [list(out[2 * o : 2 * o + 2]) for o in range(owners)], list(out[2 * owners :])


def weight_grads(order, block, sets, width, added=None, apart=False):
    lefts = [v for left, _ in sets for v in left]
    rights = [v for _, right in sets for group in right for v in group]
    many, blocks = sum(len(right) for _, right in sets), order.shape[0]

    def body(order_ref, *refs):
        left_refs, refs = refs[: len(lefts)], refs[len(lefts) :]
        right_refs, refs = refs[: len(rights)], refs[len(rights) :]
        extra_ref, out_refs = (None, refs) if added is None else (refs[0], refs[1:])
        i = k = at = 0
        for left, right in sets:
            tall = joined_rows([r[...] for r in left_refs[i : i + len(left)]])
            i += len(left)
            wides = []
            for group in right:
                wides.append(joined([r[...] for r in right_refs[at : at + len(group)]]))
                at += len(group)
            values = nn(joined_rows(wides), tall)
            for m in range(len(right)):
                value = values[m * width : (m + 1) * width]
                if added is not None:
                    value = value + extra_ref[0, k].astype(F32)
                if apart:
                    for f in range(blocks):

                        @pl.when(pl.program_id(0) == f)
                        def _():
                            out_refs[f][k] = value.astype(BF16)
                else:
                    out_refs[0][0, k] = value.astype(BF16)
                k += 1

    part = pl.BlockSpec((1, many, width, block), lambda i, ix: (i, 0, 0, 0))
    extra = [] if added is None else [added]
    if apart:
        shapes = [jax.ShapeDtypeStruct((many, width, block), BF16)] * blocks
        specs = [pl.BlockSpec((many, width, block), lambda i, ix: (0, 0, 0))] * blocks
    else:
        shapes = jax.ShapeDtypeStruct((blocks, many, width, block), BF16)
        specs = part
    return pl.pallas_call(
        body,
        out_shape=shapes,
        grid_spec=pltpu.PrefetchScalarGridSpec(
            num_scalar_prefetch=1,
            grid=(blocks,),
            in_specs=[pl.BlockSpec((v.shape[0], block), lambda i, ix: (0, ix[i])) for v in lefts]
            + [pl.BlockSpec((width, v.shape[1]), lambda i, ix: (0, 0)) for v in rights]
            + [part] * len(extra),
            out_specs=specs,
        ),
        compiler_params=params(),
        cost_estimate=cost(),
        name="weight_grads",
    )(order, *lefts, *rights, *extra)


def out_weight_grads(order, place, block, left, rights):
    nc, blocks = place.nc, order.shape[0] - 1
    width = rights[0].shape[0]
    part = width // nc

    def body(order_ref, left_ref, *refs):
        right_refs, refs = refs[: len(rights)], refs[len(rights) :]
        out_refs, value_ref = refs[:nc], refs[nc]
        value_ref[...] = nn(joined([r[...] for r in right_refs]), left_ref[...])
        for k, m in enumerate(place.masks):
            start = pl.multiple_of((order_ref[blocks] ^ m) * part, part & -part)
            out_refs[k][0] = value_ref[pl.ds(start, part), :].astype(BF16)

    return pl.pallas_call(
        body,
        out_shape=[jax.ShapeDtypeStruct((blocks, part, block), BF16)] * nc,
        grid_spec=pltpu.PrefetchScalarGridSpec(
            num_scalar_prefetch=1,
            grid=(blocks,),
            in_specs=[pl.BlockSpec((left.shape[0], block), lambda i, ix: (0, ix[i]))]
            + [pl.BlockSpec(v.shape, lambda i, ix: (0, 0)) for v in rights],
            out_specs=[pl.BlockSpec((1, part, block), lambda i, ix: (i, 0, 0))] * nc,
            scratch_shapes=[pltpu.VMEM((width, block), F32)],
        ),
        compiler_params=params(),
        cost_estimate=cost(),
        name="out_weight_grads",
    )(order, left, *rights)


def joined_rows(parts):
    return parts[0] if len(parts) == 1 else jnp.concatenate(parts, 0)


def rope_tables(positions):
    steps_half = jnp.arange(HD // 2, dtype=F32)
    inverse = jnp.exp(steps_half * (-2.0 * math.log(ROPE_BASE) / HD))
    angles = positions.astype(F32)[:, None] * inverse[None, :]
    return jnp.tile(jnp.cos(angles), (1, 4)), jnp.tile(jnp.sin(angles), (1, 4))


def make_layer(place):
    nd, nc, nf, nn_, masks = place.nd, place.nc, place.nf, place.nn, place.masks
    half = nc // 2

    def per_device(
        layer_input,
        lengths,
        attn_gain,
        w_query,
        w_key,
        w_value,
        query_gain,
        key_gain,
        w_out,
        ffn_gain,
        w_gate,
        w_up,
        w_down,
        cotangent,
    ):
        rows, slots, depth = layer_input.shape
        n = rows * slots
        block = depth // nd
        qc, kc, oc, units = w_query.shape[1], w_key.shape[1], w_out.shape[1], w_gate.shape[1]
        per = rows if slots % LANES == 0 else 1
        far, near = lax.axis_index("far"), lax.axis_index("near")
        spot = lax.axis_index("ctx")
        fars = jnp.arange(nf, dtype=jnp.int32)
        to_near = [place.block(fars, near ^ i) for i in range(nn_)]
        to_near_far = [place.block(far ^ fars, near ^ i) for i in range(nn_)]
        everywhere = jnp.arange(nd, dtype=jnp.int32)
        every = jnp.concatenate([*to_near, spot[None].astype(jnp.int32)], 0)
        positions = spot * slots + jnp.arange(slots, dtype=jnp.int32)
        cosine, sine = rope_tables(positions)
        info = jnp.concatenate([spot[None].astype(jnp.int32), lengths])
        valid = (positions[None, :] < lengths[:, None]).astype(F32).reshape(n, 1)
        qgain2 = jnp.tile(query_gain, 2)[None, :]
        kgain2 = jnp.tile(key_gain, 2)[None, :]
        gain_one, gain_two = attn_gain[None, :], ffn_gain[None, :]
        x = layer_input.reshape(n, depth)

        def gather_dp(value, tiled):
            return lax.all_gather(value, place.dp, axis=0, tiled=tiled)

        bg = (cotangent.reshape(n, depth).astype(F32) * valid).astype(BF16)
        qkv_dp = gather_dp(jnp.concatenate([w_query.T, w_key.T, w_value.T], 0), False)
        qkv_cross = place.cross(
            qkv_dp, bg, info, valid, cosine, sine, qgain2, kgain2, *to_near, every
        )
        qkv_cols = place.gather(qkv_cross)
        out_dp = gather_dp(after(w_out.T, qkv_dp), False)
        out_cross = place.cross(after(out_dp, *place.arrived(qkv_cross)))
        sizes = [768, 512] if units == 1280 else [units]
        starts = [sum(sizes[:c]) for c in range(len(sizes))]
        chunks = []
        for start, size in zip(starts, sizes):
            at = slice(start, start + size)
            local = jnp.concatenate([w_gate[:, at], w_up[:, at], w_down[:, at]], 0)
            chunks.append(gather_dp(after(local, qkv_dp), True))

        normed, lin, q, kv = project(
            info, place, x, gain_one, qkv_cols, qc, kc, qgain2, kgain2, cosine, sine,
            rows, slots,
        )
        out_cols = place.gather(out_cross, q)
        kv_cross = place.cross(kv)
        kv_all = place.gather(kv_cross)
        bg_cross = place.cross(after(bg, *place.arrived(kv_cross)))
        bg_all = place.gather(bg_cross)
        mixed_t, lse, middles, n2_cross = [], [], [], []
        before, due = place.arrived(out_cross), []
        for r in range(rows):
            m, mt, l = attend(info, after(q, *before), kv_all, masks, r, slots)
            if r == rows - 1:
                due = due + place.arrived(bg_cross)
            mid, n2 = out_project(info, place, after(m, *due), x, gain_two, out_cols, r)
            mixed_t.append(mt)
            lse.append(l)
            middles.append(mid)
            before, due = [mid], []
            if per == rows:
                n2_cross.append(place.cross(n2))
                due = place.arrived(n2_cross[-1])
            else:
                n2_cross.append(n2)
        if per != rows:
            n2_cross = [place.cross(jnp.concatenate(n2_cross, 0))]

        n2_got = [place.gather(v) for v in n2_cross]
        n2_all = [[v[i] for v in n2_got] for i in range(nc)]
        n2_flat = [v for group in n2_all for v in group]
        sums = [None] * nc
        ffn_grads, last_out = [], []

        def whole(sets, size):
            part = weight_grads(after(everywhere, *last_out), block, sets, size)
            own = lax.psum_scatter(
                part.reshape(nd * 3 * size, block), place.dp, scatter_dimension=0, tiled=True
            )
            ffn_grads.append(own.reshape(3, size, block))
            return part

        def send(sets, size):
            got = None
            for i in range(1, nn_):
                mine = weight_grads(after(to_near[i], *last_out), block, sets, size)
                part = swap(mine, "near", nn_, i)
                got = part if got is None else got + part
            return mine, (sets, size, got)

        def keep(entry):
            sets, size, got = entry
            part = weight_grads(after(to_near[0], *last_out), block, sets, size, got)
            own = lax.psum_scatter(
                part.reshape(nf * 3 * size, block), "far", scatter_dimension=0, tiled=True
            )
            ffn_grads.append(own.reshape(3, size, block))
            return part

        def scatter_core_of(k, which, *hold):
            return place.scatter_core({masks[i]: after(sums[i][k], *hold) for i in which})[0]

        near_side, far_side = range(half), range(half, nc)
        normed_cross = place.cross(after(normed, *place.arrived(n2_cross[-1])))
        waiting = []
        for c, weights in enumerate(chunks):
            acts, ends = None, c == len(chunks) - 1
            for at in (slice(half, nc), slice(0, half)) if ends else (slice(0, nc),):
                sums[at], acts = feed_forward(
                    after(info, *last_out), place, weights, n2_all[at], bg_all[at],
                    None if c == 0 else sums[at], acts, nc * n, at.start, ends,
                )
                last_out = [acts[0]]
                if ends and at.start:
                    grads = scatter_core_of(1, far_side)
                    grads_got = place.send_outer(grads)
                    last_out = [acts[0], *grads.values()]
            h, gg, ug = [[a] for a in acts]
            sets = [(n2_flat, [gg, ug]), (bg_all, [h])]
            if nn_ == 1:
                last_out = [whole(sets, sizes[c])]
            else:
                mine, entry = send(sets, sizes[c])
                waiting.append(entry)
                last_out = [mine]
            if not ends:
                last_out = last_out + place.arrived(normed_cross)
        normed_got = place.gather(normed_cross, *last_out)
        grad_parts = [scatter_core_of(1, near_side, *last_out, *grads_got)[0], *grads_got]

        middle_grad, attn_grad, mixed_grad, gf = middle_back(
            after(info, *last_out), place, grad_parts, middles, bg, gain_two, out_cols, rows, slots
        )
        branches = scatter_core_of(0, far_side, mixed_grad)
        branches |= scatter_core_of(0, near_side, mixed_grad)
        w_out_all = out_weight_grads(after(every, mixed_grad), place, block, attn_grad, mixed_t)
        w_out_core, _ = place.scatter_core(dict(zip(masks, w_out_all)))
        dqs, cores = [], []
        outer = place.combos[1:]
        last_out = [w_out_all[0], *[w_out_core[m] for m in outer]]
        for r in range(rows):
            dq, *dkv = attend_back(
                after(info, *last_out), q, kv_all, mixed_grad, lse[r], masks, r, slots
            )
            dqs.append(dq)
            last_out = [dq]
            if r == 0:
                w_out_got = place.send_outer({m: after(b, dq) for m, b in w_out_core.items()})
                if len(waiting) > 1:
                    last_out = [keep(waiting.pop(0))]
                last_out = last_out + normed_got[1:] + list(branches.values())
            cores.append(place.scatter_core(dict(zip(masks, dkv)), F32))
        dkvs = [[core[0], *place.send_outer(core)] for core, _ in cores]
        last_out = last_out + [core[m] for core, _ in cores for m in outer]

        dlins, dlin_got, gq, gk = [], [], [], []
        for r in range(rows):
            own, gq_r, gk_r, *dlin = heads_back(
                after(info, *last_out), place, dqs[r], dkvs[r], lin, qc, kc, qgain2, kgain2, cosine, sine,
                r, slots,
            )
            dlins.append(own)
            dlin_got.append(place.exchange(dlin))
            last_out = [own]
            if r == rows - 1:
                last_out = last_out + w_out_got
            if waiting and r == rows - 1:
                last_out = [keep(waiting.pop(0))]
            gq.append(gq_r[0])
            gk.append(gk_r[0])
        input_grad, ga = project_back(
            after(info, *last_out, *ffn_grads[:1]), place, dlins, x, middle_grad, gain_one, qkv_cols, rows, slots
        )
        halves = combine([w_out_core[0], *[after(g, dlins[0]) for g in w_out_got]], BF16, nn_)
        halves = [halves[0]] + [
            swap(h, "near", nn_, i) for i, h in enumerate(halves[1:], 1)
        ]

        w_out_half = combine([halves[0], *[after(h, input_grad) for h in halves[1:]]], BF16)[0]
        w_out_grad = lax.psum_scatter(
            w_out_half.reshape(nf * oc, block), "far", scatter_dimension=0, tiled=True
        )

        def summed(parts):
            total = parts[0].astype(F32)
            for p in parts[1:]:
                total = total + p.astype(F32)
            return total[0]

        gains, gains_got = place.total(jnp.concatenate([ga[0], gf[0], sum(gq), sum(gk)]))
        right = [dlin_got[r][i] for i in range(nc) for r in range(rows)]
        if per != rows:
            right = [jnp.concatenate(right, 1)]
        got = None
        for i in reversed(range(nn_)):
            part = weight_grads(
                after(to_near_far[i], input_grad, *ffn_grads[:1]), block, [(normed_got, [right])], qc + 2 * kc,
                got if i == 0 else None, i == 0,
            )
            if i:
                branch_got = place.send_outer({m: after(b, part, *gains_got) for m, b in branches.items()})
                part = swap(part, "near", nn_, i)
                got = part if got is None else got + part
        if nn_ == 1:
            branch_got = place.send_outer(branches)
        out_rows = finish_rows(middles, [branches[0], *branch_got], valid)
        gains = place.total_dp(gains, part[0])
        gq = gains[2 * depth : 2 * depth + LANES]
        gk = gains[2 * depth + LANES : 2 * depth + 2 * LANES]
        far_got = [swap(part[m], "far", nf, m) for m in range(1, nf)]
        w_qkv_grad = summed([part[0]] + [after(g, out_rows) for g in far_got])

        grads = None
        for own, start in zip(ffn_grads, starts):
            grads = finish_grads(own, start, units, grads)
        return (
            out_rows.reshape(rows, slots, depth),
            input_grad.reshape(rows, slots, depth),
            gains[:depth],
            w_qkv_grad[:qc].T,
            w_qkv_grad[qc : qc + kc].T,
            w_qkv_grad[qc + kc :].T,
            gq[:HD] + gq[HD:],
            gk[:HD] + gk[HD:],
            w_out_grad.astype(F32).T,
            gains[depth : 2 * depth],
            grads[0],
            grads[1],
            grads[2],
        )

    return per_device


def solution(mesh):
    place = Place(mesh)
    wide = P(place.dp, "ctx")
    rows = P(place.dp, "ctx", None)
    in_specs = (
        rows, P(place.dp), P(), wide, wide, wide, P(), P(), wide, P(), wide, wide, wide, rows,
    )
    out_specs = (
        rows, rows, P(), wide, wide, wide, P(), P(), wide, P(), wide, wide, wide,
    )
    return jax.shard_map(
        make_layer(place),
        mesh=place.mesh,
        in_specs=in_specs,
        out_specs=out_specs,
        check_vma=False,
    )
```

```python
import math

import jax
import jax.numpy as jnp
import numpy as np
from jax import lax
from jax.experimental import pallas as pl
from jax.experimental.pallas import tpu as pltpu
from jax.sharding import Mesh, PartitionSpec as P

HQ = 20
KVH = 5
HD = 64
GROUP = HQ // KVH
QW = HQ * HD
KVW = KVH * HD
GW = GROUP * HD
LANES = 2 * HD
NEG = -1e30
EPSILON = 1e-06
ROPE_BASE = 10000.0
F32 = jnp.float32
BF16 = jnp.bfloat16
VMEM_LIMIT = 60 << 20


def nn(a, b):
    return lax.dot_general(a, b, (((1,), (0,)), ((), ())), preferred_element_type=F32)


def nt(a, b):
    return lax.dot_general(a, b, (((1,), (1,)), ((), ())), preferred_element_type=F32)


def tn(a, b):
    return lax.dot_general(a, b, (((0,), (0,)), ((), ())), preferred_element_type=F32)


def cost(**_):
    return pl.CostEstimate(flops=1, bytes_accessed=1, transcendentals=0)


def params(limit=VMEM_LIMIT):
    return pltpu.CompilerParams(vmem_limit_bytes=limit)


def after(value, *others):
    return lax.optimization_barrier((value, *others))[0] if others else value


def swap(value, axis, size, mask):
    return lax.ppermute(value, axis, [(i, i ^ mask) for i in range(size)])


class Place:
    def __init__(self, mesh):
        grid = mesh.devices
        self.nd, self.nc = mesh.shape["dp"], mesh.shape["ctx"]
        first = tuple(grid[0, 0].coords)
        bits = [1 << i for i in range(self.nd.bit_length() - 1)]
        far = [b for b in bits if tuple(grid[b, 0].coords)[2] != first[2]]
        self.nf = 1 << len(far)
        self.nn = self.nd // self.nf
        self.far_low = 1 in far
        bits = [1 << i for i in range(self.nc.bit_length() - 1)]
        self.core = [b for b in bits if tuple(grid[0, b].coords) == first]
        self.outer = [b for b in bits if b not in self.core]
        shape = (self.nn, self.nf) if self.far_low else (self.nf, self.nn)
        self.dp = ("near", "far") if self.far_low else ("far", "near")
        self.mesh = Mesh(grid.reshape(*shape, self.nc), (*self.dp, "ctx"))
        combos = [0]
        for bit in self.outer:
            combos = combos + [c | bit for c in combos]
        self.combos = combos
        masks = list(combos)
        for bit in self.core:
            masks = [m for pair in masks for m in (pair, pair | bit)]
        self.masks = masks

    def block(self, far, near):
        return near * self.nf + far if self.far_low else far * self.nn + near

    def cross(self, own, *first):
        held = {m: swap(own, "ctx", self.nc, m) if m else own for m in self.combos}
        for bit in self.core:
            held[bit] = swap(after(own, *first), "ctx", self.nc, bit)
        return held

    def gather(self, held, *hold):
        if not isinstance(held, dict):
            held = self.cross(held)
        held = dict(held)
        for bit in self.core:
            for m in self.combos[1:]:
                held[m | bit] = swap(after(held[m], *hold), "ctx", self.nc, bit)
        return [held[m] for m in self.masks]

    def arrived(self, held):
        return [v for m, v in held.items() if m]

    def exchange(self, blocks):
        return [blocks[0]] + [
            swap(b, "ctx", self.nc, m) for b, m in zip(blocks[1:], self.masks[1:])
        ]

    def scatter_core(self, blocks, kind=BF16):
        came = []
        for bit in self.core:
            kept = {}
            for m in blocks:
                if not m & bit:
                    got = swap(blocks[m | bit].astype(BF16), "ctx", self.nc, bit)
                    came.append(got)
                    kept[m] = combine([blocks[m], got], BF16 if m else kind)[0]
            blocks = kept
        return blocks, came

    def total(self, value):
        got = [swap(value, "ctx", self.nc, m) for m in range(1, self.nc)]
        return sum(got, value), got

    def total_dp(self, value, *hold):
        value = sum([swap(value, "far", self.nf, m) for m in range(1, self.nf)], value)
        value = after(value, *hold)
        return sum([swap(value, "near", self.nn, m) for m in range(1, self.nn)], value)

    def send_outer(self, blocks):
        return [swap(b, "ctx", self.nc, m) for m, b in blocks.items() if m]


def gather_all(place, own):
    nc, nn_, nf = place.nc, place.nn, place.nf
    outer, bits, masks = place.combos[1:], place.core, place.masks
    count = nc * nn_ * nf

    def body(own_ref, *refs):
        out_refs, (send_sem, recv_sem, own_sem) = refs[:nc], refs[nc:]
        here = {a: lax.axis_index(a) for a in ("far", "near", "ctx")}
        barrier = pltpu.get_barrier_semaphore()
        partners = [("far", m) for m in range(1, nf)] + [("near", m) for m in range(1, nn_)]
        partners += [("ctx", m) for m in (*outer, *bits)]
        for axis, m in partners:
            pl.semaphore_signal(
                barrier, inc=1, device_id={axis: here[axis] ^ m}, device_id_type=pl.DeviceIdType.MESH
            )
        pl.semaphore_wait(barrier, len(partners))
        kept = pltpu.make_async_copy(own_ref, out_refs[0].at[0, 0], own_sem)
        kept.start()

        def place_of(k, i, f):
            return out_refs[masks.index(k)].at[i, f]

        sent = {}

        def send(source, key, axis, m):
            n = (masks.index(key[0]) * nn_ + key[1]) * nf + key[2]
            sent[key] = pltpu.make_async_remote_copy(
                src_ref=source,
                dst_ref=place_of(*key),
                send_sem=send_sem.at[n],
                recv_sem=recv_sem.at[n],
                device_id={axis: here[axis] ^ m},
                device_id_type=pl.DeviceIdType.MESH,
            )
            sent[key].start()

        def to_group(source, i, f):
            for m in (*outer, *bits):
                send(source, (m, i, f), "ctx", m)

        for f in range(1, nf):
            send(own_ref, (0, 0, f), "far", f)
        for i in range(1, nn_):
            send(own_ref, (0, i, 0), "near", i)
        to_group(own_ref, 0, 0)
        for f in range(nf):
            if f:
                sent[0, 0, f].wait_recv()
                for i in range(1, nn_):
                    send(place_of(0, 0, f), (0, i, f), "near", i)
                to_group(place_of(0, 0, f), 0, f)
            for i in range(1, nn_):
                sent[0, i, f].wait_recv()
                to_group(place_of(0, i, f), i, f)
        for f in range(nf):
            for i in range(nn_):
                for m in outer:
                    sent[m, i, f].wait_recv()
                    for bit in bits:
                        send(place_of(m, i, f), (m | bit, i, f), "ctx", bit)
        for (k, i, f), copy in sent.items():
            if any(k & bit for bit in bits):
                copy.wait_recv()
            copy.wait_send()
        kept.wait()

    columns, block = own.shape
    return list(
        pl.pallas_call(
            body,
            out_shape=[jax.ShapeDtypeStruct((nn_, nf, columns, block), BF16)] * nc,
            in_specs=[pl.BlockSpec(memory_space=pltpu.VMEM)],
            out_specs=[pl.BlockSpec(memory_space=pl.ANY)] * nc,
            scratch_shapes=[
                pltpu.SemaphoreType.DMA((count,)),
                pltpu.SemaphoreType.DMA((count,)),
                pltpu.SemaphoreType.DMA,
            ],
            compiler_params=pltpu.CompilerParams(
                vmem_limit_bytes=VMEM_LIMIT, collective_id=0, has_side_effects=True
            ),
            cost_estimate=cost(),
            name="gather_all",
        )(own)
    )


def combine(parts, kind, pieces=1):
    shape = parts[0].shape
    tile = 256 if pieces == 1 and shape[0] % 256 == 0 else shape[0]
    block = (tile, *shape[1:])
    out = (shape[0] // pieces, *shape[1:])
    step = tile // pieces

    def body(*refs):
        part_refs, out_refs = refs[: len(parts)], refs[len(parts) :]
        for i, o in enumerate(out_refs):
            at = slice(i * step, (i + 1) * step)
            value = part_refs[0][at].astype(F32)
            for r in part_refs[1:]:
                value = value + r[at].astype(F32)
            o[...] = value.astype(kind)

    index = lambda i: (i,) + (0,) * (len(shape) - 1)
    return pl.pallas_call(
        body,
        out_shape=[jax.ShapeDtypeStruct(out, kind)] * pieces,
        grid=(shape[0] // tile,),
        in_specs=[pl.BlockSpec(block, index)] * len(parts),
        out_specs=[pl.BlockSpec((step, *shape[1:]), index)] * pieces,
        compiler_params=params(),
        cost_estimate=cost(),
        name="combine",
    )(*parts)


def finish_rows(middles, parts, valid):
    rows, (slots, depth) = len(middles), middles[0].shape

    def body(valid_ref, *refs):
        mid_refs, part_refs, out_ref = refs[:rows], refs[rows:-1], refs[-1]
        step = pl.program_id(0)
        y = mid_refs[0][...]
        for r in range(1, rows):
            y = jnp.where(step >= r, mid_refs[r][...], y)
        for p in part_refs:
            y = y + p[...].astype(F32)
        out_ref[...] = (y * valid_ref[...]).astype(BF16)

    whole = lambda i: (0, 0)
    by_row = lambda i: (i, 0)
    return pl.pallas_call(
        body,
        out_shape=jax.ShapeDtypeStruct((rows * slots, depth), BF16),
        grid=(rows,),
        in_specs=[pl.BlockSpec((slots, 1), by_row)]
        + [pl.BlockSpec((slots, depth), whole)] * rows
        + [pl.BlockSpec((slots, depth), by_row)] * len(parts),
        out_specs=pl.BlockSpec((slots, depth), by_row),
        compiler_params=params(),
        cost_estimate=cost(),
        name="finish_rows",
    )(valid, *middles, *parts)


def finish_grads(own, start, width, previous):
    many, units, block = own.shape
    tile = 256 if units % 256 == 0 else units

    def body(own_ref, *refs):
        for k in range(many):
            refs[-many + k][...] = own_ref[k].astype(F32).T

    extra = [] if previous is None else list(previous)
    return pl.pallas_call(
        body,
        out_shape=[jax.ShapeDtypeStruct((block, width), F32)] * many,
        grid=(units // tile,),
        in_specs=[pl.BlockSpec((many, tile, block), lambda i: (0, i, 0))]
        + [pl.BlockSpec(memory_space=pl.ANY)] * len(extra),
        out_specs=[pl.BlockSpec((block, tile), lambda i: (0, start // tile + i))] * many,
        input_output_aliases={1 + k: k for k in range(len(extra))},
        compiler_params=params(),
        cost_estimate=cost(),
        name="finish_grads",
    )(own, *extra)


def head_stats(x, low):
    return lax.rsqrt(head_mean(x * x, low) + EPSILON)


def head_mean(x, low):
    first = jnp.sum(jnp.where(low, x, 0.0), -1, keepdims=True)
    second = jnp.sum(jnp.where(low, 0.0, x), -1, keepdims=True)
    return jnp.where(low, first, second) * (1.0 / HD)


def lane_masks(rows):
    lane = lax.broadcasted_iota(jnp.int32, (rows, LANES), 1)
    return lane < HD, lax.rem(lane, HD) < HD // 2


def spans(start, stop, width):
    out = []
    while start < stop:
        j = start // width
        end = min(stop, (j + 1) * width)
        out.append((j, start - j * width, end - j * width))
        start = end
    return out


def joined(parts):
    return parts[0] if len(parts) == 1 else jnp.concatenate(parts, 1)


def slot_copies(info_ref, place, w_refs, slots_ref, sem):
    copies = []
    flat = len(w_refs[0].shape) == 3
    far, near = info_ref.shape[0] - 2, info_ref.shape[0] - 1
    for k, m in enumerate(place.masks):
        block = w_refs[k].shape[-1]
        for i in range(place.nn):
            for f in range(place.nf):
                if flat:
                    source, at = w_refs[k].at[place.block(f, i)], place.block(f, i)
                else:
                    source, at = w_refs[k].at[i, f], place.block(info_ref[far] ^ f, info_ref[near] ^ i)
                start = at * block if flat else pl.multiple_of(at * block, block)
                copies.append(
                    pltpu.make_async_copy(
                        source,
                        slots_ref.at[info_ref[0] ^ m, :, pl.ds(start, block)],
                        sem.at[len(copies)],
                    )
                )
    return copies


def load_slots(*args):
    copies = slot_copies(*args)
    for c in copies:
        c.start()
    for c in copies:
        c.wait()


def project(info, place, x, gain, w_cols, qc, kc, qgain, kgain, cosine, sine, rows, slots):
    nc, depth, wc = place.nc, x.shape[1], w_cols[0].shape[-2]
    n = rows * slots

    def body(info_ref, x_ref, gain_ref, qgain_ref, kgain_ref, cos_ref, sin_ref, *refs):
        w_refs, (normed_ref, lin_ref, q_ref, kv_ref, w_ref, sem) = refs[:nc], refs[nc:]

        @pl.when(pl.program_id(0) == 0)
        def _():
            load_slots(info_ref, place, w_refs, w_ref, sem)

        xf = x_ref[...].astype(F32)
        inv = lax.rsqrt(jnp.mean(xf * xf, -1, keepdims=True) + EPSILON)
        normed_ref[...] = (xf * inv * gain_ref[...]).astype(BF16)
        for j in range(nc):
            lin_ref[j] = nt(normed_ref[...], w_ref[j])
        low, front = lane_masks(slots)
        cos, sin = cos_ref[...], sin_ref[...]

        def columns(base, width, start, stop):
            return [lin_ref[j, :, base + a : base + b] for j, a, b in spans(start, stop, width)]

        def turn(v, gain):
            v = v * head_stats(v, low) * gain
            turned = jnp.where(
                front, -pltpu.roll(v, LANES - HD // 2, 1), pltpu.roll(v, HD // 2, 1)
            )
            return v * cos + turned * sin

        for c in range(QW // LANES):
            at = slice(c * LANES, (c + 1) * LANES)
            y = turn(joined(columns(0, qc, at.start, at.stop)), qgain_ref[...])
            q_ref[:, at] = (y * (1.0 / math.sqrt(HD))).astype(BF16)
        for g in range(KVH):
            v = joined(
                columns(qc, kc, g * HD, (g + 1) * HD) + columns(qc + kc, kc, g * HD, (g + 1) * HD)
            )
            y = jnp.where(low, turn(v, kgain_ref[...]), v)
            kv_ref[:, g * LANES : (g + 1) * LANES] = y.astype(BF16)

    whole = lambda r, s: (0, 0)
    by_row = lambda r, s: (r, 0)
    return pl.pallas_call(
        body,
        out_shape=(
            jax.ShapeDtypeStruct((n, depth), BF16),
            jax.ShapeDtypeStruct((nc, n, wc), F32),
            jax.ShapeDtypeStruct((n, QW), BF16),
            jax.ShapeDtypeStruct((n, 2 * KVW), BF16),
        ),
        grid_spec=pltpu.PrefetchScalarGridSpec(
            num_scalar_prefetch=1,
            grid=(rows,),
            in_specs=[
                pl.BlockSpec((slots, depth), by_row),
                pl.BlockSpec((1, depth), whole),
                pl.BlockSpec((1, LANES), whole),
                pl.BlockSpec((1, LANES), whole),
                pl.BlockSpec((slots, LANES), whole),
                pl.BlockSpec((slots, LANES), whole),
            ]
            + [pl.BlockSpec(memory_space=pl.ANY)] * nc,
            out_specs=(
                pl.BlockSpec((slots, depth), by_row),
                pl.BlockSpec((nc, slots, wc), lambda r, s: (0, r, 0)),
                pl.BlockSpec((slots, QW), by_row),
                pl.BlockSpec((slots, 2 * KVW), by_row),
            ),
            scratch_shapes=[
                pltpu.VMEM((nc, wc, depth), BF16),
                pltpu.SemaphoreType.DMA((nc * place.nd,)),
            ],
        ),
        compiler_params=params(),
        cost_estimate=cost(
            flops=2 * n * depth * nc * wc, bytes_accessed=2 * nc * depth * wc, transcendentals=n
        ),
        name="project",
    )(info, x, gain, qgain, kgain, cosine, sine, *w_cols)


def heads_back(info, place, dq, dkv_parts, lin, qc, kc, qgain, kgain, cosine, sine, row, slots):
    nc, wc = place.nc, lin.shape[2]

    def body(info_ref, dq_ref, lin_ref, qgain_ref, kgain_ref, cos_ref, sin_ref, *refs):
        dkv_refs, refs = refs[: len(dkv_parts)], refs[len(dkv_parts) :]
        out_ref, gq_ref, gk_ref = refs[:3]
        dlin_refs, (dqs, dks, dvs, dlin_ref) = refs[3 : 3 + nc], refs[3 + nc :]
        low, front = lane_masks(slots)
        cos, sin = cos_ref[...], sin_ref[...]

        def columns(base, width, start, stop):
            return [lin_ref[j, :, base + a : base + b] for j, a, b in spans(start, stop, width)]

        def back(e, v, gain):
            t = e * sin
            e = e * cos + jnp.where(
                front, pltpu.roll(t, LANES - HD // 2, 1), -pltpu.roll(t, HD // 2, 1)
            )
            inv = head_stats(v, low)
            unit = v * inv
            part = e * unit
            u = e * gain
            return inv * (u - unit * head_mean(u * unit, low)), part

        gq = jnp.zeros((1, LANES), F32)
        for c in range(QW // LANES):
            at = slice(c * LANES, (c + 1) * LANES)
            v = joined(columns(0, qc, at.start, at.stop))
            y, part = back(dq_ref[:, at], v, qgain_ref[...])
            dqs[:, at] = y
            gq = gq + jnp.sum(part, 0, keepdims=True)
        gk = jnp.zeros((1, LANES), F32)
        for g in range(KVH):
            e = dkv_refs[0][:, g * LANES : (g + 1) * LANES].astype(F32)
            for ref in dkv_refs[1:]:
                e = e + ref[:, g * LANES : (g + 1) * LANES].astype(F32)
            v = joined(
                columns(qc, kc, g * HD, (g + 1) * HD) + columns(qc + kc, kc, g * HD, (g + 1) * HD)
            )
            y, part = back(e, v, kgain_ref[...])
            dks[:, g * HD : (g + 1) * HD] = y[:, :HD]
            dvs[:, g * HD : (g + 1) * HD] = e[:, HD:]
            gk = gk + jnp.sum(jnp.where(low, part, 0.0), 0, keepdims=True)
        gq_ref[...] = gq
        gk_ref[...] = gk
        for j in range(nc):
            dlin = jnp.concatenate(
                [
                    dqs[:, j * qc : (j + 1) * qc],
                    dks[:, j * kc : (j + 1) * kc],
                    dvs[:, j * kc : (j + 1) * kc],
                ],
                1,
            )
            out_ref[j] = dlin.astype(BF16)
            dlin_ref[j] = dlin.T.astype(BF16)
        for k, m in enumerate(place.masks):
            dlin_refs[k][...] = dlin_ref[info_ref[0] ^ m]

    whole = lambda i, s: (0, 0)
    cube = lambda i, s: (0, 0, 0)
    lane = pl.BlockSpec((1, LANES), whole)
    table = pl.BlockSpec((slots, LANES), whole)
    return pl.pallas_call(
        body,
        out_shape=(
            jax.ShapeDtypeStruct((nc, slots, wc), BF16),
            jax.ShapeDtypeStruct((1, LANES), F32),
            jax.ShapeDtypeStruct((1, LANES), F32),
            *([jax.ShapeDtypeStruct((wc, slots), BF16)] * nc),
        ),
        grid_spec=pltpu.PrefetchScalarGridSpec(
            num_scalar_prefetch=1,
            grid=(1,),
            in_specs=[
                pl.BlockSpec((slots, QW), whole),
                pl.BlockSpec((nc, slots, wc), lambda i, s: (0, row, 0)),
                lane,
                lane,
                table,
                table,
            ]
            + [pl.BlockSpec((slots, 2 * KVW), whole)] * len(dkv_parts),
            out_specs=(
                pl.BlockSpec((nc, slots, wc), cube),
                lane,
                lane,
                *([pl.BlockSpec((wc, slots), whole)] * nc),
            ),
            scratch_shapes=[
                pltpu.VMEM((slots, QW), F32),
                pltpu.VMEM((slots, KVW), F32),
                pltpu.VMEM((slots, KVW), F32),
                pltpu.VMEM((nc, wc, slots), BF16),
            ],
        ),
        compiler_params=params(),
        cost_estimate=cost(),
        name="heads_back",
    )(info, dq, lin, qgain, kgain, cosine, sine, *dkv_parts)


def project_back(info, place, dlins, x, middle_grad, gain, w_cols, rows, slots):
    nc, depth, wc = place.nc, x.shape[1], w_cols[0].shape[-2]

    def body(info_ref, x_ref, mid_ref, gain_ref, *refs):
        dlin_refs, refs = refs[:rows], refs[rows:]
        w_refs, (out_ref, ga_ref, w_ref, sem) = refs[:nc], refs[nc:]
        step = pl.program_id(0)

        @pl.when(step == 0)
        def _():
            load_slots(info_ref, place, w_refs, w_ref, sem)
            ga_ref[...] = jnp.zeros_like(ga_ref)

        grad = None
        for j in range(nc):
            dlin = dlin_refs[0][j]
            for r in range(1, rows):
                dlin = jnp.where(step >= r, dlin_refs[r][j], dlin)
            part = nn(dlin, w_ref[j])
            grad = part if grad is None else grad + part
        xf = x_ref[...].astype(F32)
        inv = lax.rsqrt(jnp.mean(xf * xf, -1, keepdims=True) + EPSILON)
        unit = xf * inv
        ga_ref[...] += jnp.sum(grad * unit, 0, keepdims=True)
        u = grad * gain_ref[...]
        back_x = inv * (u - unit * jnp.mean(u * unit, -1, keepdims=True))
        out_ref[...] = (mid_ref[...] + back_x).astype(BF16)

    whole = lambda i, s: (0, 0)
    by_row = lambda i, s: (i, 0)
    return pl.pallas_call(
        body,
        out_shape=(
            jax.ShapeDtypeStruct((rows * slots, depth), BF16),
            jax.ShapeDtypeStruct((1, depth), F32),
        ),
        grid_spec=pltpu.PrefetchScalarGridSpec(
            num_scalar_prefetch=1,
            grid=(rows,),
            in_specs=[
                pl.BlockSpec((slots, depth), by_row),
                pl.BlockSpec((slots, depth), by_row),
                pl.BlockSpec((1, depth), whole),
            ]
            + [pl.BlockSpec((nc, slots, wc), lambda i, s: (0, 0, 0))] * rows
            + [pl.BlockSpec(memory_space=pl.ANY)] * nc,
            out_specs=(pl.BlockSpec((slots, depth), by_row), pl.BlockSpec((1, depth), whole)),
            scratch_shapes=[
                pltpu.VMEM((nc, wc, depth), BF16),
                pltpu.SemaphoreType.DMA((nc * place.nd,)),
            ],
        ),
        compiler_params=params(),
        cost_estimate=cost(),
        name="project_back",
    )(info, x, middle_grad, gain, *dlins, *w_cols)


def fill_bias(bias_ref, info_ref, row, masks, slots):
    place, length = info_ref[0], info_ref[1 + row]
    query = place * slots + lax.broadcasted_iota(jnp.int32, (slots, slots), 1)
    for i, mask in enumerate(masks):
        key = (place ^ mask) * slots + lax.broadcasted_iota(jnp.int32, (slots, slots), 0)
        allowed = (key <= query) & (key < length)
        bias_ref[i * slots : (i + 1) * slots, :] = jnp.where(allowed, 0.0, NEG)


def attend(info, q, kv_pieces, masks, row, slots):
    count = len(masks)
    keys = count * slots

    def body(info_ref, q_ref, *refs):
        kv_refs, (o_ref, ot_ref, lse_ref, bias_ref) = refs[:count], refs[count:]
        live = info_ref[0] * slots < info_ref[1 + row]

        @pl.when(live & (pl.program_id(0) == 0))
        def _():
            fill_bias(bias_ref, info_ref, row, masks, slots)

        @pl.when(jnp.logical_not(live))
        def _():
            o_ref[...] = jnp.zeros_like(o_ref)
            ot_ref[...] = jnp.zeros_like(ot_ref)
            lse_ref[...] = jnp.zeros_like(lse_ref)

        @pl.when(live)
        def _():
            kv = jnp.concatenate([r[...] for r in kv_refs], 0)
            k, v = kv[:, :HD], kv[:, HD:]
            for h in range(GROUP):
                qh = q_ref[:, h * HD : (h + 1) * HD]
                e = jnp.exp(nt(k, qh) + bias_ref[...])
                l = jnp.sum(e, 0, keepdims=True)
                o = tn(v, (e * (1.0 / l)).astype(BF16))
                o_ref[:, h * HD : (h + 1) * HD] = o.T.astype(BF16)
                ot_ref[h * HD : (h + 1) * HD, :] = o.astype(BF16)
                lse_ref[0, h : h + 1, :] = jnp.log(l)

    n = slots
    return pl.pallas_call(
        body,
        out_shape=(
            jax.ShapeDtypeStruct((n, QW), BF16),
            jax.ShapeDtypeStruct((QW, n), BF16),
            jax.ShapeDtypeStruct((KVH, GROUP, slots), F32),
        ),
        grid_spec=pltpu.PrefetchScalarGridSpec(
            num_scalar_prefetch=1,
            grid=(KVH,),
            in_specs=[pl.BlockSpec((slots, GW), lambda g, s: (row, g))]
            + [pl.BlockSpec((slots, LANES), lambda g, s: (row, g))] * count,
            out_specs=(
                pl.BlockSpec((slots, GW), lambda g, s: (0, g)),
                pl.BlockSpec((GW, slots), lambda g, s: (g, 0)),
                pl.BlockSpec((1, GROUP, slots), lambda g, s: (g, 0, 0)),
            ),
            scratch_shapes=[pltpu.VMEM((keys, slots), F32)],
        ),
        compiler_params=params(),
        cost_estimate=cost(
            flops=16 * n * keys * QW, bytes_accessed=8 * n * QW, transcendentals=n * keys * HQ
        ),
        name="attend",
    )(info, q, *kv_pieces)


def attend_back(info, q, kv_pieces, do, lse, masks, row, slots):
    count = len(masks)
    keys = count * slots

    def body(info_ref, q_ref, do_ref, lse_ref, *refs):
        kv_refs, dq_ref = refs[:count], refs[count]
        dkv_refs, bias_ref = refs[count + 1 : -1], refs[-1]
        live = info_ref[0] * slots < info_ref[1 + row]

        @pl.when(live & (pl.program_id(0) == 0))
        def _():
            fill_bias(bias_ref, info_ref, row, masks, slots)

        @pl.when(jnp.logical_not(live))
        def _():
            dq_ref[...] = jnp.zeros_like(dq_ref)
            for r in dkv_refs:
                r[...] = jnp.zeros_like(r)

        @pl.when(live)
        def _():
            kv = jnp.concatenate([r[...] for r in kv_refs], 0)
            k, v = kv[:, :HD], kv[:, HD:]
            dk = jnp.zeros((keys, HD), F32)
            dv = jnp.zeros((keys, HD), F32)
            for h in range(GROUP):
                at = slice(h * HD, (h + 1) * HD)
                qh, doh = q_ref[:, at], do_ref[:, at]
                p = jnp.exp(nt(k, qh) + bias_ref[...] - lse_ref[0, h : h + 1, :])
                dp = nt(v, doh)
                delta = jnp.sum(p * dp, 0, keepdims=True)
                ds = (p * (dp - delta)).astype(BF16)
                dv = dv + nn(p.astype(BF16), doh)
                dk = dk + nn(ds, qh)
                dq_ref[:, at] = tn(k, ds).T * (1.0 / math.sqrt(HD))
            both = jnp.concatenate([dk, dv], 1).astype(BF16)
            for i, r in enumerate(dkv_refs):
                r[...] = both[i * slots : (i + 1) * slots, :]

    n = slots
    kv_spec = pl.BlockSpec((slots, LANES), lambda g, s: (row, g))
    q_spec = pl.BlockSpec((slots, GW), lambda g, s: (row, g))
    out_kv = pl.BlockSpec((slots, LANES), lambda g, s: (0, g))
    out_q = pl.BlockSpec((slots, GW), lambda g, s: (0, g))
    return pl.pallas_call(
        body,
        out_shape=(
            jax.ShapeDtypeStruct((n, QW), F32),
            *([jax.ShapeDtypeStruct((n, 2 * KVW), BF16)] * count),
        ),
        grid_spec=pltpu.PrefetchScalarGridSpec(
            num_scalar_prefetch=1,
            grid=(KVH,),
            in_specs=[
                q_spec,
                q_spec,
                pl.BlockSpec((1, GROUP, slots), lambda g, s: (g, 0, 0)),
            ]
            + [kv_spec] * count,
            out_specs=(out_q, *([out_kv] * count)),
            scratch_shapes=[pltpu.VMEM((keys, slots), F32)],
        ),
        compiler_params=params(),
        cost_estimate=cost(
            flops=40 * n * keys * QW, bytes_accessed=16 * n * QW, transcendentals=n * keys * HQ
        ),
        name="attend_back",
    )(info, q, do, lse, *kv_pieces)


def out_project(info, place, mixed, x, gain, w_cols, row):
    nc, depth, oc = place.nc, x.shape[1], w_cols[0].shape[-2]
    slots = mixed.shape[0]
    td = 256

    def body(info_ref, mixed_ref, x_ref, gain_ref, *refs):
        w_refs, (mid_ref, n2_ref, w_ref, sem) = refs[:nc], refs[nc:]
        load_slots(info_ref, place, w_refs, w_ref, sem)
        parts = [mixed_ref[:, j * oc : (j + 1) * oc] for j in range(nc)]
        square = jnp.zeros((slots, 1), F32)
        for d in range(depth // td):
            at = slice(d * td, (d + 1) * td)
            y = x_ref[:, at].astype(F32)
            for j in range(nc):
                y = y + nn(parts[j], w_ref[j, :, at])
            mid_ref[:, at] = y
            square = square + jnp.sum(y * y, -1, keepdims=True)
        inv = lax.rsqrt(square * (1.0 / depth) + EPSILON)
        n2_ref[...] = (mid_ref[...] * inv * gain_ref[...]).astype(BF16)

    whole = lambda i, s: (0, 0)
    return pl.pallas_call(
        body,
        out_shape=(
            jax.ShapeDtypeStruct((slots, depth), F32),
            jax.ShapeDtypeStruct((slots, depth), BF16),
        ),
        grid_spec=pltpu.PrefetchScalarGridSpec(
            num_scalar_prefetch=1,
            grid=(1,),
            in_specs=[
                pl.BlockSpec((slots, nc * oc), whole),
                pl.BlockSpec((slots, depth), lambda i, s: (row, 0)),
                pl.BlockSpec((1, depth), whole),
            ]
            + [pl.BlockSpec(memory_space=pl.ANY)] * nc,
            out_specs=(pl.BlockSpec((slots, depth), whole), pl.BlockSpec((slots, depth), whole)),
            scratch_shapes=[
                pltpu.VMEM((nc, oc, depth), BF16),
                pltpu.SemaphoreType.DMA((nc * place.nd,)),
            ],
        ),
        compiler_params=params(),
        cost_estimate=cost(
            flops=2 * slots * depth * nc * oc, bytes_accessed=4 * nc * depth * oc, transcendentals=0
        ),
        name="out_project",
    )(info, mixed, x, gain, *w_cols)


def middle_back(info, place, parts, middles, bg, gain, w_cols, rows, slots):
    nc, depth, oc, count = place.nc, bg.shape[1], w_cols[0].shape[-2], len(parts)
    n = rows * slots

    def body(info_ref, *refs):
        part_refs, refs = refs[:count], refs[count:]
        mid_refs, refs = refs[:rows], refs[rows:]
        bg_ref, gain_ref, refs = refs[0], refs[1], refs[2:]
        w_refs, (mg_ref, ag_ref, xg_ref, gf_ref, w_ref, sem) = refs[:nc], refs[nc:]
        step = pl.program_id(0)

        @pl.when(step == 0)
        def _():
            load_slots(info_ref, place, w_refs, w_ref, sem)
            gf_ref[...] = jnp.zeros_like(gf_ref)

        grad = part_refs[0][...].astype(F32)
        for p in part_refs[1:]:
            grad = grad + p[...].astype(F32)
        mid = mid_refs[0][...]
        for r in range(1, rows):
            mid = jnp.where(step >= r, mid_refs[r][...], mid)
        inv = lax.rsqrt(jnp.mean(mid * mid, -1, keepdims=True) + EPSILON)
        unit = mid * inv
        gf_ref[...] += jnp.sum(grad * unit, 0, keepdims=True)
        u = grad * gain_ref[...]
        y = bg_ref[...].astype(F32) + inv * (u - unit * jnp.mean(u * unit, -1, keepdims=True))
        mg_ref[...] = y
        ag_ref[...] = y.astype(BF16)
        xg_ref[...] = jnp.concatenate(
            [nt(ag_ref[...], w_ref[j]) for j in range(nc)], 1
        ).astype(BF16)

    whole = lambda i, s: (0, 0)
    by_row = lambda i, s: (i, 0)
    token = pl.BlockSpec((slots, depth), by_row)
    return pl.pallas_call(
        body,
        out_shape=(
            jax.ShapeDtypeStruct((n, depth), F32),
            jax.ShapeDtypeStruct((n, depth), BF16),
            jax.ShapeDtypeStruct((n, nc * oc), BF16),
            jax.ShapeDtypeStruct((1, depth), F32),
        ),
        grid_spec=pltpu.PrefetchScalarGridSpec(
            num_scalar_prefetch=1,
            grid=(rows,),
            in_specs=[token] * count
            + [pl.BlockSpec((slots, depth), whole)] * rows
            + [token, pl.BlockSpec((1, depth), whole)]
            + [pl.BlockSpec(memory_space=pl.ANY)] * nc,
            out_specs=(
                token,
                token,
                pl.BlockSpec((slots, nc * oc), by_row),
                pl.BlockSpec((1, depth), whole),
            ),
            scratch_shapes=[
                pltpu.VMEM((nc, oc, depth), BF16),
                pltpu.SemaphoreType.DMA((nc * place.nd,)),
            ],
        ),
        compiler_params=params(),
        cost_estimate=cost(
            flops=2 * n * depth * nc * oc, bytes_accessed=20 * n * depth, transcendentals=0
        ),
        name="middle_back",
    )(info, *parts, *middles, bg, gain, *w_cols)


def feed_forward(info, place, weights, n2, bg, sums, acts, total, first, last):
    owners, (tokens, depth), units = len(n2), bg[0].shape, weights.shape[1]
    cuts = len(n2[0])
    part = tokens // cuts
    block = depth // place.nd
    tu = 256 if units % 256 == 0 else units
    td = 256
    sum_type = BF16 if last else F32
    has_sums, has_acts = sums is not None, acts is not None

    def body(info_ref, w_ref, *refs):
        n2_refs, refs = refs[: owners * cuts], refs[owners * cuts :]
        bg_refs, refs = refs[:owners], refs[owners:]
        sum_refs = ()
        if has_sums:
            sum_refs, refs = refs[: 2 * owners], refs[2 * owners :]
        if has_acts:
            refs = refs[3:]
        out_refs, refs = refs[: 2 * owners], refs[2 * owners :]
        ht_ref, ggt_ref, ugt_ref, wg, wu, wd, acts_buf, tok_buf, out_buf = refs[:9]
        w_sem, tok_sem, out_sem = refs[9:12]
        in_buf, in_sem = refs[12:] if has_sums else (None, None)
        step = pl.program_id(0)
        slot = lax.rem(step, 2)

        def token_copies(p, to):
            found = [
                pltpu.make_async_copy(
                    n2_refs[p * cuts + i],
                    tok_buf.at[to, 0, i * part : (i + 1) * part, :],
                    tok_sem.at[to, i],
                )
                for i in range(cuts)
            ]
            return found + [
                pltpu.make_async_copy(bg_refs[p], tok_buf.at[to, 1], tok_sem.at[to, cuts])
            ]

        def sum_copies(p):
            return [
                pltpu.make_async_copy(sum_refs[2 * p + k], in_buf.at[k], in_sem.at[k])
                for k in range(2)
            ]

        def out_copies(p):
            return [
                pltpu.make_async_copy(out_buf.at[k], out_refs[2 * p + k], out_sem.at[k])
                for k in range(2)
            ]

        @pl.when(step == 0)
        def _():
            for c in token_copies(0, 0):
                c.start()
            copies = []
            for i in range(place.nd):
                for j, dst in enumerate((wg, wu, wd)):
                    start = (3 * i + j) * block
                    copies.append(
                        pltpu.make_async_copy(
                            w_ref.at[start : start + block, :],
                            dst.at[i * block : (i + 1) * block, :],
                            w_sem.at[len(copies)],
                        )
                    )
            for c in copies:
                c.start()
            for c in copies:
                c.wait()

        for p in range(owners):

            @pl.when(step == p)
            def _():
                if p + 1 < owners:
                    for c in token_copies(p + 1, (p + 1) % 2):
                        c.start()
                if has_sums:
                    for c in sum_copies(p):
                        c.start()

        for c in token_copies(0, slot):
            c.wait()
        x, b = tok_buf[slot, 0], tok_buf[slot, 1]
        for j in range(units // tu):
            at = slice(j * tu, (j + 1) * tu)
            gate, up = nn(x, wg[:, at]), nn(x, wu[:, at])
            dh = nn(b, wd[:, at])
            sig = 1.0 / (1.0 + jnp.exp(-gate))
            act = gate * sig
            h = act * up
            gg = dh * up * sig * (1.0 + gate * (1.0 - sig))
            ug = dh * act
            for k, (value, ref) in enumerate(((h, ht_ref), (gg, ggt_ref), (ug, ugt_ref))):
                acts_buf[k, :, at] = value.astype(BF16)
                ref[at, :] = value.T.astype(BF16)

        @pl.when(step > 0)
        def _():
            for c in out_copies(0):
                c.wait()

        if has_sums:
            for c in sum_copies(0):
                c.wait()
        h, gg, ug = acts_buf[0], acts_buf[1], acts_buf[2]
        for j in range(depth // td):
            at = slice(j * td, (j + 1) * td)
            values = [nt(h, wd[at, :]), nt(gg, wg[at, :]) + nt(ug, wu[at, :])]
            for k in range(2):
                value = values[k]
                if has_sums:
                    value = value + in_buf[k, :, at]
                out_buf[k, :, at] = value.astype(sum_type)
        for p in range(owners):

            @pl.when(step == p)
            def _():
                for c in out_copies(p):
                    c.start()

        @pl.when(step == owners - 1)
        def _():
            for c in out_copies(0):
                c.wait()

    any_spec = pl.BlockSpec(memory_space=pl.ANY)
    act_spec = pl.BlockSpec((units, tokens), lambda i, s: (0, i + first))
    operands = [weights, *[v for group in n2 for v in group], *bg]
    aliases = {}
    if has_sums:
        operands += [v for pair in sums for v in pair]
    if has_acts:
        for j in range(3):
            aliases[1 + len(operands) + j] = 2 * owners + j
        operands += acts
    n = owners * tokens
    scratch = [pltpu.VMEM((depth, units), BF16)] * 3 + [
        pltpu.VMEM((3, tokens, units), BF16),
        pltpu.VMEM((2, 2, tokens, depth), BF16),
        pltpu.VMEM((2, tokens, depth), sum_type),
        pltpu.SemaphoreType.DMA((3 * place.nd,)),
        pltpu.SemaphoreType.DMA((2, cuts + 1)),
        pltpu.SemaphoreType.DMA((2,)),
    ]
    if has_sums:
        scratch += [pltpu.VMEM((2, tokens, depth), F32), pltpu.SemaphoreType.DMA((2,))]
    out = pl.pallas_call(
        body,
        out_shape=(
            *([jax.ShapeDtypeStruct((tokens, depth), sum_type)] * (2 * owners)),
            *([jax.ShapeDtypeStruct((units, total), BF16)] * 3),
        ),
        grid_spec=pltpu.PrefetchScalarGridSpec(
            num_scalar_prefetch=1,
            grid=(owners,),
            in_specs=[any_spec] * len(operands),
            out_specs=(*([any_spec] * (2 * owners)), act_spec, act_spec, act_spec),
            scratch_shapes=scratch,
        ),
        input_output_aliases=aliases,
        compiler_params=params(),
        cost_estimate=cost(
            flops=12 * n * depth * units, bytes_accessed=16 * n * depth, transcendentals=n * units
        ),
        name="feed_forward",
    )(info, *operands)
    return [list(out[2 * o : 2 * o + 2]) for o in range(owners)], list(out[2 * owners :])


def weight_grads(order, block, sets, width, added=None, apart=False):
    lefts = [v for left, _ in sets for v in left]
    rights = [v for _, right in sets for group in right for v in group]
    many, blocks = sum(len(right) for _, right in sets), order.shape[0]

    def body(order_ref, *refs):
        left_refs, refs = refs[: len(lefts)], refs[len(lefts) :]
        right_refs, refs = refs[: len(rights)], refs[len(rights) :]
        extra_ref, out_refs = (None, refs) if added is None else (refs[0], refs[1:])
        i = k = at = 0
        for left, right in sets:
            tall = joined_rows([r[...] for r in left_refs[i : i + len(left)]])
            i += len(left)
            wides = []
            for group in right:
                wides.append(joined([r[...] for r in right_refs[at : at + len(group)]]))
                at += len(group)
            values = nn(joined_rows(wides), tall)
            for m in range(len(right)):
                value = values[m * width : (m + 1) * width]
                if added is not None:
                    value = value + extra_ref[0, k].astype(F32)
                if apart:
                    for f in range(blocks):

                        @pl.when(pl.program_id(0) == f)
                        def _():
                            out_refs[f][k] = value.astype(BF16)
                else:
                    out_refs[0][0, k] = value.astype(BF16)
                k += 1

    part = pl.BlockSpec((1, many, width, block), lambda i, ix: (i, 0, 0, 0))
    extra = [] if added is None else [added]
    if apart:
        shapes = [jax.ShapeDtypeStruct((many, width, block), BF16)] * blocks
        specs = [pl.BlockSpec((many, width, block), lambda i, ix: (0, 0, 0))] * blocks
    else:
        shapes = jax.ShapeDtypeStruct((blocks, many, width, block), BF16)
        specs = part
    return pl.pallas_call(
        body,
        out_shape=shapes,
        grid_spec=pltpu.PrefetchScalarGridSpec(
            num_scalar_prefetch=1,
            grid=(blocks,),
            in_specs=[pl.BlockSpec((v.shape[0], block), lambda i, ix: (0, ix[i])) for v in lefts]
            + [pl.BlockSpec((width, v.shape[1]), lambda i, ix: (0, 0)) for v in rights]
            + [part] * len(extra),
            out_specs=specs,
        ),
        compiler_params=params(),
        cost_estimate=cost(),
        name="weight_grads",
    )(order, *lefts, *rights, *extra)


def out_weight_grads(order, place, block, left, rights):
    nc, blocks = place.nc, order.shape[0] - 1
    width = rights[0].shape[0]
    part = width // nc

    def body(order_ref, left_ref, *refs):
        right_refs, refs = refs[: len(rights)], refs[len(rights) :]
        out_refs, value_ref = refs[:nc], refs[nc]
        value_ref[...] = nn(joined([r[...] for r in right_refs]), left_ref[...])
        for k, m in enumerate(place.masks):
            start = pl.multiple_of((order_ref[blocks] ^ m) * part, part & -part)
            out_refs[k][0] = value_ref[pl.ds(start, part), :].astype(BF16)

    return pl.pallas_call(
        body,
        out_shape=[jax.ShapeDtypeStruct((blocks, part, block), BF16)] * nc,
        grid_spec=pltpu.PrefetchScalarGridSpec(
            num_scalar_prefetch=1,
            grid=(blocks,),
            in_specs=[pl.BlockSpec((left.shape[0], block), lambda i, ix: (0, ix[i]))]
            + [pl.BlockSpec(v.shape, lambda i, ix: (0, 0)) for v in rights],
            out_specs=[pl.BlockSpec((1, part, block), lambda i, ix: (i, 0, 0))] * nc,
            scratch_shapes=[pltpu.VMEM((width, block), F32)],
        ),
        compiler_params=params(),
        cost_estimate=cost(),
        name="out_weight_grads",
    )(order, left, *rights)


def joined_rows(parts):
    return parts[0] if len(parts) == 1 else jnp.concatenate(parts, 0)


def rope_tables(positions):
    steps_half = jnp.arange(HD // 2, dtype=F32)
    inverse = jnp.exp(steps_half * (-2.0 * math.log(ROPE_BASE) / HD))
    angles = positions.astype(F32)[:, None] * inverse[None, :]
    return jnp.tile(jnp.cos(angles), (1, 4)), jnp.tile(jnp.sin(angles), (1, 4))


def make_layer(place):
    nd, nc, nf, nn_, masks = place.nd, place.nc, place.nf, place.nn, place.masks
    half = nc // 2

    def per_device(
        layer_input,
        lengths,
        attn_gain,
        w_query,
        w_key,
        w_value,
        query_gain,
        key_gain,
        w_out,
        ffn_gain,
        w_gate,
        w_up,
        w_down,
        cotangent,
    ):
        rows, slots, depth = layer_input.shape
        n = rows * slots
        block = depth // nd
        qc, kc, oc, units = w_query.shape[1], w_key.shape[1], w_out.shape[1], w_gate.shape[1]
        per = rows if slots % LANES == 0 else 1
        far, near = lax.axis_index("far"), lax.axis_index("near")
        spot = lax.axis_index("ctx")
        fars = jnp.arange(nf, dtype=jnp.int32)
        to_near = [place.block(fars, near ^ i) for i in range(nn_)]
        to_near_far = [place.block(far ^ fars, near ^ i) for i in range(nn_)]
        everywhere = jnp.arange(nd, dtype=jnp.int32)
        every = jnp.concatenate([*to_near, spot[None].astype(jnp.int32)], 0)
        positions = spot * slots + jnp.arange(slots, dtype=jnp.int32)
        cosine, sine = rope_tables(positions)
        info = jnp.concatenate(
            [spot[None].astype(jnp.int32), lengths, jnp.stack([far, near]).astype(jnp.int32)]
        )
        valid = (positions[None, :] < lengths[:, None]).astype(F32).reshape(n, 1)
        qgain2 = jnp.tile(query_gain, 2)[None, :]
        kgain2 = jnp.tile(key_gain, 2)[None, :]
        gain_one, gain_two = attn_gain[None, :], ffn_gain[None, :]
        x = layer_input.reshape(n, depth)

        def gather_dp(value, tiled):
            return lax.all_gather(value, place.dp, axis=0, tiled=tiled)

        bg = (cotangent.reshape(n, depth).astype(F32) * valid).astype(BF16)
        qkv_cols = gather_all(place, jnp.concatenate([w_query.T, w_key.T, w_value.T], 0))
        out_dp = gather_dp(w_out.T, False)
        out_cross = place.cross(after(out_dp, qkv_cols[1]))
        sizes = [768, 512] if units == 1280 else [units]
        starts = [sum(sizes[:c]) for c in range(len(sizes))]
        chunks = []
        for start, size in zip(starts, sizes):
            at = slice(start, start + size)
            local = jnp.concatenate([w_gate[:, at], w_up[:, at], w_down[:, at]], 0)
            chunks.append(gather_dp(after(local, qkv_cols[1]), True))

        normed, lin, q, kv = project(
            info, place, x, gain_one, qkv_cols, qc, kc, qgain2, kgain2, cosine, sine,
            rows, slots,
        )
        out_cols = place.gather(out_cross, q)
        kv_cross = place.cross(kv)
        kv_all = place.gather(kv_cross)
        bg_cross = place.cross(after(bg, *place.arrived(kv_cross)))
        bg_all = place.gather(bg_cross)
        mixed_t, lse, middles, n2_cross = [], [], [], []
        before, due = place.arrived(out_cross), []
        for r in range(rows):
            m, mt, l = attend(info, after(q, *before), kv_all, masks, r, slots)
            if r == rows - 1:
                due = due + place.arrived(bg_cross)
            mid, n2 = out_project(info, place, after(m, *due), x, gain_two, out_cols, r)
            mixed_t.append(mt)
            lse.append(l)
            middles.append(mid)
            before, due = [mid], []
            if per == rows:
                n2_cross.append(place.cross(n2))
                due = place.arrived(n2_cross[-1])
            else:
                n2_cross.append(n2)
        if per != rows:
            n2_cross = [place.cross(jnp.concatenate(n2_cross, 0))]

        n2_got = [place.gather(v) for v in n2_cross]
        n2_all = [[v[i] for v in n2_got] for i in range(nc)]
        n2_flat = [v for group in n2_all for v in group]
        sums = [None] * nc
        ffn_grads, last_out = [], []

        def whole(sets, size):
            part = weight_grads(after(everywhere, *last_out), block, sets, size)
            own = lax.psum_scatter(
                part.reshape(nd * 3 * size, block), place.dp, scatter_dimension=0, tiled=True
            )
            ffn_grads.append(own.reshape(3, size, block))
            return part

        def send(sets, size):
            got = None
            for i in range(1, nn_):
                mine = weight_grads(after(to_near[i], *last_out), block, sets, size)
                part = swap(mine, "near", nn_, i)
                got = part if got is None else got + part
            return mine, (sets, size, got)

        def keep(entry):
            sets, size, got = entry
            part = weight_grads(after(to_near[0], *last_out), block, sets, size, got)
            own = lax.psum_scatter(
                part.reshape(nf * 3 * size, block), "far", scatter_dimension=0, tiled=True
            )
            ffn_grads.append(own.reshape(3, size, block))
            return part

        def scatter_core_of(k, which, *hold):
            return place.scatter_core({masks[i]: after(sums[i][k], *hold) for i in which})[0]

        near_side, far_side = range(half), range(half, nc)
        normed_cross = place.cross(after(normed, *place.arrived(n2_cross[-1])))
        waiting = []
        for c, weights in enumerate(chunks):
            acts, ends = None, c == len(chunks) - 1
            for at in (slice(half, nc), slice(0, half)) if ends else (slice(0, nc),):
                sums[at], acts = feed_forward(
                    after(info, *last_out), place, weights, n2_all[at], bg_all[at],
                    None if c == 0 else sums[at], acts, nc * n, at.start, ends,
                )
                last_out = [acts[0]]
                if ends and at.start:
                    grads = scatter_core_of(1, far_side)
                    grads_got = place.send_outer(grads)
                    last_out = [acts[0], *grads.values()]
            h, gg, ug = [[a] for a in acts]
            sets = [(n2_flat, [gg, ug]), (bg_all, [h])]
            if nn_ == 1:
                last_out = [whole(sets, sizes[c])]
            else:
                mine, entry = send(sets, sizes[c])
                waiting.append(entry)
                last_out = [mine]
            if not ends:
                last_out = last_out + place.arrived(normed_cross)
        normed_got = place.gather(normed_cross, *last_out)
        grad_parts = [scatter_core_of(1, near_side, *last_out, *grads_got)[0], *grads_got]

        middle_grad, attn_grad, mixed_grad, gf = middle_back(
            after(info, *last_out), place, grad_parts, middles, bg, gain_two, out_cols, rows, slots
        )
        branches = scatter_core_of(0, far_side, mixed_grad)
        branches |= scatter_core_of(0, near_side, mixed_grad)
        w_out_all = out_weight_grads(after(every, mixed_grad), place, block, attn_grad, mixed_t)
        w_out_core, _ = place.scatter_core(dict(zip(masks, w_out_all)))
        dqs, cores = [], []
        outer = place.combos[1:]
        last_out = [w_out_all[0], *[w_out_core[m] for m in outer]]
        for r in range(rows):
            dq, *dkv = attend_back(
                after(info, *last_out), q, kv_all, mixed_grad, lse[r], masks, r, slots
            )
            dqs.append(dq)
            last_out = [dq]
            if r == 0:
                w_out_got = place.send_outer({m: after(b, dq) for m, b in w_out_core.items()})
                if len(waiting) > 1:
                    last_out = [keep(waiting.pop(0))]
                last_out = last_out + normed_got[1:] + list(branches.values())
            cores.append(place.scatter_core(dict(zip(masks, dkv)), F32))
        dkvs = [[core[0], *place.send_outer(core)] for core, _ in cores]
        last_out = last_out + [core[m] for core, _ in cores for m in outer]

        dlins, dlin_got, gq, gk = [], [], [], []
        for r in range(rows):
            own, gq_r, gk_r, *dlin = heads_back(
                after(info, *last_out), place, dqs[r], dkvs[r], lin, qc, kc, qgain2, kgain2, cosine, sine,
                r, slots,
            )
            dlins.append(own)
            dlin_got.append(place.exchange(dlin))
            last_out = [own]
            if r == rows - 1:
                last_out = last_out + w_out_got
            if waiting and r == rows - 1:
                last_out = [keep(waiting.pop(0))]
            gq.append(gq_r[0])
            gk.append(gk_r[0])
        input_grad, ga = project_back(
            after(info, *last_out, *ffn_grads[:1]), place, dlins, x, middle_grad, gain_one, qkv_cols, rows, slots
        )
        halves = combine([w_out_core[0], *[after(g, dlins[0]) for g in w_out_got]], BF16, nn_)
        halves = [halves[0]] + [
            swap(h, "near", nn_, i) for i, h in enumerate(halves[1:], 1)
        ]

        w_out_half = combine([halves[0], *[after(h, input_grad) for h in halves[1:]]], BF16)[0]
        w_out_grad = lax.psum_scatter(
            w_out_half.reshape(nf * oc, block), "far", scatter_dimension=0, tiled=True
        )

        def summed(parts):
            total = parts[0].astype(F32)
            for p in parts[1:]:
                total = total + p.astype(F32)
            return total[0]

        gains, gains_got = place.total(jnp.concatenate([ga[0], gf[0], sum(gq), sum(gk)]))
        right = [dlin_got[r][i] for i in range(nc) for r in range(rows)]
        if per != rows:
            right = [jnp.concatenate(right, 1)]
        got = None
        for i in reversed(range(nn_)):
            part = weight_grads(
                after(to_near_far[i], input_grad, *ffn_grads[:1]), block, [(normed_got, [right])], qc + 2 * kc,
                got if i == 0 else None, i == 0,
            )
            if i:
                branch_got = place.send_outer({m: after(b, part, *gains_got) for m, b in branches.items()})
                part = swap(part, "near", nn_, i)
                got = part if got is None else got + part
        if nn_ == 1:
            branch_got = place.send_outer(branches)
        out_rows = finish_rows(middles, [branches[0], *branch_got], valid)
        gains = place.total_dp(gains, part[0])
        gq = gains[2 * depth : 2 * depth + LANES]
        gk = gains[2 * depth + LANES : 2 * depth + 2 * LANES]
        far_got = [swap(part[m], "far", nf, m) for m in range(1, nf)]
        w_qkv_grad = summed([part[0]] + [after(g, out_rows) for g in far_got])

        grads = None
        for own, start in zip(ffn_grads, starts):
            grads = finish_grads(own, start, units, grads)
        return (
            out_rows.reshape(rows, slots, depth),
            input_grad.reshape(rows, slots, depth),
            gains[:depth],
            w_qkv_grad[:qc].T,
            w_qkv_grad[qc : qc + kc].T,
            w_qkv_grad[qc + kc :].T,
            gq[:HD] + gq[HD:],
            gk[:HD] + gk[HD:],
            w_out_grad.astype(F32).T,
            gains[depth : 2 * depth],
            grads[0],
            grads[1],
            grads[2],
        )

    return per_device


def solution(mesh):
    place = Place(mesh)
    wide = P(place.dp, "ctx")
    rows = P(place.dp, "ctx", None)
    in_specs = (
        rows, P(place.dp), P(), wide, wide, wide, P(), P(), wide, P(), wide, wide, wide, rows,
    )
    out_specs = (
        rows, rows, P(), wide, wide, wide, P(), P(), wide, P(), wide, wide, wide,
    )
    return jax.shard_map(
        make_layer(place),
        mesh=place.mesh,
        in_specs=in_specs,
        out_specs=out_specs,
        check_vma=False,
    )
```

```python
import math

import jax
import jax.numpy as jnp
import numpy as np
from jax import lax
from jax.experimental import pallas as pl
from jax.experimental.pallas import tpu as pltpu
from jax.sharding import Mesh, PartitionSpec as P

HQ = 20
KVH = 5
HD = 64
GROUP = HQ // KVH
QW = HQ * HD
KVW = KVH * HD
GW = GROUP * HD
LANES = 2 * HD
NEG = -1e30
EPSILON = 1e-06
ROPE_BASE = 10000.0
F32 = jnp.float32
BF16 = jnp.bfloat16
VMEM_LIMIT = 60 << 20


def nn(a, b):
    return lax.dot_general(a, b, (((1,), (0,)), ((), ())), preferred_element_type=F32)


def nt(a, b):
    return lax.dot_general(a, b, (((1,), (1,)), ((), ())), preferred_element_type=F32)


def tn(a, b):
    return lax.dot_general(a, b, (((0,), (0,)), ((), ())), preferred_element_type=F32)


def cost(**_):
    return pl.CostEstimate(flops=1, bytes_accessed=1, transcendentals=0)


def params(limit=VMEM_LIMIT):
    return pltpu.CompilerParams(vmem_limit_bytes=limit)


def after(value, *others):
    return lax.optimization_barrier((value, *others))[0] if others else value


def swap(value, axis, size, mask):
    return lax.ppermute(value, axis, [(i, i ^ mask) for i in range(size)])


class Place:
    def __init__(self, mesh):
        grid = mesh.devices
        self.nd, self.nc = mesh.shape["dp"], mesh.shape["ctx"]
        first = tuple(grid[0, 0].coords)
        bits = [1 << i for i in range(self.nd.bit_length() - 1)]
        far = [b for b in bits if tuple(grid[b, 0].coords)[2] != first[2]]
        self.nf = 1 << len(far)
        self.nn = self.nd // self.nf
        self.far_low = 1 in far
        bits = [1 << i for i in range(self.nc.bit_length() - 1)]
        self.core = [b for b in bits if tuple(grid[0, b].coords) == first]
        self.outer = [b for b in bits if b not in self.core]
        shape = (self.nn, self.nf) if self.far_low else (self.nf, self.nn)
        self.dp = ("near", "far") if self.far_low else ("far", "near")
        self.mesh = Mesh(grid.reshape(*shape, self.nc), (*self.dp, "ctx"))
        combos = [0]
        for bit in self.outer:
            combos = combos + [c | bit for c in combos]
        self.combos = combos
        masks = list(combos)
        for bit in self.core:
            masks = [m for pair in masks for m in (pair, pair | bit)]
        self.masks = masks

    def block(self, far, near):
        return near * self.nf + far if self.far_low else far * self.nn + near

    def cross(self, own, *first):
        held = {m: swap(own, "ctx", self.nc, m) if m else own for m in self.combos}
        for bit in self.core:
            held[bit] = swap(after(own, *first), "ctx", self.nc, bit)
        return held

    def gather(self, held, *hold):
        if not isinstance(held, dict):
            held = self.cross(held)
        held = dict(held)
        for bit in self.core:
            for m in self.combos[1:]:
                held[m | bit] = swap(after(held[m], *hold), "ctx", self.nc, bit)
        return [held[m] for m in self.masks]

    def arrived(self, held):
        return [v for m, v in held.items() if m]

    def exchange(self, blocks):
        return [blocks[0]] + [
            swap(b, "ctx", self.nc, m) for b, m in zip(blocks[1:], self.masks[1:])
        ]

    def scatter_core(self, blocks, kind=BF16):
        came = []
        for bit in self.core:
            kept = {}
            for m in blocks:
                if not m & bit:
                    got = swap(blocks[m | bit].astype(BF16), "ctx", self.nc, bit)
                    came.append(got)
                    kept[m] = combine([blocks[m], got], BF16 if m else kind)[0]
            blocks = kept
        return blocks, came

    def total(self, value):
        got = [swap(value, "ctx", self.nc, m) for m in range(1, self.nc)]
        return sum(got, value), got

    def total_dp(self, value, *hold):
        value = sum([swap(value, "far", self.nf, m) for m in range(1, self.nf)], value)
        value = after(value, *hold)
        return sum([swap(value, "near", self.nn, m) for m in range(1, self.nn)], value)

    def send_outer(self, blocks):
        return [swap(b, "ctx", self.nc, m) for m, b in blocks.items() if m]


def gather_all(place, own):
    nc, nn_, nf = place.nc, place.nn, place.nf
    outer, bits, masks = place.combos[1:], place.core, place.masks
    count = nc * nn_ * nf

    def body(own_ref, *refs):
        out_refs, (send_sem, recv_sem, own_sem) = refs[:nc], refs[nc:]
        here = {a: lax.axis_index(a) for a in ("far", "near", "ctx")}
        barrier = pltpu.get_barrier_semaphore()
        partners = [("far", m) for m in range(1, nf)] + [("near", m) for m in range(1, nn_)]
        partners += [("ctx", m) for m in (*outer, *bits)]
        for axis, m in partners:
            pl.semaphore_signal(
                barrier, inc=1, device_id={axis: here[axis] ^ m}, device_id_type=pl.DeviceIdType.MESH
            )
        pl.semaphore_wait(barrier, len(partners))
        kept = pltpu.make_async_copy(own_ref, out_refs[0].at[0, 0], own_sem)
        kept.start()

        def place_of(k, i, f):
            return out_refs[masks.index(k)].at[i, f]

        sent = {}

        def send(source, key, axis, m):
            n = (masks.index(key[0]) * nn_ + key[1]) * nf + key[2]
            sent[key] = pltpu.make_async_remote_copy(
                src_ref=source,
                dst_ref=place_of(*key),
                send_sem=send_sem.at[n],
                recv_sem=recv_sem.at[n],
                device_id={axis: here[axis] ^ m},
                device_id_type=pl.DeviceIdType.MESH,
            )
            sent[key].start()

        def to_group(source, i, f):
            for m in (*outer, *bits):
                send(source, (m, i, f), "ctx", m)

        for f in range(1, nf):
            send(own_ref, (0, 0, f), "far", f)
        for i in range(1, nn_):
            send(own_ref, (0, i, 0), "near", i)
        to_group(own_ref, 0, 0)
        for f in range(nf):
            if f:
                sent[0, 0, f].wait_recv()
                for i in range(1, nn_):
                    send(place_of(0, 0, f), (0, i, f), "near", i)
                to_group(place_of(0, 0, f), 0, f)
            for i in range(1, nn_):
                sent[0, i, f].wait_recv()
                to_group(place_of(0, i, f), i, f)
        for f in range(nf):
            for i in range(nn_):
                for m in outer:
                    sent[m, i, f].wait_recv()
                    for bit in bits:
                        send(place_of(m, i, f), (m | bit, i, f), "ctx", bit)
        for (k, i, f), copy in sent.items():
            if any(k & bit for bit in bits):
                copy.wait_recv()
            copy.wait_send()
        kept.wait()

    columns, block = own.shape
    return list(
        pl.pallas_call(
            body,
            out_shape=[jax.ShapeDtypeStruct((nn_, nf, columns, block), BF16)] * nc,
            in_specs=[pl.BlockSpec(memory_space=pltpu.VMEM)],
            out_specs=[pl.BlockSpec(memory_space=pl.ANY)] * nc,
            scratch_shapes=[
                pltpu.SemaphoreType.DMA((count,)),
                pltpu.SemaphoreType.DMA((count,)),
                pltpu.SemaphoreType.DMA,
            ],
            compiler_params=pltpu.CompilerParams(
                vmem_limit_bytes=VMEM_LIMIT, collective_id=0, has_side_effects=True
            ),
            cost_estimate=cost(),
            name="gather_all",
        )(own)
    )


def combine(parts, kind, pieces=1):
    shape = parts[0].shape
    tile = 256 if pieces == 1 and shape[0] % 256 == 0 else shape[0]
    block = (tile, *shape[1:])
    out = (shape[0] // pieces, *shape[1:])
    step = tile // pieces

    def body(*refs):
        part_refs, out_refs = refs[: len(parts)], refs[len(parts) :]
        for i, o in enumerate(out_refs):
            at = slice(i * step, (i + 1) * step)
            value = part_refs[0][at].astype(F32)
            for r in part_refs[1:]:
                value = value + r[at].astype(F32)
            o[...] = value.astype(kind)

    index = lambda i: (i,) + (0,) * (len(shape) - 1)
    return pl.pallas_call(
        body,
        out_shape=[jax.ShapeDtypeStruct(out, kind)] * pieces,
        grid=(shape[0] // tile,),
        in_specs=[pl.BlockSpec(block, index)] * len(parts),
        out_specs=[pl.BlockSpec((step, *shape[1:]), index)] * pieces,
        compiler_params=params(),
        cost_estimate=cost(),
        name="combine",
    )(*parts)


def finish_rows(middles, parts, valid):
    rows, (slots, depth) = len(middles), middles[0].shape

    def body(valid_ref, *refs):
        mid_refs, part_refs, out_ref = refs[:rows], refs[rows:-1], refs[-1]
        step = pl.program_id(0)
        y = mid_refs[0][...]
        for r in range(1, rows):
            y = jnp.where(step >= r, mid_refs[r][...], y)
        for p in part_refs:
            y = y + p[...].astype(F32)
        out_ref[...] = (y * valid_ref[...]).astype(BF16)

    whole = lambda i: (0, 0)
    by_row = lambda i: (i, 0)
    return pl.pallas_call(
        body,
        out_shape=jax.ShapeDtypeStruct((rows * slots, depth), BF16),
        grid=(rows,),
        in_specs=[pl.BlockSpec((slots, 1), by_row)]
        + [pl.BlockSpec((slots, depth), whole)] * rows
        + [pl.BlockSpec((slots, depth), by_row)] * len(parts),
        out_specs=pl.BlockSpec((slots, depth), by_row),
        compiler_params=params(),
        cost_estimate=cost(),
        name="finish_rows",
    )(valid, *middles, *parts)


def finish_grads(own, start, width, previous):
    many, units, block = own.shape
    tile = 256 if units % 256 == 0 else units

    def body(own_ref, *refs):
        for k in range(many):
            refs[-many + k][...] = own_ref[k].astype(F32).T

    extra = [] if previous is None else list(previous)
    return pl.pallas_call(
        body,
        out_shape=[jax.ShapeDtypeStruct((block, width), F32)] * many,
        grid=(units // tile,),
        in_specs=[pl.BlockSpec((many, tile, block), lambda i: (0, i, 0))]
        + [pl.BlockSpec(memory_space=pl.ANY)] * len(extra),
        out_specs=[pl.BlockSpec((block, tile), lambda i: (0, start // tile + i))] * many,
        input_output_aliases={1 + k: k for k in range(len(extra))},
        compiler_params=params(),
        cost_estimate=cost(),
        name="finish_grads",
    )(own, *extra)


def head_stats(x, low):
    return lax.rsqrt(head_mean(x * x, low) + EPSILON)


def head_mean(x, low):
    first = jnp.sum(jnp.where(low, x, 0.0), -1, keepdims=True)
    second = jnp.sum(jnp.where(low, 0.0, x), -1, keepdims=True)
    return jnp.where(low, first, second) * (1.0 / HD)


def lane_masks(rows):
    lane = lax.broadcasted_iota(jnp.int32, (rows, LANES), 1)
    return lane < HD, lax.rem(lane, HD) < HD // 2


def spans(start, stop, width):
    out = []
    while start < stop:
        j = start // width
        end = min(stop, (j + 1) * width)
        out.append((j, start - j * width, end - j * width))
        start = end
    return out


def joined(parts):
    return parts[0] if len(parts) == 1 else jnp.concatenate(parts, 1)


def slot_copies(info_ref, place, w_refs, slots_ref, sem):
    copies = []
    flat = len(w_refs[0].shape) == 3
    far, near = info_ref.shape[0] - 2, info_ref.shape[0] - 1
    for k, m in enumerate(place.masks):
        block = w_refs[k].shape[-1]
        for i in range(place.nn):
            for f in range(place.nf):
                if flat:
                    source, at = w_refs[k].at[place.block(f, i)], place.block(f, i)
                else:
                    source, at = w_refs[k].at[i, f], place.block(info_ref[far] ^ f, info_ref[near] ^ i)
                start = at * block if flat else pl.multiple_of(at * block, block)
                copies.append(
                    pltpu.make_async_copy(
                        source,
                        slots_ref.at[info_ref[0] ^ m, :, pl.ds(start, block)],
                        sem.at[len(copies)],
                    )
                )
    return copies


def load_slots(*args):
    copies = slot_copies(*args)
    for c in copies:
        c.start()
    for c in copies:
        c.wait()


def project(info, place, x, gain, w_cols, qc, kc, qgain, kgain, cosine, sine, rows, slots):
    nc, depth, wc = place.nc, x.shape[1], w_cols[0].shape[-2]
    n = rows * slots

    def body(info_ref, x_ref, gain_ref, qgain_ref, kgain_ref, cos_ref, sin_ref, *refs):
        w_refs, (normed_ref, lin_ref, q_ref, kv_ref, w_ref, sem) = refs[:nc], refs[nc:]

        @pl.when(pl.program_id(0) == 0)
        def _():
            load_slots(info_ref, place, w_refs, w_ref, sem)

        xf = x_ref[...].astype(F32)
        inv = lax.rsqrt(jnp.mean(xf * xf, -1, keepdims=True) + EPSILON)
        normed_ref[...] = (xf * inv * gain_ref[...]).astype(BF16)
        for j in range(nc):
            lin_ref[j] = nt(normed_ref[...], w_ref[j])
        low, front = lane_masks(slots)
        cos, sin = cos_ref[...], sin_ref[...]

        def columns(base, width, start, stop):
            return [lin_ref[j, :, base + a : base + b] for j, a, b in spans(start, stop, width)]

        def turn(v, gain):
            v = v * head_stats(v, low) * gain
            turned = jnp.where(
                front, -pltpu.roll(v, LANES - HD // 2, 1), pltpu.roll(v, HD // 2, 1)
            )
            return v * cos + turned * sin

        for c in range(QW // LANES):
            at = slice(c * LANES, (c + 1) * LANES)
            y = turn(joined(columns(0, qc, at.start, at.stop)), qgain_ref[...])
            q_ref[:, at] = (y * (1.0 / math.sqrt(HD))).astype(BF16)
        for g in range(KVH):
            v = joined(
                columns(qc, kc, g * HD, (g + 1) * HD) + columns(qc + kc, kc, g * HD, (g + 1) * HD)
            )
            y = jnp.where(low, turn(v, kgain_ref[...]), v)
            kv_ref[:, g * LANES : (g + 1) * LANES] = y.astype(BF16)

    whole = lambda r, s: (0, 0)
    by_row = lambda r, s: (r, 0)
    return pl.pallas_call(
        body,
        out_shape=(
            jax.ShapeDtypeStruct((n, depth), BF16),
            jax.ShapeDtypeStruct((nc, n, wc), F32),
            jax.ShapeDtypeStruct((n, QW), BF16),
            jax.ShapeDtypeStruct((n, 2 * KVW), BF16),
        ),
        grid_spec=pltpu.PrefetchScalarGridSpec(
            num_scalar_prefetch=1,
            grid=(rows,),
            in_specs=[
                pl.BlockSpec((slots, depth), by_row),
                pl.BlockSpec((1, depth), whole),
                pl.BlockSpec((1, LANES), whole),
                pl.BlockSpec((1, LANES), whole),
                pl.BlockSpec((slots, LANES), whole),
                pl.BlockSpec((slots, LANES), whole),
            ]
            + [pl.BlockSpec(memory_space=pl.ANY)] * nc,
            out_specs=(
                pl.BlockSpec((slots, depth), by_row),
                pl.BlockSpec((nc, slots, wc), lambda r, s: (0, r, 0)),
                pl.BlockSpec((slots, QW), by_row),
                pl.BlockSpec((slots, 2 * KVW), by_row),
            ),
            scratch_shapes=[
                pltpu.VMEM((nc, wc, depth), BF16),
                pltpu.SemaphoreType.DMA((nc * place.nd,)),
            ],
        ),
        compiler_params=params(),
        cost_estimate=cost(
            flops=2 * n * depth * nc * wc, bytes_accessed=2 * nc * depth * wc, transcendentals=n
        ),
        name="project",
    )(info, x, gain, qgain, kgain, cosine, sine, *w_cols)


def heads_back(info, place, dq, dkv_parts, lin, qc, kc, qgain, kgain, cosine, sine, row, slots):
    nc, wc = place.nc, lin.shape[2]

    def body(info_ref, dq_ref, lin_ref, qgain_ref, kgain_ref, cos_ref, sin_ref, *refs):
        dkv_refs, refs = refs[: len(dkv_parts)], refs[len(dkv_parts) :]
        out_ref, gq_ref, gk_ref = refs[:3]
        dlin_refs, (dqs, dks, dvs, dlin_ref) = refs[3 : 3 + nc], refs[3 + nc :]
        low, front = lane_masks(slots)
        cos, sin = cos_ref[...], sin_ref[...]

        def columns(base, width, start, stop):
            return [lin_ref[j, :, base + a : base + b] for j, a, b in spans(start, stop, width)]

        def back(e, v, gain):
            t = e * sin
            e = e * cos + jnp.where(
                front, pltpu.roll(t, LANES - HD // 2, 1), -pltpu.roll(t, HD // 2, 1)
            )
            inv = head_stats(v, low)
            unit = v * inv
            part = e * unit
            u = e * gain
            return inv * (u - unit * head_mean(u * unit, low)), part

        gq = jnp.zeros((1, LANES), F32)
        for c in range(QW // LANES):
            at = slice(c * LANES, (c + 1) * LANES)
            v = joined(columns(0, qc, at.start, at.stop))
            y, part = back(dq_ref[:, at], v, qgain_ref[...])
            dqs[:, at] = y
            gq = gq + jnp.sum(part, 0, keepdims=True)
        gk = jnp.zeros((1, LANES), F32)
        for g in range(KVH):
            e = dkv_refs[0][:, g * LANES : (g + 1) * LANES].astype(F32)
            for ref in dkv_refs[1:]:
                e = e + ref[:, g * LANES : (g + 1) * LANES].astype(F32)
            v = joined(
                columns(qc, kc, g * HD, (g + 1) * HD) + columns(qc + kc, kc, g * HD, (g + 1) * HD)
            )
            y, part = back(e, v, kgain_ref[...])
            dks[:, g * HD : (g + 1) * HD] = y[:, :HD]
            dvs[:, g * HD : (g + 1) * HD] = e[:, HD:]
            gk = gk + jnp.sum(jnp.where(low, part, 0.0), 0, keepdims=True)
        gq_ref[...] = gq
        gk_ref[...] = gk
        for j in range(nc):
            dlin = jnp.concatenate(
                [
                    dqs[:, j * qc : (j + 1) * qc],
                    dks[:, j * kc : (j + 1) * kc],
                    dvs[:, j * kc : (j + 1) * kc],
                ],
                1,
            )
            out_ref[j] = dlin.astype(BF16)
            dlin_ref[j] = dlin.T.astype(BF16)
        for k, m in enumerate(place.masks):
            dlin_refs[k][...] = dlin_ref[info_ref[0] ^ m]

    whole = lambda i, s: (0, 0)
    cube = lambda i, s: (0, 0, 0)
    lane = pl.BlockSpec((1, LANES), whole)
    table = pl.BlockSpec((slots, LANES), whole)
    return pl.pallas_call(
        body,
        out_shape=(
            jax.ShapeDtypeStruct((nc, slots, wc), BF16),
            jax.ShapeDtypeStruct((1, LANES), F32),
            jax.ShapeDtypeStruct((1, LANES), F32),
            *([jax.ShapeDtypeStruct((wc, slots), BF16)] * nc),
        ),
        grid_spec=pltpu.PrefetchScalarGridSpec(
            num_scalar_prefetch=1,
            grid=(1,),
            in_specs=[
                pl.BlockSpec((slots, QW), whole),
                pl.BlockSpec((nc, slots, wc), lambda i, s: (0, row, 0)),
                lane,
                lane,
                table,
                table,
            ]
            + [pl.BlockSpec((slots, 2 * KVW), whole)] * len(dkv_parts),
            out_specs=(
                pl.BlockSpec((nc, slots, wc), cube),
                lane,
                lane,
                *([pl.BlockSpec((wc, slots), whole)] * nc),
            ),
            scratch_shapes=[
                pltpu.VMEM((slots, QW), F32),
                pltpu.VMEM((slots, KVW), F32),
                pltpu.VMEM((slots, KVW), F32),
                pltpu.VMEM((nc, wc, slots), BF16),
            ],
        ),
        compiler_params=params(),
        cost_estimate=cost(),
        name="heads_back",
    )(info, dq, lin, qgain, kgain, cosine, sine, *dkv_parts)


def project_back(info, place, dlins, x, middle_grad, gain, w_cols, rows, slots):
    nc, depth, wc = place.nc, x.shape[1], w_cols[0].shape[-2]

    def body(info_ref, x_ref, mid_ref, gain_ref, *refs):
        dlin_refs, refs = refs[:rows], refs[rows:]
        w_refs, (out_ref, ga_ref, w_ref, sem) = refs[:nc], refs[nc:]
        step = pl.program_id(0)

        @pl.when(step == 0)
        def _():
            load_slots(info_ref, place, w_refs, w_ref, sem)
            ga_ref[...] = jnp.zeros_like(ga_ref)

        grad = None
        for j in range(nc):
            dlin = dlin_refs[0][j]
            for r in range(1, rows):
                dlin = jnp.where(step >= r, dlin_refs[r][j], dlin)
            part = nn(dlin, w_ref[j])
            grad = part if grad is None else grad + part
        xf = x_ref[...].astype(F32)
        inv = lax.rsqrt(jnp.mean(xf * xf, -1, keepdims=True) + EPSILON)
        unit = xf * inv
        ga_ref[...] += jnp.sum(grad * unit, 0, keepdims=True)
        u = grad * gain_ref[...]
        back_x = inv * (u - unit * jnp.mean(u * unit, -1, keepdims=True))
        out_ref[...] = (mid_ref[...] + back_x).astype(BF16)

    whole = lambda i, s: (0, 0)
    by_row = lambda i, s: (i, 0)
    return pl.pallas_call(
        body,
        out_shape=(
            jax.ShapeDtypeStruct((rows * slots, depth), BF16),
            jax.ShapeDtypeStruct((1, depth), F32),
        ),
        grid_spec=pltpu.PrefetchScalarGridSpec(
            num_scalar_prefetch=1,
            grid=(rows,),
            in_specs=[
                pl.BlockSpec((slots, depth), by_row),
                pl.BlockSpec((slots, depth), by_row),
                pl.BlockSpec((1, depth), whole),
            ]
            + [pl.BlockSpec((nc, slots, wc), lambda i, s: (0, 0, 0))] * rows
            + [pl.BlockSpec(memory_space=pl.ANY)] * nc,
            out_specs=(pl.BlockSpec((slots, depth), by_row), pl.BlockSpec((1, depth), whole)),
            scratch_shapes=[
                pltpu.VMEM((nc, wc, depth), BF16),
                pltpu.SemaphoreType.DMA((nc * place.nd,)),
            ],
        ),
        compiler_params=params(),
        cost_estimate=cost(),
        name="project_back",
    )(info, x, middle_grad, gain, *dlins, *w_cols)


def fill_bias(bias_ref, info_ref, row, masks, slots):
    place, length = info_ref[0], info_ref[1 + row]
    query = place * slots + lax.broadcasted_iota(jnp.int32, (slots, slots), 1)
    for i, mask in enumerate(masks):
        key = (place ^ mask) * slots + lax.broadcasted_iota(jnp.int32, (slots, slots), 0)
        allowed = (key <= query) & (key < length)
        bias_ref[i * slots : (i + 1) * slots, :] = jnp.where(allowed, 0.0, NEG)


def attend(info, q, kv_pieces, masks, row, slots):
    count = len(masks)
    keys = count * slots

    def body(info_ref, q_ref, *refs):
        kv_refs, (o_ref, ot_ref, lse_ref, bias_ref) = refs[:count], refs[count:]
        live = info_ref[0] * slots < info_ref[1 + row]

        @pl.when(live & (pl.program_id(0) == 0))
        def _():
            fill_bias(bias_ref, info_ref, row, masks, slots)

        @pl.when(jnp.logical_not(live))
        def _():
            o_ref[...] = jnp.zeros_like(o_ref)
            ot_ref[...] = jnp.zeros_like(ot_ref)
            lse_ref[...] = jnp.zeros_like(lse_ref)

        @pl.when(live)
        def _():
            kv = jnp.concatenate([r[...] for r in kv_refs], 0)
            k, v = kv[:, :HD], kv[:, HD:]
            for h in range(GROUP):
                qh = q_ref[:, h * HD : (h + 1) * HD]
                e = jnp.exp(nt(k, qh) + bias_ref[...])
                l = jnp.sum(e, 0, keepdims=True)
                o = tn(v, e.astype(BF16)) * (1.0 / l)
                o_ref[:, h * HD : (h + 1) * HD] = o.T.astype(BF16)
                ot_ref[h * HD : (h + 1) * HD, :] = o.astype(BF16)
                lse_ref[0, h : h + 1, :] = jnp.log(l)

    n = slots
    return pl.pallas_call(
        body,
        out_shape=(
            jax.ShapeDtypeStruct((n, QW), BF16),
            jax.ShapeDtypeStruct((QW, n), BF16),
            jax.ShapeDtypeStruct((KVH, GROUP, slots), F32),
        ),
        grid_spec=pltpu.PrefetchScalarGridSpec(
            num_scalar_prefetch=1,
            grid=(KVH,),
            in_specs=[pl.BlockSpec((slots, GW), lambda g, s: (row, g))]
            + [pl.BlockSpec((slots, LANES), lambda g, s: (row, g))] * count,
            out_specs=(
                pl.BlockSpec((slots, GW), lambda g, s: (0, g)),
                pl.BlockSpec((GW, slots), lambda g, s: (g, 0)),
                pl.BlockSpec((1, GROUP, slots), lambda g, s: (g, 0, 0)),
            ),
            scratch_shapes=[pltpu.VMEM((keys, slots), F32)],
        ),
        compiler_params=params(),
        cost_estimate=cost(
            flops=16 * n * keys * QW, bytes_accessed=8 * n * QW, transcendentals=n * keys * HQ
        ),
        name="attend",
    )(info, q, *kv_pieces)


def attend_back(info, q, kv_pieces, do, lse, masks, row, slots):
    count = len(masks)
    keys = count * slots

    def body(info_ref, q_ref, do_ref, lse_ref, *refs):
        kv_refs, dq_ref = refs[:count], refs[count]
        dkv_refs, bias_ref = refs[count + 1 : -1], refs[-1]
        live = info_ref[0] * slots < info_ref[1 + row]

        @pl.when(live & (pl.program_id(0) == 0))
        def _():
            fill_bias(bias_ref, info_ref, row, masks, slots)

        @pl.when(jnp.logical_not(live))
        def _():
            dq_ref[...] = jnp.zeros_like(dq_ref)
            for r in dkv_refs:
                r[...] = jnp.zeros_like(r)

        @pl.when(live)
        def _():
            kv = jnp.concatenate([r[...] for r in kv_refs], 0)
            k, v = kv[:, :HD], kv[:, HD:]
            dk = jnp.zeros((keys, HD), F32)
            dv = jnp.zeros((keys, HD), F32)
            for h in range(GROUP):
                at = slice(h * HD, (h + 1) * HD)
                qh, doh = q_ref[:, at], do_ref[:, at]
                p = jnp.exp(nt(k, qh) + bias_ref[...] - lse_ref[0, h : h + 1, :])
                dp = nt(v, doh)
                delta = jnp.sum(p * dp, 0, keepdims=True)
                ds = (p * (dp - delta)).astype(BF16)
                dv = dv + nn(p.astype(BF16), doh)
                dk = dk + nn(ds, qh)
                dq_ref[:, at] = tn(k, ds).T * (1.0 / math.sqrt(HD))
            both = jnp.concatenate([dk, dv], 1).astype(BF16)
            for i, r in enumerate(dkv_refs):
                r[...] = both[i * slots : (i + 1) * slots, :]

    n = slots
    kv_spec = pl.BlockSpec((slots, LANES), lambda g, s: (row, g))
    q_spec = pl.BlockSpec((slots, GW), lambda g, s: (row, g))
    out_kv = pl.BlockSpec((slots, LANES), lambda g, s: (0, g))
    out_q = pl.BlockSpec((slots, GW), lambda g, s: (0, g))
    return pl.pallas_call(
        body,
        out_shape=(
            jax.ShapeDtypeStruct((n, QW), F32),
            *([jax.ShapeDtypeStruct((n, 2 * KVW), BF16)] * count),
        ),
        grid_spec=pltpu.PrefetchScalarGridSpec(
            num_scalar_prefetch=1,
            grid=(KVH,),
            in_specs=[
                q_spec,
                q_spec,
                pl.BlockSpec((1, GROUP, slots), lambda g, s: (g, 0, 0)),
            ]
            + [kv_spec] * count,
            out_specs=(out_q, *([out_kv] * count)),
            scratch_shapes=[pltpu.VMEM((keys, slots), F32)],
        ),
        compiler_params=params(),
        cost_estimate=cost(
            flops=40 * n * keys * QW, bytes_accessed=16 * n * QW, transcendentals=n * keys * HQ
        ),
        name="attend_back",
    )(info, q, do, lse, *kv_pieces)


def out_project(info, place, mixed, x, gain, w_cols, row):
    nc, depth, oc = place.nc, x.shape[1], w_cols[0].shape[-2]
    slots = mixed.shape[0]
    td = 256

    def body(info_ref, mixed_ref, x_ref, gain_ref, *refs):
        w_refs, (mid_ref, n2_ref, w_ref, sem) = refs[:nc], refs[nc:]
        load_slots(info_ref, place, w_refs, w_ref, sem)
        parts = [mixed_ref[:, j * oc : (j + 1) * oc] for j in range(nc)]
        square = jnp.zeros((slots, 1), F32)
        for d in range(depth // td):
            at = slice(d * td, (d + 1) * td)
            y = x_ref[:, at].astype(F32)
            for j in range(nc):
                y = y + nn(parts[j], w_ref[j, :, at])
            mid_ref[:, at] = y
            square = square + jnp.sum(y * y, -1, keepdims=True)
        inv = lax.rsqrt(square * (1.0 / depth) + EPSILON)
        n2_ref[...] = (mid_ref[...] * inv * gain_ref[...]).astype(BF16)

    whole = lambda i, s: (0, 0)
    return pl.pallas_call(
        body,
        out_shape=(
            jax.ShapeDtypeStruct((slots, depth), F32),
            jax.ShapeDtypeStruct((slots, depth), BF16),
        ),
        grid_spec=pltpu.PrefetchScalarGridSpec(
            num_scalar_prefetch=1,
            grid=(1,),
            in_specs=[
                pl.BlockSpec((slots, nc * oc), whole),
                pl.BlockSpec((slots, depth), lambda i, s: (row, 0)),
                pl.BlockSpec((1, depth), whole),
            ]
            + [pl.BlockSpec(memory_space=pl.ANY)] * nc,
            out_specs=(pl.BlockSpec((slots, depth), whole), pl.BlockSpec((slots, depth), whole)),
            scratch_shapes=[
                pltpu.VMEM((nc, oc, depth), BF16),
                pltpu.SemaphoreType.DMA((nc * place.nd,)),
            ],
        ),
        compiler_params=params(),
        cost_estimate=cost(
            flops=2 * slots * depth * nc * oc, bytes_accessed=4 * nc * depth * oc, transcendentals=0
        ),
        name="out_project",
    )(info, mixed, x, gain, *w_cols)


def middle_back(info, place, parts, middles, bg, gain, w_cols, rows, slots):
    nc, depth, oc, count = place.nc, bg.shape[1], w_cols[0].shape[-2], len(parts)
    n = rows * slots

    def body(info_ref, *refs):
        part_refs, refs = refs[:count], refs[count:]
        mid_refs, refs = refs[:rows], refs[rows:]
        bg_ref, gain_ref, refs = refs[0], refs[1], refs[2:]
        w_refs, (mg_ref, ag_ref, xg_ref, gf_ref, w_ref, sem) = refs[:nc], refs[nc:]
        step = pl.program_id(0)

        @pl.when(step == 0)
        def _():
            load_slots(info_ref, place, w_refs, w_ref, sem)
            gf_ref[...] = jnp.zeros_like(gf_ref)

        grad = part_refs[0][...].astype(F32)
        for p in part_refs[1:]:
            grad = grad + p[...].astype(F32)
        mid = mid_refs[0][...]
        for r in range(1, rows):
            mid = jnp.where(step >= r, mid_refs[r][...], mid)
        inv = lax.rsqrt(jnp.mean(mid * mid, -1, keepdims=True) + EPSILON)
        unit = mid * inv
        gf_ref[...] += jnp.sum(grad * unit, 0, keepdims=True)
        u = grad * gain_ref[...]
        y = bg_ref[...].astype(F32) + inv * (u - unit * jnp.mean(u * unit, -1, keepdims=True))
        mg_ref[...] = y
        ag_ref[...] = y.astype(BF16)
        xg_ref[...] = jnp.concatenate(
            [nt(ag_ref[...], w_ref[j]) for j in range(nc)], 1
        ).astype(BF16)

    whole = lambda i, s: (0, 0)
    by_row = lambda i, s: (i, 0)
    token = pl.BlockSpec((slots, depth), by_row)
    return pl.pallas_call(
        body,
        out_shape=(
            jax.ShapeDtypeStruct((n, depth), F32),
            jax.ShapeDtypeStruct((n, depth), BF16),
            jax.ShapeDtypeStruct((n, nc * oc), BF16),
            jax.ShapeDtypeStruct((1, depth), F32),
        ),
        grid_spec=pltpu.PrefetchScalarGridSpec(
            num_scalar_prefetch=1,
            grid=(rows,),
            in_specs=[token] * count
            + [pl.BlockSpec((slots, depth), whole)] * rows
            + [token, pl.BlockSpec((1, depth), whole)]
            + [pl.BlockSpec(memory_space=pl.ANY)] * nc,
            out_specs=(
                token,
                token,
                pl.BlockSpec((slots, nc * oc), by_row),
                pl.BlockSpec((1, depth), whole),
            ),
            scratch_shapes=[
                pltpu.VMEM((nc, oc, depth), BF16),
                pltpu.SemaphoreType.DMA((nc * place.nd,)),
            ],
        ),
        compiler_params=params(),
        cost_estimate=cost(
            flops=2 * n * depth * nc * oc, bytes_accessed=20 * n * depth, transcendentals=0
        ),
        name="middle_back",
    )(info, *parts, *middles, bg, gain, *w_cols)


def feed_forward(info, place, weights, n2, bg, sums, acts, total, first, last):
    owners, (tokens, depth), units = len(n2), bg[0].shape, weights.shape[1]
    cuts = len(n2[0])
    part = tokens // cuts
    block = depth // place.nd
    tu = 256 if units % 256 == 0 else units
    td = 256
    sum_type = BF16 if last else F32
    has_sums, has_acts = sums is not None, acts is not None

    def body(info_ref, w_ref, *refs):
        n2_refs, refs = refs[: owners * cuts], refs[owners * cuts :]
        bg_refs, refs = refs[:owners], refs[owners:]
        sum_refs = ()
        if has_sums:
            sum_refs, refs = refs[: 2 * owners], refs[2 * owners :]
        if has_acts:
            refs = refs[3:]
        out_refs, refs = refs[: 2 * owners], refs[2 * owners :]
        ht_ref, ggt_ref, ugt_ref, wg, wu, wd, acts_buf, tok_buf, out_buf = refs[:9]
        w_sem, tok_sem, out_sem = refs[9:12]
        in_buf, in_sem = refs[12:] if has_sums else (None, None)
        step = pl.program_id(0)
        slot = lax.rem(step, 2)

        def token_copies(p, to):
            found = [
                pltpu.make_async_copy(
                    n2_refs[p * cuts + i],
                    tok_buf.at[to, 0, i * part : (i + 1) * part, :],
                    tok_sem.at[to, i],
                )
                for i in range(cuts)
            ]
            return found + [
                pltpu.make_async_copy(bg_refs[p], tok_buf.at[to, 1], tok_sem.at[to, cuts])
            ]

        def sum_copies(p):
            return [
                pltpu.make_async_copy(sum_refs[2 * p + k], in_buf.at[k], in_sem.at[k])
                for k in range(2)
            ]

        def out_copies(p):
            return [
                pltpu.make_async_copy(out_buf.at[k], out_refs[2 * p + k], out_sem.at[k])
                for k in range(2)
            ]

        @pl.when(step == 0)
        def _():
            for c in token_copies(0, 0):
                c.start()
            copies = []
            for i in range(place.nd):
                for j, dst in enumerate((wg, wu, wd)):
                    start = (3 * i + j) * block
                    copies.append(
                        pltpu.make_async_copy(
                            w_ref.at[start : start + block, :],
                            dst.at[i * block : (i + 1) * block, :],
                            w_sem.at[len(copies)],
                        )
                    )
            for c in copies:
                c.start()
            for c in copies:
                c.wait()

        for p in range(owners):

            @pl.when(step == p)
            def _():
                if p + 1 < owners:
                    for c in token_copies(p + 1, (p + 1) % 2):
                        c.start()
                if has_sums:
                    for c in sum_copies(p):
                        c.start()

        for c in token_copies(0, slot):
            c.wait()
        x, b = tok_buf[slot, 0], tok_buf[slot, 1]
        for j in range(units // tu):
            at = slice(j * tu, (j + 1) * tu)
            gate, up = nn(x, wg[:, at]), nn(x, wu[:, at])
            dh = nn(b, wd[:, at])
            sig = 1.0 / (1.0 + jnp.exp(-gate))
            act = gate * sig
            h = act * up
            gg = dh * up * sig * (1.0 + gate * (1.0 - sig))
            ug = dh * act
            for k, (value, ref) in enumerate(((h, ht_ref), (gg, ggt_ref), (ug, ugt_ref))):
                acts_buf[k, :, at] = value.astype(BF16)
                ref[at, :] = value.T.astype(BF16)

        @pl.when(step > 0)
        def _():
            for c in out_copies(0):
                c.wait()

        if has_sums:
            for c in sum_copies(0):
                c.wait()
        h, gg, ug = acts_buf[0], acts_buf[1], acts_buf[2]
        for j in range(depth // td):
            at = slice(j * td, (j + 1) * td)
            values = [nt(h, wd[at, :]), nt(gg, wg[at, :]) + nt(ug, wu[at, :])]
            for k in range(2):
                value = values[k]
                if has_sums:
                    value = value + in_buf[k, :, at]
                out_buf[k, :, at] = value.astype(sum_type)
        for p in range(owners):

            @pl.when(step == p)
            def _():
                for c in out_copies(p):
                    c.start()

        @pl.when(step == owners - 1)
        def _():
            for c in out_copies(0):
                c.wait()

    any_spec = pl.BlockSpec(memory_space=pl.ANY)
    act_spec = pl.BlockSpec((units, tokens), lambda i, s: (0, i + first))
    operands = [weights, *[v for group in n2 for v in group], *bg]
    aliases = {}
    if has_sums:
        operands += [v for pair in sums for v in pair]
    if has_acts:
        for j in range(3):
            aliases[1 + len(operands) + j] = 2 * owners + j
        operands += acts
    n = owners * tokens
    scratch = [pltpu.VMEM((depth, units), BF16)] * 3 + [
        pltpu.VMEM((3, tokens, units), BF16),
        pltpu.VMEM((2, 2, tokens, depth), BF16),
        pltpu.VMEM((2, tokens, depth), sum_type),
        pltpu.SemaphoreType.DMA((3 * place.nd,)),
        pltpu.SemaphoreType.DMA((2, cuts + 1)),
        pltpu.SemaphoreType.DMA((2,)),
    ]
    if has_sums:
        scratch += [pltpu.VMEM((2, tokens, depth), F32), pltpu.SemaphoreType.DMA((2,))]
    out = pl.pallas_call(
        body,
        out_shape=(
            *([jax.ShapeDtypeStruct((tokens, depth), sum_type)] * (2 * owners)),
            *([jax.ShapeDtypeStruct((units, total), BF16)] * 3),
        ),
        grid_spec=pltpu.PrefetchScalarGridSpec(
            num_scalar_prefetch=1,
            grid=(owners,),
            in_specs=[any_spec] * len(operands),
            out_specs=(*([any_spec] * (2 * owners)), act_spec, act_spec, act_spec),
            scratch_shapes=scratch,
        ),
        input_output_aliases=aliases,
        compiler_params=params(),
        cost_estimate=cost(
            flops=12 * n * depth * units, bytes_accessed=16 * n * depth, transcendentals=n * units
        ),
        name="feed_forward",
    )(info, *operands)
    return [list(out[2 * o : 2 * o + 2]) for o in range(owners)], list(out[2 * owners :])


def weight_grads(order, block, sets, width, added=None, apart=False):
    lefts = [v for left, _ in sets for v in left]
    rights = [v for _, right in sets for group in right for v in group]
    many, blocks = sum(len(right) for _, right in sets), order.shape[0]

    def body(order_ref, *refs):
        left_refs, refs = refs[: len(lefts)], refs[len(lefts) :]
        right_refs, refs = refs[: len(rights)], refs[len(rights) :]
        extra_ref, out_refs = (None, refs) if added is None else (refs[0], refs[1:])
        i = k = at = 0
        for left, right in sets:
            tall = joined_rows([r[...] for r in left_refs[i : i + len(left)]])
            i += len(left)
            wides = []
            for group in right:
                wides.append(joined([r[...] for r in right_refs[at : at + len(group)]]))
                at += len(group)
            values = nn(joined_rows(wides), tall)
            for m in range(len(right)):
                value = values[m * width : (m + 1) * width]
                if added is not None:
                    value = value + extra_ref[0, k].astype(F32)
                if apart:
                    for f in range(blocks):

                        @pl.when(pl.program_id(0) == f)
                        def _():
                            out_refs[f][k] = value.astype(BF16)
                else:
                    out_refs[0][0, k] = value.astype(BF16)
                k += 1

    part = pl.BlockSpec((1, many, width, block), lambda i, ix: (i, 0, 0, 0))
    extra = [] if added is None else [added]
    if apart:
        shapes = [jax.ShapeDtypeStruct((many, width, block), BF16)] * blocks
        specs = [pl.BlockSpec((many, width, block), lambda i, ix: (0, 0, 0))] * blocks
    else:
        shapes = jax.ShapeDtypeStruct((blocks, many, width, block), BF16)
        specs = part
    return pl.pallas_call(
        body,
        out_shape=shapes,
        grid_spec=pltpu.PrefetchScalarGridSpec(
            num_scalar_prefetch=1,
            grid=(blocks,),
            in_specs=[pl.BlockSpec((v.shape[0], block), lambda i, ix: (0, ix[i])) for v in lefts]
            + [pl.BlockSpec((width, v.shape[1]), lambda i, ix: (0, 0)) for v in rights]
            + [part] * len(extra),
            out_specs=specs,
        ),
        compiler_params=params(),
        cost_estimate=cost(),
        name="weight_grads",
    )(order, *lefts, *rights, *extra)


def out_weight_grads(order, place, block, left, rights):
    nc, blocks = place.nc, order.shape[0] - 1
    width = rights[0].shape[0]
    part = width // nc

    def body(order_ref, left_ref, *refs):
        right_refs, refs = refs[: len(rights)], refs[len(rights) :]
        out_refs, value_ref = refs[:nc], refs[nc]
        value_ref[...] = nn(joined([r[...] for r in right_refs]), left_ref[...])
        for k, m in enumerate(place.masks):
            start = pl.multiple_of((order_ref[blocks] ^ m) * part, part & -part)
            out_refs[k][0] = value_ref[pl.ds(start, part), :].astype(BF16)

    return pl.pallas_call(
        body,
        out_shape=[jax.ShapeDtypeStruct((blocks, part, block), BF16)] * nc,
        grid_spec=pltpu.PrefetchScalarGridSpec(
            num_scalar_prefetch=1,
            grid=(blocks,),
            in_specs=[pl.BlockSpec((left.shape[0], block), lambda i, ix: (0, ix[i]))]
            + [pl.BlockSpec(v.shape, lambda i, ix: (0, 0)) for v in rights],
            out_specs=[pl.BlockSpec((1, part, block), lambda i, ix: (i, 0, 0))] * nc,
            scratch_shapes=[pltpu.VMEM((width, block), F32)],
        ),
        compiler_params=params(),
        cost_estimate=cost(),
        name="out_weight_grads",
    )(order, left, *rights)


def joined_rows(parts):
    return parts[0] if len(parts) == 1 else jnp.concatenate(parts, 0)


def rope_tables(positions):
    steps_half = jnp.arange(HD // 2, dtype=F32)
    inverse = jnp.exp(steps_half * (-2.0 * math.log(ROPE_BASE) / HD))
    angles = positions.astype(F32)[:, None] * inverse[None, :]
    return jnp.tile(jnp.cos(angles), (1, 4)), jnp.tile(jnp.sin(angles), (1, 4))


def make_layer(place):
    nd, nc, nf, nn_, masks = place.nd, place.nc, place.nf, place.nn, place.masks
    half = nc // 2

    def per_device(
        layer_input,
        lengths,
        attn_gain,
        w_query,
        w_key,
        w_value,
        query_gain,
        key_gain,
        w_out,
        ffn_gain,
        w_gate,
        w_up,
        w_down,
        cotangent,
    ):
        rows, slots, depth = layer_input.shape
        n = rows * slots
        block = depth // nd
        qc, kc, oc, units = w_query.shape[1], w_key.shape[1], w_out.shape[1], w_gate.shape[1]
        per = rows if slots % LANES == 0 else 1
        far, near = lax.axis_index("far"), lax.axis_index("near")
        spot = lax.axis_index("ctx")
        fars = jnp.arange(nf, dtype=jnp.int32)
        to_near = [place.block(fars, near ^ i) for i in range(nn_)]
        to_near_far = [place.block(far ^ fars, near ^ i) for i in range(nn_)]
        everywhere = jnp.arange(nd, dtype=jnp.int32)
        every = jnp.concatenate([*to_near, spot[None].astype(jnp.int32)], 0)
        positions = spot * slots + jnp.arange(slots, dtype=jnp.int32)
        cosine, sine = rope_tables(positions)
        info = jnp.concatenate(
            [spot[None].astype(jnp.int32), lengths, jnp.stack([far, near]).astype(jnp.int32)]
        )
        valid = (positions[None, :] < lengths[:, None]).astype(F32).reshape(n, 1)
        qgain2 = jnp.tile(query_gain, 2)[None, :]
        kgain2 = jnp.tile(key_gain, 2)[None, :]
        gain_one, gain_two = attn_gain[None, :], ffn_gain[None, :]
        x = layer_input.reshape(n, depth)

        def gather_dp(value, tiled):
            return lax.all_gather(value, place.dp, axis=0, tiled=tiled)

        bg = (cotangent.reshape(n, depth).astype(F32) * valid).astype(BF16)
        qkv_cols = gather_all(place, jnp.concatenate([w_query.T, w_key.T, w_value.T], 0))
        out_dp = gather_dp(w_out.T, False)
        out_cross = place.cross(after(out_dp, qkv_cols[1]))
        sizes = [768, 512] if units == 1280 else [units]
        starts = [sum(sizes[:c]) for c in range(len(sizes))]
        chunks = []
        for start, size in zip(starts, sizes):
            at = slice(start, start + size)
            local = jnp.concatenate([w_gate[:, at], w_up[:, at], w_down[:, at]], 0)
            chunks.append(gather_dp(after(local, qkv_cols[1]), True))

        normed, lin, q, kv = project(
            info, place, x, gain_one, qkv_cols, qc, kc, qgain2, kgain2, cosine, sine,
            rows, slots,
        )
        out_cols = place.gather(out_cross, q)
        kv_cross = place.cross(kv)
        kv_all = place.gather(kv_cross)
        bg_cross = place.cross(after(bg, *place.arrived(kv_cross)))
        bg_all = place.gather(bg_cross)
        mixed_t, lse, middles, n2_cross = [], [], [], []
        before, due = place.arrived(out_cross), []
        for r in range(rows):
            m, mt, l = attend(info, after(q, *before), kv_all, masks, r, slots)
            if r == rows - 1:
                due = due + place.arrived(bg_cross)
            mid, n2 = out_project(info, place, after(m, *due), x, gain_two, out_cols, r)
            mixed_t.append(mt)
            lse.append(l)
            middles.append(mid)
            before, due = [mid], []
            if per == rows:
                n2_cross.append(place.cross(n2))
                due = place.arrived(n2_cross[-1])
            else:
                n2_cross.append(n2)
        if per != rows:
            n2_cross = [place.cross(jnp.concatenate(n2_cross, 0))]

        n2_got = [place.gather(v) for v in n2_cross]
        n2_all = [[v[i] for v in n2_got] for i in range(nc)]
        n2_flat = [v for group in n2_all for v in group]
        sums = [None] * nc
        ffn_grads, last_out = [], []

        def whole(sets, size):
            part = weight_grads(after(everywhere, *last_out), block, sets, size)
            own = lax.psum_scatter(
                part.reshape(nd * 3 * size, block), place.dp, scatter_dimension=0, tiled=True
            )
            ffn_grads.append(own.reshape(3, size, block))
            return part

        def send(sets, size):
            got = None
            for i in range(1, nn_):
                mine = weight_grads(after(to_near[i], *last_out), block, sets, size)
                part = swap(mine, "near", nn_, i)
                got = part if got is None else got + part
            return mine, (sets, size, got)

        def keep(entry):
            sets, size, got = entry
            part = weight_grads(after(to_near[0], *last_out), block, sets, size, got)
            own = lax.psum_scatter(
                part.reshape(nf * 3 * size, block), "far", scatter_dimension=0, tiled=True
            )
            ffn_grads.append(own.reshape(3, size, block))
            return part

        def scatter_core_of(k, which, *hold):
            return place.scatter_core({masks[i]: after(sums[i][k], *hold) for i in which})[0]

        near_side, far_side = range(half), range(half, nc)
        normed_cross = place.cross(after(normed, *place.arrived(n2_cross[-1])))
        waiting = []
        for c, weights in enumerate(chunks):
            acts, ends = None, c == len(chunks) - 1
            for at in (slice(half, nc), slice(0, half)) if ends else (slice(0, nc),):
                sums[at], acts = feed_forward(
                    after(info, *last_out), place, weights, n2_all[at], bg_all[at],
                    None if c == 0 else sums[at], acts, nc * n, at.start, ends,
                )
                last_out = [acts[0]]
                if ends and at.start:
                    grads = scatter_core_of(1, far_side)
                    grads_got = place.send_outer(grads)
                    last_out = [acts[0], *grads.values()]
            h, gg, ug = [[a] for a in acts]
            sets = [(n2_flat, [gg, ug]), (bg_all, [h])]
            if nn_ == 1:
                last_out = [whole(sets, sizes[c])]
            else:
                mine, entry = send(sets, sizes[c])
                waiting.append(entry)
                last_out = [mine]
            if not ends:
                last_out = last_out + place.arrived(normed_cross)
        normed_got = place.gather(normed_cross, *last_out)
        grad_parts = [scatter_core_of(1, near_side, *last_out, *grads_got)[0], *grads_got]

        middle_grad, attn_grad, mixed_grad, gf = middle_back(
            after(info, *last_out), place, grad_parts, middles, bg, gain_two, out_cols, rows, slots
        )
        branches = scatter_core_of(0, far_side, mixed_grad)
        branches |= scatter_core_of(0, near_side, mixed_grad)
        w_out_all = out_weight_grads(after(every, mixed_grad), place, block, attn_grad, mixed_t)
        w_out_core, _ = place.scatter_core(dict(zip(masks, w_out_all)))
        dqs, cores = [], []
        outer = place.combos[1:]
        last_out = [w_out_all[0], *[w_out_core[m] for m in outer]]
        for r in range(rows):
            dq, *dkv = attend_back(
                after(info, *last_out), q, kv_all, mixed_grad, lse[r], masks, r, slots
            )
            dqs.append(dq)
            last_out = [dq]
            if r == 0:
                w_out_got = place.send_outer({m: after(b, dq) for m, b in w_out_core.items()})
                if len(waiting) > 1:
                    last_out = [keep(waiting.pop(0))]
                last_out = last_out + normed_got[1:] + list(branches.values())
            cores.append(place.scatter_core(dict(zip(masks, dkv)), F32))
        dkvs = [[core[0], *place.send_outer(core)] for core, _ in cores]
        last_out = last_out + [core[m] for core, _ in cores for m in outer]

        dlins, dlin_got, gq, gk = [], [], [], []
        for r in range(rows):
            own, gq_r, gk_r, *dlin = heads_back(
                after(info, *last_out), place, dqs[r], dkvs[r], lin, qc, kc, qgain2, kgain2, cosine, sine,
                r, slots,
            )
            dlins.append(own)
            dlin_got.append(place.exchange(dlin))
            last_out = [own]
            if r == rows - 1:
                last_out = last_out + w_out_got
            if waiting and r == rows - 1:
                last_out = [keep(waiting.pop(0))]
            gq.append(gq_r[0])
            gk.append(gk_r[0])
        input_grad, ga = project_back(
            after(info, *last_out, *ffn_grads[:1]), place, dlins, x, middle_grad, gain_one, qkv_cols, rows, slots
        )
        halves = combine([w_out_core[0], *[after(g, dlins[0]) for g in w_out_got]], BF16, nn_)
        halves = [halves[0]] + [
            swap(h, "near", nn_, i) for i, h in enumerate(halves[1:], 1)
        ]

        w_out_half = combine([halves[0], *[after(h, input_grad) for h in halves[1:]]], BF16)[0]
        w_out_grad = lax.psum_scatter(
            w_out_half.reshape(nf * oc, block), "far", scatter_dimension=0, tiled=True
        )

        def summed(parts):
            total = parts[0].astype(F32)
            for p in parts[1:]:
                total = total + p.astype(F32)
            return total[0]

        gains, gains_got = place.total(jnp.concatenate([ga[0], gf[0], sum(gq), sum(gk)]))
        right = [dlin_got[r][i] for i in range(nc) for r in range(rows)]
        if per != rows:
            right = [jnp.concatenate(right, 1)]
        got = None
        for i in reversed(range(nn_)):
            part = weight_grads(
                after(to_near_far[i], input_grad, *ffn_grads[:1]), block, [(normed_got, [right])], qc + 2 * kc,
                got if i == 0 else None, i == 0,
            )
            if i:
                branch_got = place.send_outer({m: after(b, part, *gains_got) for m, b in branches.items()})
                part = swap(part, "near", nn_, i)
                got = part if got is None else got + part
        if nn_ == 1:
            branch_got = place.send_outer(branches)
        out_rows = finish_rows(middles, [branches[0], *branch_got], valid)
        gains = place.total_dp(gains, part[0])
        gq = gains[2 * depth : 2 * depth + LANES]
        gk = gains[2 * depth + LANES : 2 * depth + 2 * LANES]
        far_got = [swap(part[m], "far", nf, m) for m in range(1, nf)]
        w_qkv_grad = summed([part[0]] + [after(g, out_rows) for g in far_got])

        grads = None
        for own, start in zip(ffn_grads, starts):
            grads = finish_grads(own, start, units, grads)
        return (
            out_rows.reshape(rows, slots, depth),
            input_grad.reshape(rows, slots, depth),
            gains[:depth],
            w_qkv_grad[:qc].T,
            w_qkv_grad[qc : qc + kc].T,
            w_qkv_grad[qc + kc :].T,
            gq[:HD] + gq[HD:],
            gk[:HD] + gk[HD:],
            w_out_grad.astype(F32).T,
            gains[depth : 2 * depth],
            grads[0],
            grads[1],
            grads[2],
        )

    return per_device


def solution(mesh):
    place = Place(mesh)
    wide = P(place.dp, "ctx")
    rows = P(place.dp, "ctx", None)
    in_specs = (
        rows, P(place.dp), P(), wide, wide, wide, P(), P(), wide, P(), wide, wide, wide, rows,
    )
    out_specs = (
        rows, rows, P(), wide, wide, wide, P(), P(), wide, P(), wide, wide, wide,
    )
    return jax.shard_map(
        make_layer(place),
        mesh=place.mesh,
        in_specs=in_specs,
        out_specs=out_specs,
        check_vma=False,
    )
```

```python
import math

import jax
import jax.numpy as jnp
import numpy as np
from jax import lax
from jax.experimental import pallas as pl
from jax.experimental.pallas import tpu as pltpu
from jax.sharding import Mesh, PartitionSpec as P

HQ = 20
KVH = 5
HD = 64
GROUP = HQ // KVH
QW = HQ * HD
KVW = KVH * HD
GW = GROUP * HD
LANES = 2 * HD
NEG = -1e30
EPSILON = 1e-06
ROPE_BASE = 10000.0
F32 = jnp.float32
BF16 = jnp.bfloat16
VMEM_LIMIT = 60 << 20


def nn(a, b):
    return lax.dot_general(a, b, (((1,), (0,)), ((), ())), preferred_element_type=F32)


def nt(a, b):
    return lax.dot_general(a, b, (((1,), (1,)), ((), ())), preferred_element_type=F32)


def tn(a, b):
    return lax.dot_general(a, b, (((0,), (0,)), ((), ())), preferred_element_type=F32)


def cost(**_):
    return pl.CostEstimate(flops=1, bytes_accessed=1, transcendentals=0)


def params(limit=VMEM_LIMIT):
    return pltpu.CompilerParams(vmem_limit_bytes=limit)


def after(value, *others):
    return lax.optimization_barrier((value, *others))[0] if others else value


def swap(value, axis, size, mask):
    return lax.ppermute(value, axis, [(i, i ^ mask) for i in range(size)])


class Place:
    def __init__(self, mesh):
        grid = mesh.devices
        self.nd, self.nc = mesh.shape["dp"], mesh.shape["ctx"]
        first = tuple(grid[0, 0].coords)
        bits = [1 << i for i in range(self.nd.bit_length() - 1)]
        far = [b for b in bits if tuple(grid[b, 0].coords)[2] != first[2]]
        self.nf = 1 << len(far)
        self.nn = self.nd // self.nf
        self.far_low = 1 in far
        bits = [1 << i for i in range(self.nc.bit_length() - 1)]
        self.core = [b for b in bits if tuple(grid[0, b].coords) == first]
        self.outer = [b for b in bits if b not in self.core]
        shape = (self.nn, self.nf) if self.far_low else (self.nf, self.nn)
        self.dp = ("near", "far") if self.far_low else ("far", "near")
        self.mesh = Mesh(grid.reshape(*shape, self.nc), (*self.dp, "ctx"))
        combos = [0]
        for bit in self.outer:
            combos = combos + [c | bit for c in combos]
        self.combos = combos
        masks = list(combos)
        for bit in self.core:
            masks = [m for pair in masks for m in (pair, pair | bit)]
        self.masks = masks

    def block(self, far, near):
        return near * self.nf + far if self.far_low else far * self.nn + near

    def cross(self, own, *first):
        held = {m: swap(own, "ctx", self.nc, m) if m else own for m in self.combos}
        for bit in self.core:
            held[bit] = swap(after(own, *first), "ctx", self.nc, bit)
        return held

    def gather(self, held, *hold):
        if not isinstance(held, dict):
            held = self.cross(held)
        held = dict(held)
        for bit in self.core:
            for m in self.combos[1:]:
                held[m | bit] = swap(after(held[m], *hold), "ctx", self.nc, bit)
        return [held[m] for m in self.masks]

    def arrived(self, held):
        return [v for m, v in held.items() if m]

    def exchange(self, blocks):
        return [blocks[0]] + [
            swap(b, "ctx", self.nc, m) for b, m in zip(blocks[1:], self.masks[1:])
        ]

    def scatter_core(self, blocks, kind=BF16):
        came = []
        for bit in self.core:
            kept = {}
            for m in blocks:
                if not m & bit:
                    got = swap(blocks[m | bit].astype(BF16), "ctx", self.nc, bit)
                    came.append(got)
                    kept[m] = combine([blocks[m], got], BF16 if m else kind)[0]
            blocks = kept
        return blocks, came

    def total(self, value):
        got = [swap(value, "ctx", self.nc, m) for m in range(1, self.nc)]
        return sum(got, value), got

    def total_dp(self, value, *hold):
        value = sum([swap(value, "far", self.nf, m) for m in range(1, self.nf)], value)
        value = after(value, *hold)
        return sum([swap(value, "near", self.nn, m) for m in range(1, self.nn)], value)

    def send_outer(self, blocks):
        return [swap(b, "ctx", self.nc, m) for m, b in blocks.items() if m]


def gather_all(place, own):
    nc, nn_, nf = place.nc, place.nn, place.nf
    outer, bits, masks = place.combos[1:], place.core, place.masks
    count = nc * nn_ * nf

    def body(own_ref, *refs):
        out_refs, (send_sem, recv_sem, own_sem) = refs[:nc], refs[nc:]
        here = {a: lax.axis_index(a) for a in ("far", "near", "ctx")}
        barrier = pltpu.get_barrier_semaphore()
        partners = [("far", m) for m in range(1, nf)] + [("near", m) for m in range(1, nn_)]
        partners += [("ctx", m) for m in (*outer, *bits)]
        for axis, m in partners:
            pl.semaphore_signal(
                barrier, inc=1, device_id={axis: here[axis] ^ m}, device_id_type=pl.DeviceIdType.MESH
            )
        pl.semaphore_wait(barrier, len(partners))
        kept = pltpu.make_async_copy(own_ref, out_refs[0].at[0, 0], own_sem)
        kept.start()

        def place_of(k, i, f):
            return out_refs[masks.index(k)].at[i, f]

        sent = {}

        def send(source, key, axis, m):
            n = (masks.index(key[0]) * nn_ + key[1]) * nf + key[2]
            sent[key] = pltpu.make_async_remote_copy(
                src_ref=source,
                dst_ref=place_of(*key),
                send_sem=send_sem.at[n],
                recv_sem=recv_sem.at[n],
                device_id={axis: here[axis] ^ m},
                device_id_type=pl.DeviceIdType.MESH,
            )
            sent[key].start()

        def to_group(source, i, f):
            for m in (*outer, *bits):
                send(source, (m, i, f), "ctx", m)

        for f in range(1, nf):
            send(own_ref, (0, 0, f), "far", f)
        for i in range(1, nn_):
            send(own_ref, (0, i, 0), "near", i)
        to_group(own_ref, 0, 0)
        for f in range(nf):
            if f:
                sent[0, 0, f].wait_recv()
                for i in range(1, nn_):
                    send(place_of(0, 0, f), (0, i, f), "near", i)
                to_group(place_of(0, 0, f), 0, f)
            for i in range(1, nn_):
                sent[0, i, f].wait_recv()
                to_group(place_of(0, i, f), i, f)
        for f in range(nf):
            for i in range(nn_):
                for m in outer:
                    sent[m, i, f].wait_recv()
                    for bit in bits:
                        send(place_of(m, i, f), (m | bit, i, f), "ctx", bit)
        for (k, i, f), copy in sent.items():
            if any(k & bit for bit in bits):
                copy.wait_recv()
            copy.wait_send()
        kept.wait()

    columns, block = own.shape
    return list(
        pl.pallas_call(
            body,
            out_shape=[jax.ShapeDtypeStruct((nn_, nf, columns, block), BF16)] * nc,
            in_specs=[pl.BlockSpec(memory_space=pltpu.VMEM)],
            out_specs=[pl.BlockSpec(memory_space=pl.ANY)] * nc,
            scratch_shapes=[
                pltpu.SemaphoreType.DMA((count,)),
                pltpu.SemaphoreType.DMA((count,)),
                pltpu.SemaphoreType.DMA,
            ],
            compiler_params=pltpu.CompilerParams(
                vmem_limit_bytes=VMEM_LIMIT, collective_id=0, has_side_effects=True
            ),
            cost_estimate=cost(),
            name="gather_all",
        )(own)
    )


def combine(parts, kind, pieces=1):
    shape = parts[0].shape
    tile = 256 if pieces == 1 and shape[0] % 256 == 0 else shape[0]
    block = (tile, *shape[1:])
    out = (shape[0] // pieces, *shape[1:])
    step = tile // pieces

    def body(*refs):
        part_refs, out_refs = refs[: len(parts)], refs[len(parts) :]
        for i, o in enumerate(out_refs):
            at = slice(i * step, (i + 1) * step)
            value = part_refs[0][at].astype(F32)
            for r in part_refs[1:]:
                value = value + r[at].astype(F32)
            o[...] = value.astype(kind)

    index = lambda i: (i,) + (0,) * (len(shape) - 1)
    return pl.pallas_call(
        body,
        out_shape=[jax.ShapeDtypeStruct(out, kind)] * pieces,
        grid=(shape[0] // tile,),
        in_specs=[pl.BlockSpec(block, index)] * len(parts),
        out_specs=[pl.BlockSpec((step, *shape[1:]), index)] * pieces,
        compiler_params=params(),
        cost_estimate=cost(),
        name="combine",
    )(*parts)


def finish_rows(middles, parts, valid):
    rows, (slots, depth) = len(middles), middles[0].shape

    def body(valid_ref, *refs):
        mid_refs, part_refs, out_ref = refs[:rows], refs[rows:-1], refs[-1]
        step = pl.program_id(0)
        y = mid_refs[0][...]
        for r in range(1, rows):
            y = jnp.where(step >= r, mid_refs[r][...], y)
        for p in part_refs:
            y = y + p[...].astype(F32)
        out_ref[...] = (y * valid_ref[...]).astype(BF16)

    whole = lambda i: (0, 0)
    by_row = lambda i: (i, 0)
    return pl.pallas_call(
        body,
        out_shape=jax.ShapeDtypeStruct((rows * slots, depth), BF16),
        grid=(rows,),
        in_specs=[pl.BlockSpec((slots, 1), by_row)]
        + [pl.BlockSpec((slots, depth), whole)] * rows
        + [pl.BlockSpec((slots, depth), by_row)] * len(parts),
        out_specs=pl.BlockSpec((slots, depth), by_row),
        compiler_params=params(),
        cost_estimate=cost(),
        name="finish_rows",
    )(valid, *middles, *parts)


def finish_grads(own, start, width, previous):
    many, units, block = own.shape
    tile = 256 if units % 256 == 0 else units

    def body(own_ref, *refs):
        for k in range(many):
            refs[-many + k][...] = own_ref[k].astype(F32).T

    extra = [] if previous is None else list(previous)
    return pl.pallas_call(
        body,
        out_shape=[jax.ShapeDtypeStruct((block, width), F32)] * many,
        grid=(units // tile,),
        in_specs=[pl.BlockSpec((many, tile, block), lambda i: (0, i, 0))]
        + [pl.BlockSpec(memory_space=pl.ANY)] * len(extra),
        out_specs=[pl.BlockSpec((block, tile), lambda i: (0, start // tile + i))] * many,
        input_output_aliases={1 + k: k for k in range(len(extra))},
        compiler_params=params(),
        cost_estimate=cost(),
        name="finish_grads",
    )(own, *extra)


def head_stats(x, low):
    return lax.rsqrt(head_mean(x * x, low) + EPSILON)


def head_mean(x, low):
    first = jnp.sum(jnp.where(low, x, 0.0), -1, keepdims=True)
    second = jnp.sum(jnp.where(low, 0.0, x), -1, keepdims=True)
    return jnp.where(low, first, second) * (1.0 / HD)


def lane_masks(rows):
    lane = lax.broadcasted_iota(jnp.int32, (rows, LANES), 1)
    return lane < HD, lax.rem(lane, HD) < HD // 2


def spans(start, stop, width):
    out = []
    while start < stop:
        j = start // width
        end = min(stop, (j + 1) * width)
        out.append((j, start - j * width, end - j * width))
        start = end
    return out


def joined(parts):
    return parts[0] if len(parts) == 1 else jnp.concatenate(parts, 1)


def slot_copies(info_ref, place, w_refs, slots_ref, sem):
    copies = []
    flat = len(w_refs[0].shape) == 3
    far, near = info_ref.shape[0] - 2, info_ref.shape[0] - 1
    for k, m in enumerate(place.masks):
        block = w_refs[k].shape[-1]
        for i in range(place.nn):
            for f in range(place.nf):
                if flat:
                    source, at = w_refs[k].at[place.block(f, i)], place.block(f, i)
                else:
                    source, at = w_refs[k].at[i, f], place.block(info_ref[far] ^ f, info_ref[near] ^ i)
                start = at * block if flat else pl.multiple_of(at * block, block)
                copies.append(
                    pltpu.make_async_copy(
                        source,
                        slots_ref.at[info_ref[0] ^ m, :, pl.ds(start, block)],
                        sem.at[len(copies)],
                    )
                )
    return copies


def load_slots(*args):
    copies = slot_copies(*args)
    for c in copies:
        c.start()
    for c in copies:
        c.wait()


def project(info, place, x, gain, w_cols, qc, kc, qgain, kgain, cosine, sine, rows, slots):
    nc, depth, wc = place.nc, x.shape[1], w_cols[0].shape[-2]
    n = rows * slots

    def body(info_ref, x_ref, gain_ref, qgain_ref, kgain_ref, cos_ref, sin_ref, *refs):
        w_refs, (normed_ref, lin_ref, q_ref, kv_ref, w_ref, sem) = refs[:nc], refs[nc:]

        @pl.when(pl.program_id(0) == 0)
        def _():
            load_slots(info_ref, place, w_refs, w_ref, sem)

        xf = x_ref[...].astype(F32)
        inv = lax.rsqrt(jnp.mean(xf * xf, -1, keepdims=True) + EPSILON)
        normed_ref[...] = (xf * inv * gain_ref[...]).astype(BF16)
        for j in range(nc):
            lin_ref[j] = nt(normed_ref[...], w_ref[j])
        low, front = lane_masks(slots)
        cos, sin = cos_ref[...], sin_ref[...]

        def columns(base, width, start, stop):
            return [lin_ref[j, :, base + a : base + b] for j, a, b in spans(start, stop, width)]

        def turn(v, gain):
            v = v * head_stats(v, low) * gain
            turned = jnp.where(
                front, -pltpu.roll(v, LANES - HD // 2, 1), pltpu.roll(v, HD // 2, 1)
            )
            return v * cos + turned * sin

        for c in range(QW // LANES):
            at = slice(c * LANES, (c + 1) * LANES)
            y = turn(joined(columns(0, qc, at.start, at.stop)), qgain_ref[...])
            q_ref[:, at] = (y * (1.0 / math.sqrt(HD))).astype(BF16)
        for g in range(KVH):
            v = joined(
                columns(qc, kc, g * HD, (g + 1) * HD) + columns(qc + kc, kc, g * HD, (g + 1) * HD)
            )
            y = jnp.where(low, turn(v, kgain_ref[...]), v)
            kv_ref[:, g * LANES : (g + 1) * LANES] = y.astype(BF16)

    whole = lambda r, s: (0, 0)
    by_row = lambda r, s: (r, 0)
    return pl.pallas_call(
        body,
        out_shape=(
            jax.ShapeDtypeStruct((n, depth), BF16),
            jax.ShapeDtypeStruct((nc, n, wc), F32),
            jax.ShapeDtypeStruct((n, QW), BF16),
            jax.ShapeDtypeStruct((n, 2 * KVW), BF16),
        ),
        grid_spec=pltpu.PrefetchScalarGridSpec(
            num_scalar_prefetch=1,
            grid=(rows,),
            in_specs=[
                pl.BlockSpec((slots, depth), by_row),
                pl.BlockSpec((1, depth), whole),
                pl.BlockSpec((1, LANES), whole),
                pl.BlockSpec((1, LANES), whole),
                pl.BlockSpec((slots, LANES), whole),
                pl.BlockSpec((slots, LANES), whole),
            ]
            + [pl.BlockSpec(memory_space=pl.ANY)] * nc,
            out_specs=(
                pl.BlockSpec((slots, depth), by_row),
                pl.BlockSpec((nc, slots, wc), lambda r, s: (0, r, 0)),
                pl.BlockSpec((slots, QW), by_row),
                pl.BlockSpec((slots, 2 * KVW), by_row),
            ),
            scratch_shapes=[
                pltpu.VMEM((nc, wc, depth), BF16),
                pltpu.SemaphoreType.DMA((nc * place.nd,)),
            ],
        ),
        compiler_params=params(),
        cost_estimate=cost(
            flops=2 * n * depth * nc * wc, bytes_accessed=2 * nc * depth * wc, transcendentals=n
        ),
        name="project",
    )(info, x, gain, qgain, kgain, cosine, sine, *w_cols)


def heads_back(info, place, dq, dkv_parts, lin, qc, kc, qgain, kgain, cosine, sine, row, slots):
    nc, wc = place.nc, lin.shape[2]

    def body(info_ref, dq_ref, lin_ref, qgain_ref, kgain_ref, cos_ref, sin_ref, *refs):
        dkv_refs, refs = refs[: len(dkv_parts)], refs[len(dkv_parts) :]
        out_ref, gq_ref, gk_ref = refs[:3]
        dlin_refs, (dqs, dks, dvs, dlin_ref) = refs[3 : 3 + nc], refs[3 + nc :]
        low, front = lane_masks(slots)
        cos, sin = cos_ref[...], sin_ref[...]

        def columns(base, width, start, stop):
            return [lin_ref[j, :, base + a : base + b] for j, a, b in spans(start, stop, width)]

        def back(e, v, gain):
            t = e * sin
            e = e * cos + jnp.where(
                front, pltpu.roll(t, LANES - HD // 2, 1), -pltpu.roll(t, HD // 2, 1)
            )
            inv = head_stats(v, low)
            unit = v * inv
            part = e * unit
            u = e * gain
            return inv * (u - unit * head_mean(u * unit, low)), part

        gq = jnp.zeros((1, LANES), F32)
        for c in range(QW // LANES):
            at = slice(c * LANES, (c + 1) * LANES)
            v = joined(columns(0, qc, at.start, at.stop))
            y, part = back(dq_ref[:, at], v, qgain_ref[...])
            dqs[:, at] = y
            gq = gq + jnp.sum(part, 0, keepdims=True)
        gk = jnp.zeros((1, LANES), F32)
        for g in range(KVH):
            e = dkv_refs[0][:, g * LANES : (g + 1) * LANES].astype(F32)
            for ref in dkv_refs[1:]:
                e = e + ref[:, g * LANES : (g + 1) * LANES].astype(F32)
            v = joined(
                columns(qc, kc, g * HD, (g + 1) * HD) + columns(qc + kc, kc, g * HD, (g + 1) * HD)
            )
            y, part = back(e, v, kgain_ref[...])
            dks[:, g * HD : (g + 1) * HD] = y[:, :HD]
            dvs[:, g * HD : (g + 1) * HD] = e[:, HD:]
            gk = gk + jnp.sum(jnp.where(low, part, 0.0), 0, keepdims=True)
        gq_ref[...] = gq
        gk_ref[...] = gk
        for j in range(nc):
            dlin = jnp.concatenate(
                [
                    dqs[:, j * qc : (j + 1) * qc],
                    dks[:, j * kc : (j + 1) * kc],
                    dvs[:, j * kc : (j + 1) * kc],
                ],
                1,
            )
            out_ref[j] = dlin.astype(BF16)
            dlin_ref[j] = dlin.T.astype(BF16)
        for k, m in enumerate(place.masks):
            dlin_refs[k][...] = dlin_ref[info_ref[0] ^ m]

    whole = lambda i, s: (0, 0)
    cube = lambda i, s: (0, 0, 0)
    lane = pl.BlockSpec((1, LANES), whole)
    table = pl.BlockSpec((slots, LANES), whole)
    return pl.pallas_call(
        body,
        out_shape=(
            jax.ShapeDtypeStruct((nc, slots, wc), BF16),
            jax.ShapeDtypeStruct((1, LANES), F32),
            jax.ShapeDtypeStruct((1, LANES), F32),
            *([jax.ShapeDtypeStruct((wc, slots), BF16)] * nc),
        ),
        grid_spec=pltpu.PrefetchScalarGridSpec(
            num_scalar_prefetch=1,
            grid=(1,),
            in_specs=[
                pl.BlockSpec((slots, QW), whole),
                pl.BlockSpec((nc, slots, wc), lambda i, s: (0, row, 0)),
                lane,
                lane,
                table,
                table,
            ]
            + [pl.BlockSpec((slots, 2 * KVW), whole)] * len(dkv_parts),
            out_specs=(
                pl.BlockSpec((nc, slots, wc), cube),
                lane,
                lane,
                *([pl.BlockSpec((wc, slots), whole)] * nc),
            ),
            scratch_shapes=[
                pltpu.VMEM((slots, QW), F32),
                pltpu.VMEM((slots, KVW), F32),
                pltpu.VMEM((slots, KVW), F32),
                pltpu.VMEM((nc, wc, slots), BF16),
            ],
        ),
        compiler_params=params(),
        cost_estimate=cost(),
        name="heads_back",
    )(info, dq, lin, qgain, kgain, cosine, sine, *dkv_parts)


def project_back(info, place, dlins, x, middle_grad, gain, w_cols, rows, slots):
    nc, depth, wc = place.nc, x.shape[1], w_cols[0].shape[-2]

    def body(info_ref, x_ref, mid_ref, gain_ref, *refs):
        dlin_refs, refs = refs[:rows], refs[rows:]
        w_refs, (out_ref, ga_ref, w_ref, sem) = refs[:nc], refs[nc:]
        step = pl.program_id(0)

        @pl.when(step == 0)
        def _():
            load_slots(info_ref, place, w_refs, w_ref, sem)
            ga_ref[...] = jnp.zeros_like(ga_ref)

        grad = None
        for j in range(nc):
            dlin = dlin_refs[0][j]
            for r in range(1, rows):
                dlin = jnp.where(step >= r, dlin_refs[r][j], dlin)
            part = nn(dlin, w_ref[j])
            grad = part if grad is None else grad + part
        xf = x_ref[...].astype(F32)
        inv = lax.rsqrt(jnp.mean(xf * xf, -1, keepdims=True) + EPSILON)
        unit = xf * inv
        ga_ref[...] += jnp.sum(grad * unit, 0, keepdims=True)
        u = grad * gain_ref[...]
        back_x = inv * (u - unit * jnp.mean(u * unit, -1, keepdims=True))
        out_ref[...] = (mid_ref[...] + back_x).astype(BF16)

    whole = lambda i, s: (0, 0)
    by_row = lambda i, s: (i, 0)
    return pl.pallas_call(
        body,
        out_shape=(
            jax.ShapeDtypeStruct((rows * slots, depth), BF16),
            jax.ShapeDtypeStruct((1, depth), F32),
        ),
        grid_spec=pltpu.PrefetchScalarGridSpec(
            num_scalar_prefetch=1,
            grid=(rows,),
            in_specs=[
                pl.BlockSpec((slots, depth), by_row),
                pl.BlockSpec((slots, depth), by_row),
                pl.BlockSpec((1, depth), whole),
            ]
            + [pl.BlockSpec((nc, slots, wc), lambda i, s: (0, 0, 0))] * rows
            + [pl.BlockSpec(memory_space=pl.ANY)] * nc,
            out_specs=(pl.BlockSpec((slots, depth), by_row), pl.BlockSpec((1, depth), whole)),
            scratch_shapes=[
                pltpu.VMEM((nc, wc, depth), BF16),
                pltpu.SemaphoreType.DMA((nc * place.nd,)),
            ],
        ),
        compiler_params=params(),
        cost_estimate=cost(),
        name="project_back",
    )(info, x, middle_grad, gain, *dlins, *w_cols)


def fill_bias(bias_ref, info_ref, row, masks, slots):
    place, length = info_ref[0], info_ref[1 + row]
    query = place * slots + lax.broadcasted_iota(jnp.int32, (slots, slots), 1)
    for i, mask in enumerate(masks):
        key = (place ^ mask) * slots + lax.broadcasted_iota(jnp.int32, (slots, slots), 0)
        allowed = (key <= query) & (key < length)
        bias_ref[i * slots : (i + 1) * slots, :] = jnp.where(allowed, 0.0, NEG)


def attend(info, q, kv_pieces, masks, row, slots):
    count = len(masks)
    keys = count * slots

    def body(info_ref, q_ref, *refs):
        kv_refs, (o_ref, ot_ref, lse_ref, bias_ref) = refs[:count], refs[count:]
        live = info_ref[0] * slots < info_ref[1 + row]

        @pl.when(live & (pl.program_id(0) == 0))
        def _():
            fill_bias(bias_ref, info_ref, row, masks, slots)

        @pl.when(jnp.logical_not(live))
        def _():
            o_ref[...] = jnp.zeros_like(o_ref)
            ot_ref[...] = jnp.zeros_like(ot_ref)
            lse_ref[...] = jnp.zeros_like(lse_ref)

        @pl.when(live)
        def _():
            kv = jnp.concatenate([r[...] for r in kv_refs], 0)
            k, v = kv[:, :HD], kv[:, HD:]
            for h in range(GROUP):
                qh = q_ref[:, h * HD : (h + 1) * HD]
                e = jnp.exp(nt(k, qh) + bias_ref[...])
                l = jnp.sum(e, 0, keepdims=True)
                o = tn(v, (e * (1.0 / l)).astype(BF16))
                o_ref[:, h * HD : (h + 1) * HD] = o.T.astype(BF16)
                ot_ref[h * HD : (h + 1) * HD, :] = o.astype(BF16)
                lse_ref[0, h : h + 1, :] = jnp.log(l)

    n = slots
    return pl.pallas_call(
        body,
        out_shape=(
            jax.ShapeDtypeStruct((n, QW), BF16),
            jax.ShapeDtypeStruct((QW, n), BF16),
            jax.ShapeDtypeStruct((KVH, GROUP, slots), F32),
        ),
        grid_spec=pltpu.PrefetchScalarGridSpec(
            num_scalar_prefetch=1,
            grid=(KVH,),
            in_specs=[pl.BlockSpec((slots, GW), lambda g, s: (row, g))]
            + [pl.BlockSpec((slots, LANES), lambda g, s: (row, g))] * count,
            out_specs=(
                pl.BlockSpec((slots, GW), lambda g, s: (0, g)),
                pl.BlockSpec((GW, slots), lambda g, s: (g, 0)),
                pl.BlockSpec((1, GROUP, slots), lambda g, s: (g, 0, 0)),
            ),
            scratch_shapes=[pltpu.VMEM((keys, slots), F32)],
        ),
        compiler_params=params(),
        cost_estimate=cost(
            flops=16 * n * keys * QW, bytes_accessed=8 * n * QW, transcendentals=n * keys * HQ
        ),
        name="attend",
    )(info, q, *kv_pieces)


def attend_back(info, q, kv_pieces, do, lse, masks, row, slots):
    count = len(masks)
    keys = count * slots

    def body(info_ref, q_ref, do_ref, lse_ref, *refs):
        kv_refs, dq_ref = refs[:count], refs[count]
        dkv_refs, bias_ref = refs[count + 1 : -1], refs[-1]
        live = info_ref[0] * slots < info_ref[1 + row]

        @pl.when(live & (pl.program_id(0) == 0))
        def _():
            fill_bias(bias_ref, info_ref, row, masks, slots)

        @pl.when(jnp.logical_not(live))
        def _():
            dq_ref[...] = jnp.zeros_like(dq_ref)
            for r in dkv_refs:
                r[...] = jnp.zeros_like(r)

        @pl.when(live)
        def _():
            kv = jnp.concatenate([r[...] for r in kv_refs], 0)
            k, v = kv[:, :HD], kv[:, HD:]
            dk = jnp.zeros((keys, HD), F32)
            dv = jnp.zeros((keys, HD), F32)
            for h in range(GROUP):
                at = slice(h * HD, (h + 1) * HD)
                qh, doh = q_ref[:, at], do_ref[:, at]
                p = jnp.exp(nt(k, qh) + bias_ref[...] - lse_ref[0, h : h + 1, :])
                dp = nt(v, doh)
                delta = jnp.sum(p * dp, 0, keepdims=True)
                ds = (p * (dp - delta)).astype(BF16)
                dv = dv + nn(p.astype(BF16), doh)
                dk = dk + nn(ds, qh)
                dq_ref[:, at] = tn(k, ds).T * (1.0 / math.sqrt(HD))
            both = jnp.concatenate([dk, dv], 1).astype(BF16)
            for i, r in enumerate(dkv_refs):
                r[...] = both[i * slots : (i + 1) * slots, :]

    n = slots
    kv_spec = pl.BlockSpec((slots, LANES), lambda g, s: (row, g))
    q_spec = pl.BlockSpec((slots, GW), lambda g, s: (row, g))
    out_kv = pl.BlockSpec((slots, LANES), lambda g, s: (0, g))
    out_q = pl.BlockSpec((slots, GW), lambda g, s: (0, g))
    return pl.pallas_call(
        body,
        out_shape=(
            jax.ShapeDtypeStruct((n, QW), F32),
            *([jax.ShapeDtypeStruct((n, 2 * KVW), BF16)] * count),
        ),
        grid_spec=pltpu.PrefetchScalarGridSpec(
            num_scalar_prefetch=1,
            grid=(KVH,),
            in_specs=[
                q_spec,
                q_spec,
                pl.BlockSpec((1, GROUP, slots), lambda g, s: (g, 0, 0)),
            ]
            + [kv_spec] * count,
            out_specs=(out_q, *([out_kv] * count)),
            scratch_shapes=[pltpu.VMEM((keys, slots), F32)],
        ),
        compiler_params=params(),
        cost_estimate=cost(
            flops=40 * n * keys * QW, bytes_accessed=16 * n * QW, transcendentals=n * keys * HQ
        ),
        name="attend_back",
    )(info, q, do, lse, *kv_pieces)


def out_project(info, place, mixed, x, gain, w_cols, row):
    nc, depth, oc = place.nc, x.shape[1], w_cols[0].shape[-2]
    slots = mixed.shape[0]
    td = 256

    def body(info_ref, mixed_ref, x_ref, gain_ref, *refs):
        w_refs, (mid_ref, n2_ref, w_ref, sem) = refs[:nc], refs[nc:]
        load_slots(info_ref, place, w_refs, w_ref, sem)
        parts = [mixed_ref[:, j * oc : (j + 1) * oc] for j in range(nc)]
        square = jnp.zeros((slots, 1), F32)
        for d in range(depth // td):
            at = slice(d * td, (d + 1) * td)
            y = x_ref[:, at].astype(F32)
            for j in range(nc):
                y = y + nn(parts[j], w_ref[j, :, at])
            mid_ref[:, at] = y
            square = square + jnp.sum(y * y, -1, keepdims=True)
        inv = lax.rsqrt(square * (1.0 / depth) + EPSILON)
        n2_ref[...] = (mid_ref[...] * inv * gain_ref[...]).astype(BF16)

    whole = lambda i, s: (0, 0)
    return pl.pallas_call(
        body,
        out_shape=(
            jax.ShapeDtypeStruct((slots, depth), F32),
            jax.ShapeDtypeStruct((slots, depth), BF16),
        ),
        grid_spec=pltpu.PrefetchScalarGridSpec(
            num_scalar_prefetch=1,
            grid=(1,),
            in_specs=[
                pl.BlockSpec((slots, nc * oc), whole),
                pl.BlockSpec((slots, depth), lambda i, s: (row, 0)),
                pl.BlockSpec((1, depth), whole),
            ]
            + [pl.BlockSpec(memory_space=pl.ANY)] * nc,
            out_specs=(pl.BlockSpec((slots, depth), whole), pl.BlockSpec((slots, depth), whole)),
            scratch_shapes=[
                pltpu.VMEM((nc, oc, depth), BF16),
                pltpu.SemaphoreType.DMA((nc * place.nd,)),
            ],
        ),
        compiler_params=params(),
        cost_estimate=cost(
            flops=2 * slots * depth * nc * oc, bytes_accessed=4 * nc * depth * oc, transcendentals=0
        ),
        name="out_project",
    )(info, mixed, x, gain, *w_cols)


def middle_back(info, place, parts, middles, bg, gain, w_cols, rows, slots):
    nc, depth, oc, count = place.nc, bg.shape[1], w_cols[0].shape[-2], len(parts)
    n = rows * slots

    def body(info_ref, *refs):
        part_refs, refs = refs[:count], refs[count:]
        mid_refs, refs = refs[:rows], refs[rows:]
        bg_ref, gain_ref, refs = refs[0], refs[1], refs[2:]
        w_refs, (mg_ref, ag_ref, xg_ref, gf_ref, w_ref, sem) = refs[:nc], refs[nc:]
        step = pl.program_id(0)

        @pl.when(step == 0)
        def _():
            load_slots(info_ref, place, w_refs, w_ref, sem)
            gf_ref[...] = jnp.zeros_like(gf_ref)

        grad = part_refs[0][...].astype(F32)
        for p in part_refs[1:]:
            grad = grad + p[...].astype(F32)
        mid = mid_refs[0][...]
        for r in range(1, rows):
            mid = jnp.where(step >= r, mid_refs[r][...], mid)
        inv = lax.rsqrt(jnp.mean(mid * mid, -1, keepdims=True) + EPSILON)
        unit = mid * inv
        gf_ref[...] += jnp.sum(grad * unit, 0, keepdims=True)
        u = grad * gain_ref[...]
        y = bg_ref[...].astype(F32) + inv * (u - unit * jnp.mean(u * unit, -1, keepdims=True))
        mg_ref[...] = y
        ag_ref[...] = y.astype(BF16)
        xg_ref[...] = jnp.concatenate(
            [nt(ag_ref[...], w_ref[j]) for j in range(nc)], 1
        ).astype(BF16)

    whole = lambda i, s: (0, 0)
    by_row = lambda i, s: (i, 0)
    token = pl.BlockSpec((slots, depth), by_row)
    return pl.pallas_call(
        body,
        out_shape=(
            jax.ShapeDtypeStruct((n, depth), F32),
            jax.ShapeDtypeStruct((n, depth), BF16),
            jax.ShapeDtypeStruct((n, nc * oc), BF16),
            jax.ShapeDtypeStruct((1, depth), F32),
        ),
        grid_spec=pltpu.PrefetchScalarGridSpec(
            num_scalar_prefetch=1,
            grid=(rows,),
            in_specs=[token] * count
            + [pl.BlockSpec((slots, depth), whole)] * rows
            + [token, pl.BlockSpec((1, depth), whole)]
            + [pl.BlockSpec(memory_space=pl.ANY)] * nc,
            out_specs=(
                token,
                token,
                pl.BlockSpec((slots, nc * oc), by_row),
                pl.BlockSpec((1, depth), whole),
            ),
            scratch_shapes=[
                pltpu.VMEM((nc, oc, depth), BF16),
                pltpu.SemaphoreType.DMA((nc * place.nd,)),
            ],
        ),
        compiler_params=params(),
        cost_estimate=cost(
            flops=2 * n * depth * nc * oc, bytes_accessed=20 * n * depth, transcendentals=0
        ),
        name="middle_back",
    )(info, *parts, *middles, bg, gain, *w_cols)


def feed_forward(info, place, weights, n2, bg, sums, acts, total, first, last):
    owners, (tokens, depth), units = len(n2), bg[0].shape, weights.shape[1]
    cuts = len(n2[0])
    part = tokens // cuts
    block = depth // place.nd
    tu = 256 if units % 256 == 0 else units
    td = 256
    sum_type = BF16 if last else F32
    has_sums, has_acts = sums is not None, acts is not None

    def body(info_ref, w_ref, *refs):
        n2_refs, refs = refs[: owners * cuts], refs[owners * cuts :]
        bg_refs, refs = refs[:owners], refs[owners:]
        sum_refs = ()
        if has_sums:
            sum_refs, refs = refs[: 2 * owners], refs[2 * owners :]
        if has_acts:
            refs = refs[3:]
        out_refs, refs = refs[: 2 * owners], refs[2 * owners :]
        ht_ref, ggt_ref, ugt_ref, wg, wu, wd, acts_buf, tok_buf, out_buf = refs[:9]
        w_sem, tok_sem, out_sem = refs[9:12]
        in_buf, in_sem = refs[12:] if has_sums else (None, None)
        step = pl.program_id(0)
        slot = lax.rem(step, 2)

        def token_copies(p, to):
            found = [
                pltpu.make_async_copy(
                    n2_refs[p * cuts + i],
                    tok_buf.at[to, 0, i * part : (i + 1) * part, :],
                    tok_sem.at[to, i],
                )
                for i in range(cuts)
            ]
            return found + [
                pltpu.make_async_copy(bg_refs[p], tok_buf.at[to, 1], tok_sem.at[to, cuts])
            ]

        def sum_copies(p):
            return [
                pltpu.make_async_copy(sum_refs[2 * p + k], in_buf.at[k], in_sem.at[k])
                for k in range(2)
            ]

        def out_copies(p):
            return [
                pltpu.make_async_copy(out_buf.at[k], out_refs[2 * p + k], out_sem.at[k])
                for k in range(2)
            ]

        @pl.when(step == 0)
        def _():
            for c in token_copies(0, 0):
                c.start()
            copies = []
            for i in range(place.nd):
                for j, dst in enumerate((wg, wu, wd)):
                    start = (3 * i + j) * block
                    copies.append(
                        pltpu.make_async_copy(
                            w_ref.at[start : start + block, :],
                            dst.at[i * block : (i + 1) * block, :],
                            w_sem.at[len(copies)],
                        )
                    )
            for c in copies:
                c.start()
            for c in copies:
                c.wait()

        for p in range(owners):

            @pl.when(step == p)
            def _():
                if p + 1 < owners:
                    for c in token_copies(p + 1, (p + 1) % 2):
                        c.start()
                if has_sums:
                    for c in sum_copies(p):
                        c.start()

        for c in token_copies(0, slot):
            c.wait()
        x, b = tok_buf[slot, 0], tok_buf[slot, 1]
        for j in range(units // tu):
            at = slice(j * tu, (j + 1) * tu)
            gate, up = nn(x, wg[:, at]), nn(x, wu[:, at])
            dh = nn(b, wd[:, at])
            sig = 1.0 / (1.0 + jnp.exp(-gate))
            act = gate * sig
            h = act * up
            gg = dh * up * sig * (1.0 + gate * (1.0 - sig))
            ug = dh * act
            for k, (value, ref) in enumerate(((h, ht_ref), (gg, ggt_ref), (ug, ugt_ref))):
                acts_buf[k, :, at] = value.astype(BF16)
                ref[at, :] = value.T.astype(BF16)

        @pl.when(step > 0)
        def _():
            for c in out_copies(0):
                c.wait()

        if has_sums:
            for c in sum_copies(0):
                c.wait()
        h, gg, ug = acts_buf[0], acts_buf[1], acts_buf[2]
        for j in range(depth // td):
            at = slice(j * td, (j + 1) * td)
            values = [nt(h, wd[at, :]), nt(gg, wg[at, :]) + nt(ug, wu[at, :])]
            for k in range(2):
                value = values[k]
                if has_sums:
                    value = value + in_buf[k, :, at]
                out_buf[k, :, at] = value.astype(sum_type)
        for p in range(owners):

            @pl.when(step == p)
            def _():
                for c in out_copies(p):
                    c.start()

        @pl.when(step == owners - 1)
        def _():
            for c in out_copies(0):
                c.wait()

    any_spec = pl.BlockSpec(memory_space=pl.ANY)
    act_spec = pl.BlockSpec((units, tokens), lambda i, s: (0, i + first))
    operands = [weights, *[v for group in n2 for v in group], *bg]
    aliases = {}
    if has_sums:
        operands += [v for pair in sums for v in pair]
    if has_acts:
        for j in range(3):
            aliases[1 + len(operands) + j] = 2 * owners + j
        operands += acts
    n = owners * tokens
    scratch = [pltpu.VMEM((depth, units), BF16)] * 3 + [
        pltpu.VMEM((3, tokens, units), BF16),
        pltpu.VMEM((2, 2, tokens, depth), BF16),
        pltpu.VMEM((2, tokens, depth), sum_type),
        pltpu.SemaphoreType.DMA((3 * place.nd,)),
        pltpu.SemaphoreType.DMA((2, cuts + 1)),
        pltpu.SemaphoreType.DMA((2,)),
    ]
    if has_sums:
        scratch += [pltpu.VMEM((2, tokens, depth), F32), pltpu.SemaphoreType.DMA((2,))]
    out = pl.pallas_call(
        body,
        out_shape=(
            *([jax.ShapeDtypeStruct((tokens, depth), sum_type)] * (2 * owners)),
            *([jax.ShapeDtypeStruct((units, total), BF16)] * 3),
        ),
        grid_spec=pltpu.PrefetchScalarGridSpec(
            num_scalar_prefetch=1,
            grid=(owners,),
            in_specs=[any_spec] * len(operands),
            out_specs=(*([any_spec] * (2 * owners)), act_spec, act_spec, act_spec),
            scratch_shapes=scratch,
        ),
        input_output_aliases=aliases,
        compiler_params=params(),
        cost_estimate=cost(
            flops=12 * n * depth * units, bytes_accessed=16 * n * depth, transcendentals=n * units
        ),
        name="feed_forward",
    )(info, *operands)
    return [list(out[2 * o : 2 * o + 2]) for o in range(owners)], list(out[2 * owners :])


def weight_grads(order, block, sets, width, added=None, apart=False):
    lefts = [v for left, _ in sets for v in left]
    rights = [v for _, right in sets for group in right for v in group]
    many, blocks = sum(len(right) for _, right in sets), order.shape[0]

    def body(order_ref, *refs):
        left_refs, refs = refs[: len(lefts)], refs[len(lefts) :]
        right_refs, refs = refs[: len(rights)], refs[len(rights) :]
        extra_ref, out_refs = (None, refs) if added is None else (refs[0], refs[1:])
        i = k = at = 0
        for left, right in sets:
            tall = joined_rows([r[...] for r in left_refs[i : i + len(left)]])
            i += len(left)
            wides = []
            for group in right:
                wides.append(joined([r[...] for r in right_refs[at : at + len(group)]]))
                at += len(group)
            values = nn(joined_rows(wides), tall)
            for m in range(len(right)):
                value = values[m * width : (m + 1) * width]
                if added is not None:
                    value = value + extra_ref[0, k].astype(F32)
                if apart:
                    for f in range(blocks):

                        @pl.when(pl.program_id(0) == f)
                        def _():
                            out_refs[f][k] = value.astype(BF16)
                else:
                    out_refs[0][0, k] = value.astype(BF16)
                k += 1

    part = pl.BlockSpec((1, many, width, block), lambda i, ix: (i, 0, 0, 0))
    extra = [] if added is None else [added]
    if apart:
        shapes = [jax.ShapeDtypeStruct((many, width, block), BF16)] * blocks
        specs = [pl.BlockSpec((many, width, block), lambda i, ix: (0, 0, 0))] * blocks
    else:
        shapes = jax.ShapeDtypeStruct((blocks, many, width, block), BF16)
        specs = part
    return pl.pallas_call(
        body,
        out_shape=shapes,
        grid_spec=pltpu.PrefetchScalarGridSpec(
            num_scalar_prefetch=1,
            grid=(blocks,),
            in_specs=[pl.BlockSpec((v.shape[0], block), lambda i, ix: (0, ix[i])) for v in lefts]
            + [pl.BlockSpec((width, v.shape[1]), lambda i, ix: (0, 0)) for v in rights]
            + [part] * len(extra),
            out_specs=specs,
        ),
        compiler_params=params(),
        cost_estimate=cost(),
        name="weight_grads",
    )(order, *lefts, *rights, *extra)


def out_weight_grads(order, place, block, left, rights):
    nc, blocks = place.nc, order.shape[0] - 1
    width = rights[0].shape[0]
    part = width // nc

    def body(order_ref, left_ref, *refs):
        right_refs, refs = refs[: len(rights)], refs[len(rights) :]
        out_refs, value_ref = refs[:nc], refs[nc]
        value_ref[...] = nn(joined([r[...] for r in right_refs]), left_ref[...])
        for k, m in enumerate(place.masks):
            start = pl.multiple_of((order_ref[blocks] ^ m) * part, part & -part)
            out_refs[k][0] = value_ref[pl.ds(start, part), :].astype(BF16)

    return pl.pallas_call(
        body,
        out_shape=[jax.ShapeDtypeStruct((blocks, part, block), BF16)] * nc,
        grid_spec=pltpu.PrefetchScalarGridSpec(
            num_scalar_prefetch=1,
            grid=(blocks,),
            in_specs=[pl.BlockSpec((left.shape[0], block), lambda i, ix: (0, ix[i]))]
            + [pl.BlockSpec(v.shape, lambda i, ix: (0, 0)) for v in rights],
            out_specs=[pl.BlockSpec((1, part, block), lambda i, ix: (i, 0, 0))] * nc,
            scratch_shapes=[pltpu.VMEM((width, block), F32)],
        ),
        compiler_params=params(),
        cost_estimate=cost(),
        name="out_weight_grads",
    )(order, left, *rights)


def joined_rows(parts):
    return parts[0] if len(parts) == 1 else jnp.concatenate(parts, 0)


def rope_tables(positions):
    steps_half = jnp.arange(HD // 2, dtype=F32)
    inverse = jnp.exp(steps_half * (-2.0 * math.log(ROPE_BASE) / HD))
    angles = positions.astype(F32)[:, None] * inverse[None, :]
    return jnp.tile(jnp.cos(angles), (1, 4)), jnp.tile(jnp.sin(angles), (1, 4))


def make_layer(place):
    nd, nc, nf, nn_, masks = place.nd, place.nc, place.nf, place.nn, place.masks
    half = nc // 2

    def per_device(
        layer_input,
        lengths,
        attn_gain,
        w_query,
        w_key,
        w_value,
        query_gain,
        key_gain,
        w_out,
        ffn_gain,
        w_gate,
        w_up,
        w_down,
        cotangent,
    ):
        rows, slots, depth = layer_input.shape
        n = rows * slots
        block = depth // nd
        qc, kc, oc, units = w_query.shape[1], w_key.shape[1], w_out.shape[1], w_gate.shape[1]
        per = rows if slots % LANES == 0 else 1
        far, near = lax.axis_index("far"), lax.axis_index("near")
        spot = lax.axis_index("ctx")
        fars = jnp.arange(nf, dtype=jnp.int32)
        to_near = [place.block(fars, near ^ i) for i in range(nn_)]
        to_near_far = [place.block(far ^ fars, near ^ i) for i in range(nn_)]
        everywhere = jnp.arange(nd, dtype=jnp.int32)
        every = jnp.concatenate([*to_near, spot[None].astype(jnp.int32)], 0)
        positions = spot * slots + jnp.arange(slots, dtype=jnp.int32)
        cosine, sine = rope_tables(positions)
        info = jnp.concatenate(
            [spot[None].astype(jnp.int32), lengths, jnp.stack([far, near]).astype(jnp.int32)]
        )
        valid = (positions[None, :] < lengths[:, None]).astype(F32).reshape(n, 1)
        qgain2 = jnp.tile(query_gain, 2)[None, :]
        kgain2 = jnp.tile(key_gain, 2)[None, :]
        gain_one, gain_two = attn_gain[None, :], ffn_gain[None, :]
        x = layer_input.reshape(n, depth)

        def gather_dp(value, tiled):
            return lax.all_gather(value, place.dp, axis=0, tiled=tiled)

        bg = (cotangent.reshape(n, depth).astype(F32) * valid).astype(BF16)
        qkv_cols = gather_all(place, jnp.concatenate([w_query.T, w_key.T, w_value.T], 0))
        out_dp = gather_dp(w_out.T, False)
        out_cross = place.cross(after(out_dp, qkv_cols[1]))
        sizes = [768, 512] if units == 1280 else [units]
        starts = [sum(sizes[:c]) for c in range(len(sizes))]
        chunks = []
        for start, size in zip(starts, sizes):
            at = slice(start, start + size)
            local = jnp.concatenate([w_gate[:, at], w_up[:, at], w_down[:, at]], 0)
            chunks.append(gather_dp(after(local, qkv_cols[1]), True))

        normed, lin, q, kv = project(
            info, place, x, gain_one, qkv_cols, qc, kc, qgain2, kgain2, cosine, sine,
            rows, slots,
        )
        out_cols = place.gather(out_cross, q)
        kv_cross = place.cross(kv)
        kv_all = place.gather(kv_cross)
        bg_cross = place.cross(after(bg, *place.arrived(kv_cross)))
        bg_all = place.gather(bg_cross)
        mixed_t, lse, middles, n2_cross = [], [], [], []
        before, due = place.arrived(out_cross), []
        for r in range(rows):
            m, mt, l = attend(info, after(q, *before), kv_all, masks, r, slots)
            if r == rows - 1:
                due = due + place.arrived(bg_cross)
            mid, n2 = out_project(info, place, after(m, *due), x, gain_two, out_cols, r)
            mixed_t.append(mt)
            lse.append(l)
            middles.append(mid)
            before, due = [mid], []
            if per == rows:
                n2_cross.append(place.cross(n2))
                due = place.arrived(n2_cross[-1])
            else:
                n2_cross.append(n2)
        if per != rows:
            n2_cross = [place.cross(jnp.concatenate(n2_cross, 0))]

        n2_got = [place.gather(v) for v in n2_cross]
        n2_all = [[v[i] for v in n2_got] for i in range(nc)]
        n2_flat = [v for group in n2_all for v in group]
        sums = [None] * nc
        ffn_grads, last_out = [], []

        def whole(sets, size):
            part = weight_grads(after(everywhere, *last_out), block, sets, size)
            own = lax.psum_scatter(
                part.reshape(nd * 3 * size, block), place.dp, scatter_dimension=0, tiled=True
            )
            ffn_grads.append(own.reshape(3, size, block))
            return part

        def send(sets, size):
            got = None
            for i in range(1, nn_):
                mine = weight_grads(after(to_near[i], *last_out), block, sets, size)
                part = swap(mine, "near", nn_, i)
                got = part if got is None else got + part
            return mine, (sets, size, got)

        def keep(entry):
            sets, size, got = entry
            part = weight_grads(after(to_near[0], *last_out), block, sets, size, got)
            own = lax.psum_scatter(
                part.reshape(nf * 3 * size, block), "far", scatter_dimension=0, tiled=True
            )
            ffn_grads.append(own.reshape(3, size, block))
            return part

        def scatter_core_of(k, which, *hold):
            return place.scatter_core({masks[i]: after(sums[i][k], *hold) for i in which})[0]

        near_side, far_side = range(half), range(half, nc)
        normed_cross = place.cross(after(normed, *place.arrived(n2_cross[-1])))
        waiting = []
        for c, weights in enumerate(chunks):
            acts, ends = None, c == len(chunks) - 1
            for at in (slice(half, nc), slice(0, half)) if ends else (slice(0, nc),):
                sums[at], acts = feed_forward(
                    after(info, *last_out), place, weights, n2_all[at], bg_all[at],
                    None if c == 0 else sums[at], acts, nc * n, at.start, ends,
                )
                last_out = [acts[0]]
                if ends and at.start:
                    grads = scatter_core_of(1, far_side)
                    grads_got = place.send_outer(grads)
                    last_out = [acts[0], *grads.values()]
            h, gg, ug = [[a] for a in acts]
            sets = [(n2_flat, [gg, ug]), (bg_all, [h])]
            if nn_ == 1:
                last_out = [whole(sets, sizes[c])]
            else:
                mine, entry = send(sets, sizes[c])
                waiting.append(entry)
                last_out = [mine]
            if not ends:
                last_out = last_out + place.arrived(normed_cross)
        normed_got = place.gather(normed_cross, *last_out)
        grad_parts = [scatter_core_of(1, near_side, *last_out, *grads_got)[0], *grads_got]

        middle_grad, attn_grad, mixed_grad, gf = middle_back(
            after(info, *last_out), place, grad_parts, middles, bg, gain_two, out_cols, rows, slots
        )
        branches = scatter_core_of(0, far_side, mixed_grad)
        branches |= scatter_core_of(0, near_side, mixed_grad)
        w_out_all = out_weight_grads(after(every, mixed_grad), place, block, attn_grad, mixed_t)
        w_out_core, _ = place.scatter_core(dict(zip(masks, w_out_all)))
        dqs, cores = [], []
        outer = place.combos[1:]
        last_out = [w_out_all[0], *[w_out_core[m] for m in outer]]
        for r in range(rows):
            dq, *dkv = attend_back(
                after(info, *last_out), q, kv_all, mixed_grad, lse[r], masks, r, slots
            )
            dqs.append(dq)
            last_out = [dq]
            if r == 0:
                w_out_got = place.send_outer({m: after(b, dq) for m, b in w_out_core.items()})
                if len(waiting) > 1:
                    last_out = [keep(waiting.pop(0))]
                last_out = last_out + normed_got[1:] + list(branches.values())
            cores.append(place.scatter_core(dict(zip(masks, dkv)), F32))
        dkvs = [[core[0], *place.send_outer(core)] for core, _ in cores]
        last_out = last_out + [core[m] for core, _ in cores for m in outer]

        dlins, dlin_got, gq, gk = [], [], [], []
        for r in range(rows):
            own, gq_r, gk_r, *dlin = heads_back(
                after(info, *last_out), place, dqs[r], dkvs[r], lin, qc, kc, qgain2, kgain2, cosine, sine,
                r, slots,
            )
            dlins.append(own)
            dlin_got.append(place.exchange(dlin))
            last_out = [own]
            if r == rows - 1:
                last_out = last_out + w_out_got
            if waiting and r == rows - 1:
                last_out = [keep(waiting.pop(0))]
            gq.append(gq_r[0])
            gk.append(gk_r[0])
        input_grad, ga = project_back(
            after(info, *last_out, *ffn_grads[:1]), place, dlins, x, middle_grad, gain_one, qkv_cols, rows, slots
        )
        halves = combine([w_out_core[0], *[after(g, input_grad) for g in w_out_got]], BF16, nn_)
        halves = [halves[0]] + [
            swap(h, "near", nn_, i) for i, h in enumerate(halves[1:], 1)
        ]

        w_out_half = combine([halves[0], *[after(h, input_grad) for h in halves[1:]]], BF16)[0]
        w_out_grad = lax.psum_scatter(
            w_out_half.reshape(nf * oc, block), "far", scatter_dimension=0, tiled=True
        )

        def summed(parts):
            total = parts[0].astype(F32)
            for p in parts[1:]:
                total = total + p.astype(F32)
            return total[0]

        gains, gains_got = place.total(jnp.concatenate([ga[0], gf[0], sum(gq), sum(gk)]))
        right = [dlin_got[r][i] for i in range(nc) for r in range(rows)]
        if per != rows:
            right = [jnp.concatenate(right, 1)]
        got = None
        for i in reversed(range(nn_)):
            part = weight_grads(
                after(to_near_far[i], input_grad, *ffn_grads[:1]), block, [(normed_got, [right])], qc + 2 * kc,
                got if i == 0 else None, i == 0,
            )
            if i:
                branch_got = place.send_outer({m: after(b, part, *gains_got) for m, b in branches.items()})
                part = swap(part, "near", nn_, i)
                got = part if got is None else got + part
        if nn_ == 1:
            branch_got = place.send_outer(branches)
        out_rows = finish_rows(middles, [branches[0], *branch_got], valid)
        gains = place.total_dp(gains, part[0])
        gq = gains[2 * depth : 2 * depth + LANES]
        gk = gains[2 * depth + LANES : 2 * depth + 2 * LANES]
        far_got = [swap(part[m], "far", nf, m) for m in range(1, nf)]
        w_qkv_grad = summed([part[0]] + [after(g, out_rows) for g in far_got])

        grads = None
        for own, start in zip(ffn_grads, starts):
            grads = finish_grads(own, start, units, grads)
        return (
            out_rows.reshape(rows, slots, depth),
            input_grad.reshape(rows, slots, depth),
            gains[:depth],
            w_qkv_grad[:qc].T,
            w_qkv_grad[qc : qc + kc].T,
            w_qkv_grad[qc + kc :].T,
            gq[:HD] + gq[HD:],
            gk[:HD] + gk[HD:],
            w_out_grad.astype(F32).T,
            gains[depth : 2 * depth],
            grads[0],
            grads[1],
            grads[2],
        )

    return per_device


def solution(mesh):
    place = Place(mesh)
    wide = P(place.dp, "ctx")
    rows = P(place.dp, "ctx", None)
    in_specs = (
        rows, P(place.dp), P(), wide, wide, wide, P(), P(), wide, P(), wide, wide, wide, rows,
    )
    out_specs = (
        rows, rows, P(), wide, wide, wide, P(), P(), wide, P(), wide, wide, wide,
    )
    return jax.shard_map(
        make_layer(place),
        mesh=place.mesh,
        in_specs=in_specs,
        out_specs=out_specs,
        check_vma=False,
    )
```
